32 devices in a mesh: tun: 8 (over y, x, core), sec: 4 (over z).
Axes of the slice: x: 2, y: 2, z: 4, core: 2. Of those that a mesh axis runs over, the one named last changes fastest.
Arguments:
- concentration: float32 [2, 4, 8, 8, 2048], P(None, 'sec', None, None, 'tun'), may hold values from -6 to 6
- velocity: float32 [3, 4, 8, 8, 2048], P(None, 'sec', None, None, 'tun'), may hold values from -3 to 3
Outputs:
- new_concentration: float32 [2, 4, 8, 8, 2048], P(None, 'sec', None, None, 'tun')
The draws below stay inside these ranges and needn't reach their ends.
All inputs are finite; a program needn't handle non-finite values.
Results may differ from the reference program's by a relative error of at most 0.00002.
Values sent between devices are 32-bit elements; how exact they have to be, the bound alone decides.
No kernel may reach another device: no remote copies, remote signals or barrier semaphores. Data moves between devices by JAX's collectives and lax.ppermute only.
A program may use at most 64 MiB of HBM per device.

```python
import math
import jax
import jax.numpy as jnp
from jax import lax

BINS = 2
CS = 8
NX = 2048
N_SEC = 4


def levels(key, dims, shards, smallest, largest):
    level = 1.0
    for axis_at, blocks in shards:
        steps = jax.random.uniform(jax.random.fold_in(jax.random.fold_in(key, 6), axis_at), (blocks,), jnp.float32, smallest / len(shards), largest / len(shards))
        level = level * jnp.repeat(jnp.exp(steps), dims[axis_at] // blocks).reshape((-1,) + (1,) * (len(dims) - 1 - axis_at))
    return level


def normal_values(own_key, shape, spread, limit, pieces=(), dtype=jnp.bfloat16):
    values = jax.random.normal(own_key, shape, jnp.float32) * spread
    if len(pieces) > 0:
        values = levels(own_key, shape, pieces, -0.22, 0.18) * values
    return jnp.clip(values, min=-limit, max=limit).astype(dtype)


def setup_inputs(seed: int = 0) -> dict:
    splits = jax.random.split(jax.random.key(seed), 3)
    return {
        "concentration": normal_values(splits[0], (BINS, N_SEC, CS, CS, NX), 1.0, 6.0, ((1, 4), (4, 8)), jnp.float32),
        "velocity": normal_values(splits[1], (3, N_SEC, CS, CS, NX), 0.7, 3.0, ((1, 4), (4, 8)), jnp.float32),
    }


TIME_STEP = 0.1
DIFFUSIVITY = (0.4, 0.15)
SETTLING = (0.05, 0.6)

def assemble(left_part, middle_part, right_part, axis):
    count_elem = left_part.shape[axis]
    zero_slab = jnp.zeros_like(lax.slice_in_dim(left_part, 0, 1, 1, axis))
    even_nodes = jnp.concatenate([left_part, zero_slab], axis) + jnp.concatenate([zero_slab, right_part], axis)
    head_nodes = lax.slice_in_dim(even_nodes, 0, count_elem, 1, axis)
    paired = jnp.stack([head_nodes, middle_part], axis=axis + 1)
    shape_list = list(head_nodes.shape)
    shape_list[axis] = 2 * count_elem
    woven = paired.reshape(shape_list)
    return jnp.concatenate([woven, lax.slice_in_dim(even_nodes, count_elem, count_elem + 1, 1, axis)], axis)

def line_terms(field, axis):
    length = field.shape[axis]
    left_node = lax.slice_in_dim(field, 0, length - 1, 2, axis)
    mid_node = lax.slice_in_dim(field, 1, length - 1, 2, axis)
    right_node = lax.slice_in_dim(field, 2, length, 2, axis)
    weight_left = (-1.5 * left_node + 2.0 * mid_node - 0.5 * right_node) / 3.0
    weight_mid = 0.5 * (right_node - left_node) * (4.0 / 3.0)
    weight_right = (0.5 * left_node - 2.0 * mid_node + 1.5 * right_node) / 3.0
    gradient = assemble(weight_left, weight_mid, weight_right, axis)
    stiffness = assemble(-1.5 * weight_left - 0.5 * weight_mid + 0.5 * weight_right, 2.0 * weight_left - 2.0 * weight_right, -0.5 * weight_left + 0.5 * weight_mid + 1.5 * weight_right, axis)
    return (gradient, stiffness)

def local_mass(length, axis):
    index = jnp.arange(length)
    inner = jnp.where(index % 2 == 1, 4.0 / 3.0, 2.0 / 3.0)
    masses = jnp.where((index == 0) | (index == length - 1), 1.0 / 3.0, inner).astype(jnp.float32)
    shape_list = [1, 1, 1, 1]
    shape_list[axis] = length
    return masses.reshape(shape_list)

def full_mass(length, axis):
    index = jnp.arange(length)
    masses = jnp.where(index % 2 == 1, 4.0 / 3.0, 2.0 / 3.0).astype(jnp.float32)
    shape_list = [1, 1, 1, 1]
    shape_list[axis] = length
    return masses.reshape(shape_list)

def residual(dust, flow):
    mass_y = local_mass(dust.shape[1], 1)
    mass_z = local_mass(dust.shape[2], 2)
    mass_x = local_mass(dust.shape[3], 3)
    kappa = jnp.array(DIFFUSIVITY, jnp.float32).reshape(2, 1, 1, 1)
    settle = jnp.array(SETTLING, jnp.float32).reshape(2, 1, 1, 1)
    grad_y, stiff_y = line_terms(dust, 1)
    grad_z, stiff_z = line_terms(dust, 2)
    grad_x, stiff_x = line_terms(dust, 3)
    term_y = ((flow[0:1] - settle) * grad_y + kappa * stiff_y) * (mass_z * mass_x)
    term_z = (flow[1:2] * grad_z + kappa * stiff_z) * (mass_y * mass_x)
    term_x = (flow[2:3] * grad_x + kappa * stiff_x) * (mass_y * mass_z)
    return -(term_y + term_z + term_x)

def reference(concentration, velocity):
    side_count = math.isqrt(N_SEC)
    grid_side = side_count * CS

    def to_grid(array):
        comps = array.shape[0]
        shaped = array.reshape(comps, side_count, side_count, CS, CS, NX)
        return shaped.transpose(0, 1, 3, 2, 4, 5).reshape(comps, grid_side, grid_side, NX)

    def from_grid(array):
        comps = array.shape[0]
        shaped = array.reshape(comps, side_count, CS, side_count, CS, NX)
        return shaped.transpose(0, 1, 3, 2, 4, 5).reshape(comps, side_count * side_count, CS, CS, NX)

    def extend(array):
        padded = jnp.pad(array, ((0, 0), (0, 1), (0, 1), (0, 0)))
        return jnp.concatenate([padded, padded[..., 0:1]], 3)
    vertical = jnp.arange(grid_side).reshape(1, grid_side, 1, 1)
    across = jnp.arange(grid_side).reshape(1, 1, grid_side, 1)
    interior = jnp.where((vertical == 0) | (across == 0), 0.0, 1.0).astype(jnp.float32)
    mass = full_mass(grid_side, 1) * full_mass(grid_side, 2) * full_mass(NX, 3)
    dust = to_grid(concentration) * interior
    flow_ext = extend(to_grid(velocity))

    def tendency(field):
        partial_value = residual(extend(field), flow_ext)[:, :grid_side, :grid_side]
        main_part = partial_value[..., :NX]
        folded = jnp.concatenate([main_part[..., 0:1] + partial_value[..., NX:NX + 1], main_part[..., 1:]], 3)
        return interior * folded / mass
    segment = dust + TIME_STEP * tendency(dust)
    result = 0.5 * dust + 0.5 * (segment + TIME_STEP * tendency(segment))
    return from_grid(result)
```

```python
import math

import jax
import jax.numpy as jnp
from jax import lax
from jax.experimental import pallas as pl
from jax.experimental.pallas import tpu as pltpu
from jax.sharding import PartitionSpec as P

TIME_STEP = 0.1
DIFFUSIVITY = (0.4, 0.15)
SETTLING = (0.05, 0.6)
LANES = 128


def section_place(side):
    place = lax.axis_index("sec")
    return place // side, lax.rem(place, side)


def wall_mask(row, col, y, shape):
    across = lax.broadcasted_iota(jnp.int32, shape, 0)
    wall = (across == 0) & (col == 0)
    if y == 0:
        wall = wall | (row == 0)
    return wall


def gather_rows(ref, b, z, size):
    shape = (size, ref.shape[-1])
    at = lax.broadcasted_iota(jnp.int32, shape, 0)
    rows = jnp.broadcast_to(ref[b, z : z + 1, :], shape)
    for y in range(1, size):
        row = ref[b, y * size + z : y * size + z + 1, :]
        rows = jnp.where(at == y, jnp.broadcast_to(row, shape), rows)
    return rows


def fill_payload(side, row, col, tiles, rows_of, refs):
    y_out, z_out, right_out, left_out = refs
    bins, _, size, length = y_out.shape
    lane = lax.broadcasted_iota(jnp.int32, (size, LANES), 1)
    right = jnp.zeros((size, LANES), jnp.float32)
    left = jnp.zeros((size, LANES), jnp.float32)
    for b in range(bins):
        for y in range(size):
            tile = tiles(b, y)
            slot = b * size + y
            last = pltpu.roll(tile[:, length - LANES :], (2 * slot + 2) % LANES, 1)
            right = jnp.where((lane == 2 * slot) | (lane == 2 * slot + 1), last, right)
            first = tile[:, :LANES]
            if slot:
                first = pltpu.roll(first, slot, 1)
            left = jnp.where(lane == slot, first, left)
        if side == 2:
            for k in range(2):
                y_out[b, k] = jnp.where(row == 0, tiles(b, size - 2 + k), tiles(b, k))
                z_out[b, k] = jnp.where(col == 0, rows_of(b, size - 2 + k), rows_of(b, k))
        else:
            for k in range(2):
                y_out[b, k] = tiles(b, size - 2 + k)
                z_out[b, k] = rows_of(b, size - 2 + k)
            y_out[b, 2] = tiles(b, 0)
            z_out[b, 2] = rows_of(b, 0)
    right_out[...] = right
    left_out[...] = left


def pack_kernel(side, size, conc_ref, y_out, z_out, right_out, left_out):
    row, col = section_place(side)
    bins = conc_ref.shape[0]
    length = conc_ref.shape[-1]
    shape = (size, length)
    up = lax.broadcasted_iota(jnp.int32, shape, 0)

    def tiles(b, y):
        return jnp.where(
            wall_mask(row, col, y, shape), 0.0, conc_ref[b, y * size : (y + 1) * size, :]
        )

    def rows_of(b, z):
        wall = (up == 0) & (row == 0)
        if z == 0:
            wall = wall | (col == 0)
        return jnp.where(wall, 0.0, gather_rows(conc_ref, b, z, size))

    fill_payload(side, row, col, tiles, rows_of, (y_out, z_out, right_out, left_out))


def slope_and_bend(m1, p1, m2, p2):
    return (p1 - m1) - (p2 - m2), (p2 + m2) - 2.0 * (p1 + m1)


def tendency(side, size, row, col, tiles, vel_ref, halo):
    y_in, z_in, right_in, left_in = halo
    bins = len(DIFFUSIVITY)
    length = vel_ref.shape[-1]
    shape = (size, length)
    z_at = lax.broadcasted_iota(jnp.int32, shape, 0)
    x_at = lax.broadcasted_iota(jnp.int32, shape, 1)
    z_even, x_even = z_at % 2 == 0, x_at % 2 == 0
    z_near = jnp.where(z_even, 0.5, 1.0)
    z_far = jnp.where(z_even, 0.25, 0.0)
    x_near = jnp.where(x_even, 0.5, 1.0)
    x_far = jnp.where(x_even, 0.25, 0.0)
    centre = jnp.where(z_even, 3.5, 2.0) + jnp.where(x_even, 3.5, 2.0)
    z_first, z_last, z_before = z_at == 0, z_at == size - 1, z_at == size - 2
    x_first, x_last, x_before = x_at == 0, x_at == length - 1, x_at == length - 2
    hi = 0 if side == 2 else 2
    left_msg, right_msg = right_in[...], left_in[...]

    def column(message, slot):
        return jnp.broadcast_to(message[:, slot : slot + 1], shape)

    for b in range(bins):
        kappa, settle = DIFFUSIVITY[b], SETTLING[b]
        above = jnp.where(row == side - 1, 0.0, y_in[b, hi])
        for y in range(size):
            f = tiles(b, y)
            nearer = tiles(b, y - 1) if y > 0 else y_in[b, 1]
            farther = tiles(b, y + 1) if y < size - 1 else above
            if y % 2 == 0:
                m2 = tiles(b, y - 2) if y > 0 else y_in[b, 0]
                p2 = tiles(b, y + 2) if y < size - 2 else above
                gy, ky = slope_and_bend(nearer, farther, 0.25 * m2, 0.25 * p2)
                self_weight = centre + 3.5
            else:
                gy = 0.5 * (farther - nearer)
                ky = -(farther + nearer)
                self_weight = centre + 2.0

            z_lo2 = jnp.broadcast_to(z_in[b, 0, y : y + 1, :], shape)
            z_lo1 = jnp.broadcast_to(z_in[b, 1, y : y + 1, :], shape)
            z_hi = jnp.where(
                col == side - 1, 0.0, jnp.broadcast_to(z_in[b, hi, y : y + 1, :], shape)
            )
            near, far = f * z_near, f * z_far
            gz, kz = slope_and_bend(
                jnp.where(z_first, z_lo1, pltpu.roll(near, 1, 0)),
                jnp.where(z_last, 0.5 * z_hi, pltpu.roll(near, size - 1, 0)),
                jnp.where(z_first, 0.25 * z_lo2, pltpu.roll(far, 2, 0)),
                jnp.where(z_before, 0.25 * z_hi, pltpu.roll(far, size - 2, 0)),
            )

            slot = b * size + y
            x_lo2, x_lo1 = column(left_msg, 2 * slot), column(left_msg, 2 * slot + 1)
            x_hi = column(right_msg, slot)
            near, far = f * x_near, f * x_far
            gx, kx = slope_and_bend(
                jnp.where(x_first, x_lo1, pltpu.roll(near, 1, 1)),
                jnp.where(x_last, 0.5 * x_hi, pltpu.roll(near, length - 1, 1)),
                jnp.where(x_first, 0.25 * x_lo2, pltpu.roll(far, 2, 1)),
                jnp.where(x_before, 0.25 * x_hi, pltpu.roll(far, length - 2, 1)),
            )

            at = slice(y * size, (y + 1) * size)
            moved = (vel_ref[0, at, :] - settle) * gy + vel_ref[1, at, :] * gz + vel_ref[2, at, :] * gx
            rate = moved + kappa * (self_weight * f + (ky + kz + kx))
            yield b, y, f, jnp.where(wall_mask(row, col, y, shape), 0.0, -rate)


def first_kernel(
    side, size, conc_ref, vel_ref, y_in, z_in, right_in, left_in,
    seg_ref, y_out, z_out, right_out, left_out,
):
    row, col = section_place(side)
    shape = (size, conc_ref.shape[-1])

    def dust(b, y):
        return jnp.where(
            wall_mask(row, col, y, shape), 0.0, conc_ref[b, y * size : (y + 1) * size, :]
        )

    halo = (y_in, z_in, right_in, left_in)
    for b, y, f, rate in tendency(side, size, row, col, dust, vel_ref, halo):
        seg_ref[b, y * size : (y + 1) * size, :] = f + TIME_STEP * rate

    def tiles(b, y):
        return seg_ref[b, y * size : (y + 1) * size, :]

    def rows_of(b, z):
        return gather_rows(seg_ref, b, z, size)

    fill_payload(side, row, col, tiles, rows_of, (y_out, z_out, right_out, left_out))


def second_kernel(side, size, conc_ref, vel_ref, seg_ref, y_in, z_in, right_in, left_in, out_ref):
    row, col = section_place(side)
    shape = (size, conc_ref.shape[-1])

    def tiles(b, y):
        return seg_ref[b, y * size : (y + 1) * size, :]

    halo = (y_in, z_in, right_in, left_in)
    for b, y, f, rate in tendency(side, size, row, col, tiles, vel_ref, halo):
        at = slice(y * size, (y + 1) * size)
        dust = jnp.where(wall_mask(row, col, y, shape), 0.0, conc_ref[b, at, :])
        out_ref[b, at, :] = 0.5 * dust + 0.5 * (f + TIME_STEP * rate)


def shift(block, axis, distance, moves):
    return lax.ppermute(block, axis, [(s, moves(s, distance)) for s in range(lax.axis_size(axis))])


def body(concentration, velocity):
    side = math.isqrt(lax.axis_size("sec"))
    tunnel = lax.axis_size("tun")
    bins, _, size, _, length = concentration.shape
    conc = concentration.reshape(bins, size * size, length)
    vel = velocity.reshape(3, size * size, length)
    planes = 2 if side == 2 else 3
    f32 = jnp.float32
    payload = [
        jax.ShapeDtypeStruct((bins, planes, size, length), f32),
        jax.ShapeDtypeStruct((bins, planes, size, length), f32),
        jax.ShapeDtypeStruct((size, LANES), f32),
        jax.ShapeDtypeStruct((size, LANES), f32),
    ]
    field = jax.ShapeDtypeStruct((bins, size * size, length), f32)

    def call(kernel, outs, *args):
        return pl.pallas_call(
            lambda *refs: kernel(side, size, *refs),
            out_shape=outs,
            in_specs=[pl.BlockSpec(memory_space=pltpu.VMEM)] * len(args),
            out_specs=jax.tree.map(lambda _: pl.BlockSpec(memory_space=pltpu.VMEM), outs),
            name=kernel.__name__,
        )(*args)

    def along_tunnel(s, d):
        return (s + d) % tunnel

    def along_y(s, d):
        return (s // side + d) % side * side + s % side

    def along_z(s, d):
        return s // side * side + (s % side + d) % side

    def exchange(y_out, z_out, right_out, left_out):
        right_in = shift(right_out, "tun", 1, along_tunnel)
        left_in = shift(left_out, "tun", -1, along_tunnel)
        if side == 2:
            z_in = shift(z_out, "sec", 1, along_z)
            y_in = shift(y_out, "sec", 1, along_y)
        else:
            z_in, y_in = (
                jnp.concatenate(
                    [shift(out[:, :2], "sec", 1, move), shift(out[:, 2:], "sec", -1, move)], 1
                )
                for out, move in ((z_out, along_z), (y_out, along_y))
            )
        return y_in, z_in, right_in, left_in

    halo = exchange(*call(pack_kernel, payload, conc))
    segment, *sends = call(first_kernel, [field] + payload, conc, vel, *halo)
    halo = exchange(*sends)
    result = call(second_kernel, field, conc, vel, segment, *halo)
    return result.reshape(concentration.shape)


def solution(mesh):
    spec = P(None, "sec", None, None, "tun")
    return jax.shard_map(
        body, mesh=mesh, in_specs=(spec, spec), out_specs=spec, check_vma=False
    )
```

```python
import math

import jax
import jax.numpy as jnp
from jax import lax
from jax.experimental import pallas as pl
from jax.experimental.pallas import tpu as pltpu
from jax.sharding import PartitionSpec as P

TIME_STEP = 0.1
DIFFUSIVITY = (0.4, 0.15)
SETTLING = (0.05, 0.6)
LANES = 128


def section_place(side):
    place = lax.axis_index("sec")
    return place // side, lax.rem(place, side)


def wall_mask(row, col, y, shape):
    across = lax.broadcasted_iota(jnp.int32, shape, 0)
    wall = (across == 0) & (col == 0)
    if y == 0:
        wall = wall | (row == 0)
    return wall


def gather_rows(ref, b, z, size):
    shape = (size, ref.shape[-1])
    at = lax.broadcasted_iota(jnp.int32, shape, 0)
    rows = jnp.broadcast_to(ref[b, z : z + 1, :], shape)
    for y in range(1, size):
        row = ref[b, y * size + z : y * size + z + 1, :]
        rows = jnp.where(at == y, jnp.broadcast_to(row, shape), rows)
    return rows


def fill_payload(side, row, col, tiles, rows_of, refs):
    y_out, z_out, right_out, left_out = refs
    bins, _, size, length = y_out.shape
    lane = lax.broadcasted_iota(jnp.int32, (size, LANES), 1)
    right = jnp.zeros((size, LANES), jnp.float32)
    left = jnp.zeros((size, LANES), jnp.float32)
    for b in range(bins):
        for y in range(size):
            tile = tiles(b, y)
            slot = b * size + y
            last = pltpu.roll(tile[:, length - LANES :], (2 * slot + 2) % LANES, 1)
            right = jnp.where((lane == 2 * slot) | (lane == 2 * slot + 1), last, right)
            first = tile[:, :LANES]
            if slot:
                first = pltpu.roll(first, slot, 1)
            left = jnp.where(lane == slot, first, left)
        if side == 2:
            for k in range(2):
                y_out[b, k] = jnp.where(row == 0, tiles(b, size - 2 + k), tiles(b, k))
                z_out[b, k] = jnp.where(col == 0, rows_of(b, size - 2 + k), rows_of(b, k))
        else:
            for k in range(2):
                y_out[b, k] = tiles(b, size - 2 + k)
                z_out[b, k] = rows_of(b, size - 2 + k)
            y_out[b, 2] = tiles(b, 0)
            z_out[b, 2] = rows_of(b, 0)
    right_out[...] = right
    left_out[...] = left


def pack_kernel(side, size, conc_ref, _, y_out, z_out, right_out, left_out):
    row, col = section_place(side)
    bins = conc_ref.shape[0]
    length = conc_ref.shape[-1]
    shape = (size, length)
    up = lax.broadcasted_iota(jnp.int32, shape, 0)

    def tiles(b, y):
        return jnp.where(
            wall_mask(row, col, y, shape), 0.0, conc_ref[b, y * size : (y + 1) * size, :]
        )

    def rows_of(b, z):
        wall = (up == 0) & (row == 0)
        if z == 0:
            wall = wall | (col == 0)
        return jnp.where(wall, 0.0, gather_rows(conc_ref, b, z, size))

    fill_payload(side, row, col, tiles, rows_of, (y_out, z_out, right_out, left_out))


def slope_and_bend(m1, p1, m2, p2):
    return (p1 - m1) - (p2 - m2), (p2 + m2) - 2.0 * (p1 + m1)


def tendency(side, size, row, col, tiles, vel_ref, halo):
    y_in, z_in, right_in, left_in = halo
    bins = len(DIFFUSIVITY)
    length = vel_ref.shape[-1]
    shape = (size, length)
    z_at = lax.broadcasted_iota(jnp.int32, shape, 0)
    x_at = lax.broadcasted_iota(jnp.int32, shape, 1)
    z_even, x_even = z_at % 2 == 0, x_at % 2 == 0
    z_near = jnp.where(z_even, 0.5, 1.0)
    z_far = jnp.where(z_even, 0.25, 0.0)
    x_near = jnp.where(x_even, 0.5, 1.0)
    x_far = jnp.where(x_even, 0.25, 0.0)
    centre = jnp.where(z_even, 3.5, 2.0) + jnp.where(x_even, 3.5, 2.0)
    z_first, z_last, z_before = z_at == 0, z_at == size - 1, z_at == size - 2
    x_first, x_last, x_before = x_at == 0, x_at == length - 1, x_at == length - 2
    hi = 0 if side == 2 else 2
    left_msg, right_msg = right_in[...], left_in[...]

    def column(message, slot):
        return jnp.broadcast_to(message[:, slot : slot + 1], shape)

    for b in range(bins):
        kappa, settle = DIFFUSIVITY[b], SETTLING[b]
        above = jnp.where(row == side - 1, 0.0, y_in[b, hi])
        for y in range(size):
            f = tiles(b, y)
            nearer = tiles(b, y - 1) if y > 0 else y_in[b, 1]
            farther = tiles(b, y + 1) if y < size - 1 else above
            if y % 2 == 0:
                m2 = tiles(b, y - 2) if y > 0 else y_in[b, 0]
                p2 = tiles(b, y + 2) if y < size - 2 else above
                gy, ky = slope_and_bend(nearer, farther, 0.25 * m2, 0.25 * p2)
                self_weight = centre + 3.5
            else:
                gy = 0.5 * (farther - nearer)
                ky = -(farther + nearer)
                self_weight = centre + 2.0

            z_lo2 = jnp.broadcast_to(z_in[b, 0, y : y + 1, :], shape)
            z_lo1 = jnp.broadcast_to(z_in[b, 1, y : y + 1, :], shape)
            z_hi = jnp.where(
                col == side - 1, 0.0, jnp.broadcast_to(z_in[b, hi, y : y + 1, :], shape)
            )
            near, far = f * z_near, f * z_far
            gz, kz = slope_and_bend(
                jnp.where(z_first, z_lo1, pltpu.roll(near, 1, 0)),
                jnp.where(z_last, 0.5 * z_hi, pltpu.roll(near, size - 1, 0)),
                jnp.where(z_first, 0.25 * z_lo2, pltpu.roll(far, 2, 0)),
                jnp.where(z_before, 0.25 * z_hi, pltpu.roll(far, size - 2, 0)),
            )

            slot = b * size + y
            x_lo2, x_lo1 = column(left_msg, 2 * slot), column(left_msg, 2 * slot + 1)
            x_hi = column(right_msg, slot)
            near, far = f * x_near, f * x_far
            gx, kx = slope_and_bend(
                jnp.where(x_first, x_lo1, pltpu.roll(near, 1, 1)),
                jnp.where(x_last, 0.5 * x_hi, pltpu.roll(near, length - 1, 1)),
                jnp.where(x_first, 0.25 * x_lo2, pltpu.roll(far, 2, 1)),
                jnp.where(x_before, 0.25 * x_hi, pltpu.roll(far, length - 2, 1)),
            )

            at = slice(y * size, (y + 1) * size)
            moved = (vel_ref[0, at, :] - settle) * gy + vel_ref[1, at, :] * gz + vel_ref[2, at, :] * gx
            rate = moved + kappa * (self_weight * f + (ky + kz + kx))
            yield b, y, f, jnp.where(wall_mask(row, col, y, shape), 0.0, -rate)


def first_kernel(
    side, size, conc_ref, vel_ref, y_in, z_in, right_in, left_in,
    seg_ref, y_out, z_out, right_out, left_out,
):
    row, col = section_place(side)
    shape = (size, conc_ref.shape[-1])

    def dust(b, y):
        return jnp.where(
            wall_mask(row, col, y, shape), 0.0, conc_ref[b, y * size : (y + 1) * size, :]
        )

    halo = (y_in, z_in, right_in, left_in)
    for b, y, f, rate in tendency(side, size, row, col, dust, vel_ref, halo):
        seg_ref[b, y * size : (y + 1) * size, :] = f + TIME_STEP * rate

    def tiles(b, y):
        return seg_ref[b, y * size : (y + 1) * size, :]

    def rows_of(b, z):
        return gather_rows(seg_ref, b, z, size)

    fill_payload(side, row, col, tiles, rows_of, (y_out, z_out, right_out, left_out))


def second_kernel(side, size, conc_ref, vel_ref, seg_ref, y_in, z_in, right_in, left_in, out_ref):
    row, col = section_place(side)
    shape = (size, conc_ref.shape[-1])

    def tiles(b, y):
        return seg_ref[b, y * size : (y + 1) * size, :]

    halo = (y_in, z_in, right_in, left_in)
    for b, y, f, rate in tendency(side, size, row, col, tiles, vel_ref, halo):
        at = slice(y * size, (y + 1) * size)
        dust = jnp.where(wall_mask(row, col, y, shape), 0.0, conc_ref[b, at, :])
        out_ref[b, at, :] = 0.5 * dust + 0.5 * (f + TIME_STEP * rate)


def shift(block, axis, distance, moves):
    return lax.ppermute(block, axis, [(s, moves(s, distance)) for s in range(lax.axis_size(axis))])


def body(concentration, velocity):
    side = math.isqrt(lax.axis_size("sec"))
    tunnel = lax.axis_size("tun")
    bins, _, size, _, length = concentration.shape
    conc = concentration.reshape(bins, size * size, length)
    vel = velocity.reshape(3, size * size, length)
    planes = 2 if side == 2 else 3
    f32 = jnp.float32
    payload = [
        pltpu.VMEM((bins, planes, size, length), f32),
        pltpu.VMEM((bins, planes, size, length), f32),
        pltpu.VMEM((size, LANES), f32),
        pltpu.VMEM((size, LANES), f32),
    ]
    field = (bins, size * size, length)

    def call(kernel, outs, *args):
        args = [pltpu.with_memory_space_constraint(arg, pltpu.VMEM) for arg in args]
        return pl.pallas_call(
            lambda *refs: kernel(side, size, *refs),
            out_shape=outs,
            in_specs=[pl.BlockSpec(memory_space=pltpu.VMEM)] * len(args),
            out_specs=jax.tree.map(lambda _: pl.BlockSpec(memory_space=pltpu.VMEM), outs),
            name=kernel.__name__,
        )(*args)

    def along_tunnel(s, d):
        return (s + d) % tunnel

    def along_y(s, d):
        return (s // side + d) % side * side + s % side

    def along_z(s, d):
        return s // side * side + (s % side + d) % side

    def exchange(y_out, z_out, right_out, left_out):
        right_in = shift(right_out, "tun", 1, along_tunnel)
        left_in = shift(left_out, "tun", -1, along_tunnel)
        if side == 2:
            z_in = shift(z_out, "sec", 1, along_z)
            y_in = shift(y_out, "sec", 1, along_y)
        else:
            z_in, y_in = (
                jnp.concatenate(
                    [shift(out[:, :2], "sec", 1, move), shift(out[:, 2:], "sec", -1, move)], 1
                )
                for out, move in ((z_out, along_z), (y_out, along_y))
            )
        return y_in, z_in, right_in, left_in

    halo = exchange(*call(pack_kernel, payload, conc, vel))
    segment, *sends = call(first_kernel, [pltpu.VMEM(field, f32)] + payload, conc, vel, *halo)
    halo = exchange(*sends)
    result = call(second_kernel, jax.ShapeDtypeStruct(field, f32), conc, vel, segment, *halo)
    return result.reshape(concentration.shape)


def solution(mesh):
    spec = P(None, "sec", None, None, "tun")
    return jax.shard_map(
        body, mesh=mesh, in_specs=(spec, spec), out_specs=spec, check_vma=False
    )
```

```python
import math

import jax
import jax.numpy as jnp
from jax import lax
from jax.experimental import pallas as pl
from jax.experimental.pallas import tpu as pltpu
from jax.sharding import PartitionSpec as P

TIME_STEP = 0.1
DIFFUSIVITY = (0.4, 0.15)
SETTLING = (0.05, 0.6)
LANES = 128
ORDER = ("y","z","other","pair")


def section_place(side):
    place = lax.axis_index("sec")
    return place // side, lax.rem(place, side)


def pair_is_right():
    return lax.rem(lax.axis_index("tun"), 2) == 0


def wall_mask(row, col, y, shape):
    across = lax.broadcasted_iota(jnp.int32, shape, 0)
    wall = (across == 0) & (col == 0)
    if y == 0:
        wall = wall | (row == 0)
    return wall


def gather_rows(ref, b, z, size):
    shape = (size, ref.shape[-1])
    at = lax.broadcasted_iota(jnp.int32, shape, 0)
    rows = jnp.broadcast_to(ref[b, z : z + 1, :], shape)
    for y in range(1, size):
        row = ref[b, y * size + z : y * size + z + 1, :]
        rows = jnp.where(at == y, jnp.broadcast_to(row, shape), rows)
    return rows


def fill_payload(side, row, col, tiles, rows_of, refs):
    send = dict(zip(ORDER, refs))
    y_out, z_out = send["y"], send["z"]
    bins, _, size, length = y_out.shape
    lane = lax.broadcasted_iota(jnp.int32, (size, LANES), 1)
    right = jnp.zeros((size, LANES), jnp.float32)
    left = jnp.zeros((size, LANES), jnp.float32)
    for b in range(bins):
        for y in range(size):
            tile = tiles(b, y)
            slot = b * size + y
            last = pltpu.roll(tile[:, length - LANES :], (2 * slot + 2) % LANES, 1)
            right = jnp.where((lane == 2 * slot) | (lane == 2 * slot + 1), last, right)
            first = tile[:, :LANES]
            if slot:
                first = pltpu.roll(first, slot, 1)
            left = jnp.where(lane == slot, first, left)
        if side == 2:
            for k in range(2):
                y_out[b, k] = jnp.where(row == 0, tiles(b, size - 2 + k), tiles(b, k))
                z_out[b, k] = jnp.where(col == 0, rows_of(b, size - 2 + k), rows_of(b, k))
        else:
            for k in range(2):
                y_out[b, k] = tiles(b, size - 2 + k)
                z_out[b, k] = rows_of(b, size - 2 + k)
            y_out[b, 2] = tiles(b, 0)
            z_out[b, 2] = rows_of(b, 0)
    send["pair"][...] = jnp.where(pair_is_right(), right, left)
    send["other"][...] = jnp.where(pair_is_right(), left, right)


def pack_kernel(
    side, size, conc_hbm, vel_hbm, conc_ref, vel_ref, *refs
):
    *sends, sems = refs
    load = pltpu.make_async_copy(conc_hbm, conc_ref, sems.at[0])
    load_vel = pltpu.make_async_copy(vel_hbm, vel_ref, sems.at[1])
    load.start()
    load_vel.start()
    row, col = section_place(side)
    length = conc_ref.shape[-1]
    shape = (size, length)
    up = lax.broadcasted_iota(jnp.int32, shape, 0)

    def tiles(b, y):
        return jnp.where(
            wall_mask(row, col, y, shape), 0.0, conc_ref[b, y * size : (y + 1) * size, :]
        )

    def rows_of(b, z):
        wall = (up == 0) & (row == 0)
        if z == 0:
            wall = wall | (col == 0)
        return jnp.where(wall, 0.0, gather_rows(conc_ref, b, z, size))

    load.wait()
    fill_payload(side, row, col, tiles, rows_of, sends)
    load_vel.wait()


def slope_and_bend(m1, p1, m2, p2):
    return (p1 - m1) - (p2 - m2), (p2 + m2) - 2.0 * (p1 + m1)


def tendency(side, size, row, col, tiles, vel_ref, halo):
    got = dict(zip(ORDER, halo))
    y_in, z_in = got["y"], got["z"]
    bins = len(DIFFUSIVITY)
    length = vel_ref.shape[-1]
    shape = (size, length)
    z_at = lax.broadcasted_iota(jnp.int32, shape, 0)
    x_at = lax.broadcasted_iota(jnp.int32, shape, 1)
    z_even, x_even = z_at % 2 == 0, x_at % 2 == 0
    z_near = jnp.where(z_even, 0.5, 1.0)
    z_far = jnp.where(z_even, 0.25, 0.0)
    x_near = jnp.where(x_even, 0.5, 1.0)
    x_far = jnp.where(x_even, 0.25, 0.0)
    centre = jnp.where(z_even, 3.5, 2.0) + jnp.where(x_even, 3.5, 2.0)
    z_first, z_last, z_before = z_at == 0, z_at == size - 1, z_at == size - 2
    x_first, x_last, x_before = x_at == 0, x_at == length - 1, x_at == length - 2
    hi = 0 if side == 2 else 2
    pair, other = got["pair"][...], got["other"][...]
    left_msg = jnp.where(pair_is_right(), other, pair)
    right_msg = jnp.where(pair_is_right(), pair, other)

    def column(message, slot):
        return jnp.broadcast_to(message[:, slot : slot + 1], shape)

    for b in range(bins):
        kappa, settle = DIFFUSIVITY[b], SETTLING[b]
        above = jnp.where(row == side - 1, 0.0, y_in[b, hi])
        for y in range(size):
            f = tiles(b, y)
            nearer = tiles(b, y - 1) if y > 0 else y_in[b, 1]
            farther = tiles(b, y + 1) if y < size - 1 else above
            if y % 2 == 0:
                m2 = tiles(b, y - 2) if y > 0 else y_in[b, 0]
                p2 = tiles(b, y + 2) if y < size - 2 else above
                gy, ky = slope_and_bend(nearer, farther, 0.25 * m2, 0.25 * p2)
                self_weight = centre + 3.5
            else:
                gy = 0.5 * (farther - nearer)
                ky = -(farther + nearer)
                self_weight = centre + 2.0

            z_lo2 = jnp.broadcast_to(z_in[b, 0, y : y + 1, :], shape)
            z_lo1 = jnp.broadcast_to(z_in[b, 1, y : y + 1, :], shape)
            z_hi = jnp.where(
                col == side - 1, 0.0, jnp.broadcast_to(z_in[b, hi, y : y + 1, :], shape)
            )
            near, far = f * z_near, f * z_far
            gz, kz = slope_and_bend(
                jnp.where(z_first, z_lo1, pltpu.roll(near, 1, 0)),
                jnp.where(z_last, 0.5 * z_hi, pltpu.roll(near, size - 1, 0)),
                jnp.where(z_first, 0.25 * z_lo2, pltpu.roll(far, 2, 0)),
                jnp.where(z_before, 0.25 * z_hi, pltpu.roll(far, size - 2, 0)),
            )

            slot = b * size + y
            x_lo2, x_lo1 = column(left_msg, 2 * slot), column(left_msg, 2 * slot + 1)
            x_hi = column(right_msg, slot)
            near, far = f * x_near, f * x_far
            gx, kx = slope_and_bend(
                jnp.where(x_first, x_lo1, pltpu.roll(near, 1, 1)),
                jnp.where(x_last, 0.5 * x_hi, pltpu.roll(near, length - 1, 1)),
                jnp.where(x_first, 0.25 * x_lo2, pltpu.roll(far, 2, 1)),
                jnp.where(x_before, 0.25 * x_hi, pltpu.roll(far, length - 2, 1)),
            )

            at = slice(y * size, (y + 1) * size)
            moved = (vel_ref[0, at, :] - settle) * gy + vel_ref[1, at, :] * gz + vel_ref[2, at, :] * gx
            rate = moved + kappa * (self_weight * f + (ky + kz + kx))
            yield b, y, f, jnp.where(wall_mask(row, col, y, shape), 0.0, -rate)


def first_kernel(side, size, conc_ref, vel_ref, *refs):
    halo, seg_ref, sends = refs[: len(ORDER)], refs[len(ORDER)], refs[len(ORDER) + 1 :]
    row, col = section_place(side)
    shape = (size, conc_ref.shape[-1])

    def dust(b, y):
        return jnp.where(
            wall_mask(row, col, y, shape), 0.0, conc_ref[b, y * size : (y + 1) * size, :]
        )

    for b, y, f, rate in tendency(side, size, row, col, dust, vel_ref, halo):
        seg_ref[b, y * size : (y + 1) * size, :] = f + TIME_STEP * rate

    def tiles(b, y):
        return seg_ref[b, y * size : (y + 1) * size, :]

    def rows_of(b, z):
        return gather_rows(seg_ref, b, z, size)

    fill_payload(side, row, col, tiles, rows_of, sends)


def second_kernel(side, size, conc_ref, vel_ref, seg_ref, *refs):
    *halo, out_ref = refs
    row, col = section_place(side)
    shape = (size, conc_ref.shape[-1])

    def tiles(b, y):
        return seg_ref[b, y * size : (y + 1) * size, :]

    for b, y, f, rate in tendency(side, size, row, col, tiles, vel_ref, halo):
        at = slice(y * size, (y + 1) * size)
        dust = jnp.where(wall_mask(row, col, y, shape), 0.0, conc_ref[b, at, :])
        out_ref[b, at, :] = 0.5 * dust + 0.5 * (f + TIME_STEP * rate)


def shift(block, axis, distance, moves):
    return lax.ppermute(block, axis, [(s, moves(s, distance)) for s in range(lax.axis_size(axis))])


def body(concentration, velocity):
    side = math.isqrt(lax.axis_size("sec"))
    tunnel = lax.axis_size("tun")
    bins, _, size, _, length = concentration.shape
    conc = concentration.reshape(bins, size * size, length)
    vel = velocity.reshape(3, size * size, length)
    planes = 2 if side == 2 else 3
    f32 = jnp.float32
    shapes = {
        "y": (bins, planes, size, length),
        "z": (bins, planes, size, length),
        "pair": (size, LANES),
        "other": (size, LANES),
    }
    payload = [pltpu.VMEM(shapes[name], f32) for name in ORDER]
    field = (bins, size * size, length)

    vmem = pl.BlockSpec(memory_space=pltpu.VMEM)

    def call(kernel, outs, *args):
        args = [pltpu.with_memory_space_constraint(arg, pltpu.VMEM) for arg in args]
        return pl.pallas_call(
            lambda *refs: kernel(side, size, *refs),
            out_shape=outs,
            in_specs=[vmem] * len(args),
            out_specs=jax.tree.map(lambda _: vmem, outs),
            name=kernel.__name__,
        )(*args)

    def along_pair(s, _):
        return s + 1 - 2 * (s % 2)

    def along_other(s, _):
        return (s - 1 + 2 * (s % 2)) % tunnel

    def along_y(s, d):
        return (s // side + d) % side * side + s % side

    def along_z(s, d):
        return s // side * side + (s % side + d) % side

    def across(out, move):
        if side == 2:
            return shift(out, "sec", 1, move)
        return jnp.concatenate(
            [shift(out[:, :2], "sec", 1, move), shift(out[:, 2:], "sec", -1, move)], 1
        )

    def exchange(sends):
        moves = {
            "y": lambda out: across(out, along_y),
            "z": lambda out: across(out, along_z),
            "pair": lambda out: shift(out, "tun", 0, along_pair),
            "other": lambda out: shift(out, "tun", 0, along_other),
        }
        return [moves[name](out) for name, out in zip(ORDER, sends)]

    conc, vel, *sends = pl.pallas_call(
        lambda *refs: pack_kernel(side, size, *refs),
        out_shape=[pltpu.VMEM(conc.shape, f32), pltpu.VMEM(vel.shape, f32)] + payload,
        in_specs=[pl.BlockSpec(memory_space=pltpu.HBM)] * 2,
        out_specs=[vmem] * 6,
        scratch_shapes=[pltpu.SemaphoreType.DMA((2,))],
        name="pack_kernel",
    )(conc, vel)
    halo = exchange(sends)
    segment, *sends = call(first_kernel, [pltpu.VMEM(field, f32)] + payload, conc, vel, *halo)
    halo = exchange(sends)
    result = call(second_kernel, jax.ShapeDtypeStruct(field, f32), conc, vel, segment, *halo)
    return result.reshape(concentration.shape)


def solution(mesh):
    spec = P(None, "sec", None, None, "tun")
    return jax.shard_map(
        body, mesh=mesh, in_specs=(spec, spec), out_specs=spec, check_vma=False
    )
```

```python
import math

import jax
import jax.numpy as jnp
from jax import lax
from jax.experimental import pallas as pl
from jax.experimental.pallas import tpu as pltpu
from jax.sharding import PartitionSpec as P

TIME_STEP = 0.1
DIFFUSIVITY = (0.4, 0.15)
SETTLING = (0.05, 0.6)
BINS = 2
LANES = 128
ORDER = ("y", "z", "other", "pair")
F32 = jnp.float32


class Place:
    def __init__(self, side, size, length):
        self.side, self.size, self.length = side, size, length
        place = lax.axis_index("sec")
        self.row, self.col = place // side, lax.rem(place, side)
        self.pair_right = lax.rem(lax.axis_index("tun"), 2) == 0
        self.shape = (size, length)
        self.z_at = lax.broadcasted_iota(jnp.int32, self.shape, 0)
        self.lane = lax.broadcasted_iota(jnp.int32, (size, LANES), 1)

    def off_wall(self, y, tile):
        wall = (self.z_at == 0) & (self.col == 0)
        if y == 0:
            wall = wall | (self.row == 0)
        return jnp.where(wall, 0.0, tile)

    def at(self, y):
        return slice(y * self.size, (y + 1) * self.size)

    def rows(self, ref, lead, z):
        rows = jnp.broadcast_to(ref[lead, z : z + 1, :], self.shape)
        for y in range(1, self.size):
            row = ref[lead, y * self.size + z : y * self.size + z + 1, :]
            rows = jnp.where(self.z_at == y, jnp.broadcast_to(row, self.shape), rows)
        return rows

    def first_columns(self, ref, leads):
        packed = jnp.zeros((self.size, LANES), F32)
        for n, lead in enumerate(leads):
            for y in range(self.size):
                to = 2 * (n * self.size + y)
                tile = ref[lead, self.at(y), :LANES]
                packed = jnp.where(self.lane == to, pltpu.roll(tile, to, 1) if to else tile, packed)
        return packed

    def last_columns(self, ref, leads):
        packed = jnp.zeros((self.size, LANES), F32)
        for n, lead in enumerate(leads):
            for y in range(self.size):
                to = 2 * (n * self.size + y)
                tile = pltpu.roll(ref[lead, self.at(y), self.length - LANES :], to + 2, 1)
                packed = jnp.where((self.lane == to) | (self.lane == to + 1), tile, packed)
        return packed

    def for_bins(self, packed):
        width = 2 * self.size
        return sum((pltpu.roll(packed, b * width, 1) for b in range(1, BINS)), packed)

    def by_bin(self, values):
        out = values[-1]
        for b in reversed(range(BINS - 1)):
            out = jnp.where(self.lane < 2 * self.size * (b + 1), values[b], out)
        return out

    def write_across(self, out, up, down, forward):
        if self.side == 2:
            for i in range(out.shape[0]):
                if i >= len(down):
                    out[i] = up[i]
                elif i >= len(up):
                    out[i] = down[i]
                else:
                    out[i] = jnp.where(forward, up[i], down[i])
        else:
            for i, plane in enumerate(up + down):
                out[i] = plane

    def write_tunnel(self, pair, other, right, left):
        pair[...] = jnp.where(self.pair_right, right, left)
        other[...] = jnp.where(self.pair_right, left, right)

    def read_tunnel(self, pair, other):
        pair, other = pair[...], other[...]
        return jnp.where(self.pair_right, other, pair), jnp.where(self.pair_right, pair, other)


def low_weights(flow, kappa):
    return (-0.25 * TIME_STEP) * (flow + kappa), TIME_STEP * (flow + 2.0 * kappa)


def pack_kernel(side, size, conc_hbm, vel_hbm, dust_ref, vel_ref, *refs):
    *sends, sems = refs
    load = pltpu.make_async_copy(conc_hbm, dust_ref, sems.at[0])
    load_vel = pltpu.make_async_copy(vel_hbm, vel_ref, sems.at[1])
    load.start()
    load_vel.start()
    here = Place(side, size, dust_ref.shape[-1])
    load.wait()
    for b in range(BINS):
        for y in range(size):
            dust_ref[b, here.at(y), :] = here.off_wall(y, dust_ref[b, here.at(y), :])
    load_vel.wait()
    send = dict(zip(ORDER, sends))
    bins = range(BINS)
    ends = (size - 2, size - 1)
    here.write_across(
        send["y"],
        [dust_ref[b, here.at(y), :] for b in bins for y in ends],
        [dust_ref[b, here.at(0), :] for b in bins] + [vel_ref[0, here.at(0), :]],
        here.row == 0,
    )
    here.write_across(
        send["z"],
        [here.rows(dust_ref, b, z) for b in bins for z in ends],
        [here.rows(dust_ref, b, 0) for b in bins] + [here.rows(vel_ref, 1, 0)],
        here.col == 0,
    )
    flow = here.for_bins(here.first_columns(vel_ref, [2]))
    left = here.first_columns(dust_ref, bins) + pltpu.roll(flow, LANES // 2, 1)
    here.write_tunnel(send["pair"], send["other"], here.last_columns(dust_ref, bins), left)


def slope_and_bend(m1, p1, m2, p2):
    return (p1 - m1) - (p2 - m2), (p2 + m2) - 2.0 * (p1 + m1)


def inner_rates(here, field, vel_ref):
    size, length, shape = here.size, here.length, here.shape
    x_at = lax.broadcasted_iota(jnp.int32, shape, 1)
    weights = []
    for index, count in ((here.z_at, size), (x_at, length)):
        even = index % 2 == 0
        near, far = jnp.where(even, 0.5, 1.0), jnp.where(even, 0.25, 0.0)
        weights.append(
            (
                jnp.where(index == count - 1, 0.0, near),
                jnp.where(index == 0, 0.0, near),
                jnp.where(index == count - 2, 0.0, far),
                jnp.where(index == 0, 0.0, far),
            )
        )
    centre = jnp.where(here.z_at % 2 == 0, 3.5, 2.0) + jnp.where(x_at % 2 == 0, 3.5, 2.0)

    def along(f, axis, count):
        m1, p1, m2, p2 = weights[axis]
        return slope_and_bend(
            pltpu.roll(f * m1, 1, axis),
            pltpu.roll(f * p1, count - 1, axis),
            pltpu.roll(f * m2, 2, axis),
            pltpu.roll(f * p2, count - 2, axis),
        )

    zero = jnp.zeros(shape, F32)
    for b in range(BINS):
        kappa, settle = DIFFUSIVITY[b], SETTLING[b]

        def tile(y, b=b):
            return field[b, here.at(y), :] if 0 <= y < size else zero

        for y in range(size):
            f = tile(y)
            if y % 2 == 0:
                gy, ky = slope_and_bend(
                    tile(y - 1), tile(y + 1), 0.25 * tile(y - 2), 0.25 * tile(y + 2)
                )
                own = centre + 3.5
            else:
                gy, ky = 0.5 * (tile(y + 1) - tile(y - 1)), -(tile(y + 1) + tile(y - 1))
                own = centre + 2.0
            gz, kz = along(f, 0, size)
            gx, kx = along(f, 1, length)
            u0, u1, u2 = (vel_ref[i, here.at(y), :] for i in range(3))
            moved = (u0 - settle) * gy + u1 * gz + u2 * gx
            yield b, y, f, -(moved + kappa * (own * f + (ky + kz + kx)))


def first_inner_kernel(side, size, dust_ref, vel_ref, part_ref, y_w, z_w, x_w):
    here = Place(side, size, dust_ref.shape[-1])
    for b, y, f, rate in inner_rates(here, dust_ref, vel_ref):
        part_ref[b, here.at(y), :] = here.off_wall(y, f + TIME_STEP * rate)
    ends = (0, size - 2, size - 1)
    y_flow = [vel_ref[0, here.at(y), :] for y in ends]
    z_flow = [here.rows(vel_ref, 1, z) for z in ends]
    for b in range(BINS):
        kappa = DIFFUSIVITY[b]
        for out, flow in ((y_w, [u - SETTLING[b] for u in y_flow]), (z_w, z_flow)):
            out[b, 0], out[b, 1] = low_weights(flow[0], kappa)
            out[b, 2] = (0.25 * TIME_STEP) * (flow[1] - kappa)
            out[b, 3] = (-TIME_STEP) * (0.5 * flow[2] - kappa)
    kappa = here.by_bin(DIFFUSIVITY)
    even = here.lane % 2 == 0
    flow = here.for_bins(here.first_columns(vel_ref, [2]))
    far, _ = low_weights(flow, kappa)
    _, near = low_weights(pltpu.roll(flow, 1, 1), kappa)
    x_w[0] = jnp.where(even, far, near)
    flow = here.for_bins(here.last_columns(vel_ref, [2]))
    x_w[1] = jnp.where(
        even, (0.25 * TIME_STEP) * (flow - kappa), (-TIME_STEP) * (0.5 * flow - kappa)
    )


def pair_sum(product):
    return product + pltpu.roll(product, LANES - 1, 1)


def add_halo(here, part_ref, y_w, z_w, x_w, y_add, z_add, x_low, x_next, share):
    size, length = here.size, here.length
    x_next = jnp.where(here.lane % 2 == 0, x_next, pltpu.roll(x_next, 1, 1))
    x_high = share * x_w[1] * x_next
    x_low = share * x_low
    first, last = here.lane == 0, here.lane >= LANES - 2
    for b in range(BINS):
        z_low, z_before, z_last = z_add[b]
        y_low, y_before, y_last = y_add[b]
        for y in range(size):
            tile = part_ref[b, here.at(y), :]

            def row(plane, y=y):
                return jnp.broadcast_to(plane[y : y + 1, :], here.shape)

            add = jnp.where(
                here.z_at == 0,
                row(z_low),
                jnp.where(here.z_at == size - 1, row(z_last), row(z_before)),
            )
            tile += share * jnp.where((here.z_at == 0) | (here.z_at >= size - 2), add, 0.0)
            for at, plane in ((0, y_low), (size - 2, y_before), (size - 1, y_last)):
                if y == at:
                    tile += share * plane
            to = 2 * (b * size + y)
            low = pltpu.roll(x_low, (LANES - to) % LANES, 1) if to else x_low
            high = pltpu.roll(x_high, (LANES - 2 - to) % LANES, 1)
            low, high = jnp.where(first, low, 0.0), jnp.where(last, high, 0.0)
            inner = [jnp.zeros((size, length - 2 * LANES), F32)] if length > 2 * LANES else []
            tile += jnp.concatenate([low] + inner + [high], 1)
            yield b, y, here.off_wall(y, tile)


def above(here, planes, inside):
    return [jnp.where(inside, plane, 0.0) for plane in planes]


def first_outer_kernel(side, size, part_ref, y_w, z_w, x_w, *refs):
    here = Place(side, size, part_ref.shape[-1])
    got = dict(zip(ORDER, refs[:4]))
    seg_ref, sends = refs[4], refs[5:]
    bins = range(BINS)
    adds, flows = [], []
    for name, weights, at in (("y", y_w, here.row), ("z", z_w, here.col)):
        ref = got[name]
        hi = 0 if side == 2 else 2 * BINS
        add = []
        for b in bins:
            low = ref[2 * b] * weights[b, 0] + ref[2 * b + 1] * weights[b, 1]
            nxt = jnp.where(at == side - 1, 0.0, ref[hi + b])
            add.append((low, nxt * weights[b, 2], nxt * weights[b, 3]))
        adds.append(add)
        flows.append(ref[hi + BINS])
    from_left, from_right = here.read_tunnel(got["pair"], got["other"])
    x_low = pair_sum(from_left * x_w[0])
    for b, y, tile in add_halo(
        here, part_ref, y_w, z_w, x_w, adds[0], adds[1], x_low, from_right, 1.0
    ):
        seg_ref[b, here.at(y), :] = tile

    send = dict(zip(ORDER, sends))
    messages = []
    for axis, flow in enumerate(flows):
        up, down = [], []
        for b in bins:
            if axis == 0:
                far, near, own = (seg_ref[b, here.at(y), :] for y in (size - 2, size - 1, 0))
                weights = low_weights(flow - SETTLING[b], DIFFUSIVITY[b])
            else:
                far, near, own = (here.rows(seg_ref, b, z) for z in (size - 2, size - 1, 0))
                weights = low_weights(flow, DIFFUSIVITY[b])
            up.append(far * weights[0] + near * weights[1])
            down.append(own)
        messages.append((up, down))
    here.write_across(send["y"], *messages[0], here.row == 0)
    here.write_across(send["z"], *messages[1], here.col == 0)
    kappa = here.by_bin(DIFFUSIVITY)
    flow = pltpu.roll(from_right, LANES // 2, 1)
    far, _ = low_weights(flow, kappa)
    _, near = low_weights(pltpu.roll(flow, 1, 1), kappa)
    weights = jnp.where(here.lane % 2 == 0, far, near)
    right = pair_sum(weights * here.last_columns(seg_ref, bins))
    here.write_tunnel(send["pair"], send["other"], right, here.first_columns(seg_ref, bins))


def second_inner_kernel(side, size, dust_ref, vel_ref, seg_ref, part_ref):
    here = Place(side, size, dust_ref.shape[-1])
    for b, y, f, rate in inner_rates(here, seg_ref, vel_ref):
        result = 0.5 * dust_ref[b, here.at(y), :] + 0.5 * (f + TIME_STEP * rate)
        part_ref[b, here.at(y), :] = here.off_wall(y, result)


def second_outer_kernel(side, size, part_ref, y_w, z_w, x_w, *refs):
    here = Place(side, size, part_ref.shape[-1])
    got = dict(zip(ORDER, refs[:4]))
    out_hbm, result, sems = refs[4:]
    adds = []
    for name, weights, at in (("y", y_w, here.row), ("z", z_w, here.col)):
        ref = got[name]
        hi = 0 if side == 2 else BINS
        add = []
        for b in range(BINS):
            nxt = jnp.where(at == side - 1, 0.0, ref[hi + b])
            add.append((ref[b], nxt * weights[b, 2], nxt * weights[b, 3]))
        adds.append(add)
    x_low, from_right = here.read_tunnel(got["pair"], got["other"])
    stores = [
        pltpu.make_async_copy(result.at[b], out_hbm.at[b], sems.at[b]) for b in range(BINS)
    ]
    for b, y, tile in add_halo(
        here, part_ref, y_w, z_w, x_w, adds[0], adds[1], x_low, from_right, 0.5
    ):
        result[b, here.at(y), :] = tile
        if y == size - 1:
            stores[b].start()
    for store in stores:
        store.wait()


def shift(block, axis, moves):
    return lax.ppermute(block, axis, [(s, moves(s)) for s in range(lax.axis_size(axis))])


def body(concentration, velocity):
    side = math.isqrt(lax.axis_size("sec"))
    tunnel = lax.axis_size("tun")
    size, length = concentration.shape[-2:]
    conc = concentration.reshape(BINS, size * size, length)
    vel = velocity.reshape(3, size * size, length)
    vmem = pl.BlockSpec(memory_space=pltpu.VMEM)
    hbm = pl.BlockSpec(memory_space=pltpu.HBM)

    def payload(up, down):
        planes = max(up, down) if side == 2 else up + down
        shapes = {"y": (planes, size, length), "z": (planes, size, length)}
        return [pltpu.VMEM(shapes.get(name, (size, LANES)), F32) for name in ORDER]

    def call(kernel, outs, *args):
        args = [pltpu.with_memory_space_constraint(arg, pltpu.VMEM) for arg in args]
        return pl.pallas_call(
            lambda *refs: kernel(side, size, *refs),
            out_shape=outs,
            in_specs=[vmem] * len(args),
            out_specs=[vmem] * len(outs),
            name=kernel.__name__,
        )(*args)

    def along_pair(s):
        return s + 1 - 2 * (s % 2)

    def along_other(s):
        return (s - 1 + 2 * (s % 2)) % tunnel

    def along_y(d):
        return lambda s: (s // side + d) % side * side + s % side

    def along_z(d):
        return lambda s: s // side * side + (s % side + d) % side

    def across(out, up, move):
        if side == 2:
            return shift(out, "sec", move(1))
        return jnp.concatenate(
            [shift(out[:up], "sec", move(1)), shift(out[up:], "sec", move(-1))], 0
        )

    def exchange(sends, up):
        moves = {
            "y": lambda out: across(out, up, along_y),
            "z": lambda out: across(out, up, along_z),
            "pair": lambda out: shift(out, "tun", along_pair),
            "other": lambda out: shift(out, "tun", along_other),
        }
        return [moves[name](out) for name, out in zip(ORDER, sends)]

    first, second = payload(2 * BINS, BINS + 1), payload(BINS, BINS)
    dust, vel, *sends = pl.pallas_call(
        lambda *refs: pack_kernel(side, size, *refs),
        out_shape=[pltpu.VMEM(conc.shape, F32), pltpu.VMEM(vel.shape, F32)] + first,
        in_specs=[hbm] * 2,
        out_specs=[vmem] * (2 + len(first)),
        scratch_shapes=[pltpu.SemaphoreType.DMA((2,))],
        name="pack_kernel",
    )(conc, vel)
    halo = exchange(sends, 2 * BINS)
    field = pltpu.VMEM(conc.shape, F32)
    weights = [pltpu.VMEM((BINS, 4, size, length), F32)] * 2 + [pltpu.VMEM((2, size, LANES), F32)]
    part, *weights = call(first_inner_kernel, [field] + weights, dust, vel)
    segment, *sends = call(first_outer_kernel, [field] + second, part, *weights, *halo)
    halo = exchange(sends, BINS)
    (part,) = call(second_inner_kernel, [field], dust, vel, segment)
    args = [pltpu.with_memory_space_constraint(a, pltpu.VMEM) for a in (part, *weights, *halo)]
    result = pl.pallas_call(
        lambda *refs: second_outer_kernel(side, size, *refs),
        out_shape=jax.ShapeDtypeStruct(conc.shape, F32),
        in_specs=[vmem] * len(args),
        out_specs=hbm,
        scratch_shapes=[pltpu.VMEM(conc.shape, F32), pltpu.SemaphoreType.DMA((BINS,))],
        name="second_outer_kernel",
    )(*args)
    return result.reshape(concentration.shape)


def solution(mesh):
    spec = P(None, "sec", None, None, "tun")
    return jax.shard_map(
        body, mesh=mesh, in_specs=(spec, spec), out_specs=spec, check_vma=False
    )
```

```python
import math

import jax
import jax.numpy as jnp
from jax import lax
from jax.experimental import pallas as pl
from jax.experimental.pallas import tpu as pltpu
from jax.sharding import PartitionSpec as P

TIME_STEP = 0.1
DIFFUSIVITY = (0.4, 0.15)
SETTLING = (0.05, 0.6)
BINS = 2
LANES = 128
ORDER = ("y", "z", "other", "pair")
SECOND = ("y", "z")
F32 = jnp.float32


def roll(tile, by):
    by %= LANES
    return pltpu.roll(tile, by, 1) if by else tile


class Place:
    def __init__(self, side, size, length):
        self.side, self.size, self.length = side, size, length
        place = lax.axis_index("sec")
        self.row, self.col = place // side, lax.rem(place, side)
        self.pair_right = lax.rem(lax.axis_index("tun"), 2) == 0
        self.shape = (size, length)
        self.z_at = lax.broadcasted_iota(jnp.int32, self.shape, 0)
        self.lane = lax.broadcasted_iota(jnp.int32, (size, LANES), 1)
        self.strip_x, self.strip_y = self.lane % 4, self.lane // 4 % size

    def off_wall(self, y, tile):
        wall = (self.z_at == 0) & (self.col == 0)
        if y == 0:
            wall = wall | (self.row == 0)
        return jnp.where(wall, 0.0, tile)

    def at(self, y):
        return slice(y * self.size, (y + 1) * self.size)

    def rows(self, ref, lead, z):
        rows = jnp.broadcast_to(ref[lead, z : z + 1, :], self.shape)
        for y in range(1, self.size):
            row = ref[lead, y * self.size + z : y * self.size + z + 1, :]
            rows = jnp.where(self.z_at == y, jnp.broadcast_to(row, self.shape), rows)
        return rows

    def columns(self, ref, leads, last, keep):
        packed = jnp.zeros((self.size, LANES), F32)
        for n, lead in enumerate(leads):
            for y in range(self.size):
                to = 4 * (n * self.size + y)
                if last:
                    tile = pltpu.roll(ref[lead, self.at(y), self.length - LANES :], (to + 4) % LANES, 1)
                else:
                    tile = ref[lead, self.at(y), :LANES]
                    tile = pltpu.roll(tile, to, 1) if to else tile
                packed = jnp.where((self.lane >= to + keep[0]) & (self.lane < to + keep[1]), tile, packed)
        return packed

    def for_bins(self, packed):
        return sum((roll(packed, b * 4 * self.size) for b in range(1, BINS)), packed)

    def by_bin(self, values):
        out = values[-1]
        for b in reversed(range(BINS - 1)):
            out = jnp.where(self.lane < 4 * self.size * (b + 1), values[b], out)
        return out

    def off_strip_wall(self, strip):
        z_at = lax.broadcasted_iota(jnp.int32, strip.shape, 0)
        wall = (z_at == 0) & (self.col == 0) | (self.strip_y == 0) & (self.row == 0)
        return jnp.where(wall, 0.0, strip)

    def write_across(self, out, up, down, forward):
        if self.side == 2:
            for i in range(out.shape[0]):
                if i >= len(down):
                    out[i] = up[i]
                elif i >= len(up):
                    out[i] = down[i]
                else:
                    out[i] = jnp.where(forward, up[i], down[i])
        else:
            for i, plane in enumerate(up + down):
                out[i] = plane

    def write_tunnel(self, pair, other, right, left):
        pair[...] = jnp.where(self.pair_right, right, left)
        other[...] = jnp.where(self.pair_right, left, right)

    def read_tunnel(self, pair, other):
        pair, other = pair[...], other[...]
        return jnp.where(self.pair_right, other, pair), jnp.where(self.pair_right, pair, other)


def low_weights(flow, kappa):
    return (-0.25 * TIME_STEP) * (flow + kappa), TIME_STEP * (flow + 2.0 * kappa)


def pack_kernel(side, size, conc_hbm, vel_hbm, dust_ref, vel_ref, *refs):
    *sends, sems = refs
    load = pltpu.make_async_copy(conc_hbm, dust_ref, sems.at[0])
    load_vel = pltpu.make_async_copy(vel_hbm, vel_ref, sems.at[1])
    load.start()
    load_vel.start()
    here = Place(side, size, dust_ref.shape[-1])
    load.wait()
    for b in range(BINS):
        for y in range(size):
            dust_ref[b, here.at(y), :] = here.off_wall(y, dust_ref[b, here.at(y), :])
    load_vel.wait()
    send = dict(zip(ORDER, sends))
    bins = range(BINS)
    ends = (size - 2, size - 1)
    here.write_across(
        send["y"],
        [dust_ref[b, here.at(y), :] for b in bins for y in ends],
        [dust_ref[b, here.at(0), :] for b in bins] + [vel_ref[0, here.at(0), :]],
        here.row == 0,
    )
    here.write_across(
        send["z"],
        [here.rows(dust_ref, b, z) for b in bins for z in ends],
        [here.rows(dust_ref, b, 0) for b in bins] + [here.rows(vel_ref, 1, 0)],
        here.col == 0,
    )
    half = LANES // 2
    u0, u1, u2 = (here.columns(vel_ref, [i], True, (2, 4)) for i in range(3))
    right = here.columns(dust_ref, bins, True, (0, 4))
    right += roll(u0, half) + roll(u1, half - 2) + roll(u2, half + 4 * size)
    u0, u1, u2 = (here.columns(vel_ref, [i], False, (0, 1)) for i in range(3))
    left = here.columns(dust_ref, bins, False, (0, 4))
    left += roll(u0, half) + roll(u1, half + 1) + roll(u2, half + 2)
    here.write_tunnel(send["pair"], send["other"], right, left)


def slope_and_bend(m1, p1, m2, p2):
    return (p1 - m1) - (p2 - m2), (p2 + m2) - 2.0 * (p1 + m1)


def inner_rates(here, field, vel_ref):
    size, length, shape = here.size, here.length, here.shape
    x_at = lax.broadcasted_iota(jnp.int32, shape, 1)
    weights = []
    for index, count in ((here.z_at, size), (x_at, length)):
        even = index % 2 == 0
        near, far = jnp.where(even, 0.5, 1.0), jnp.where(even, 0.25, 0.0)
        weights.append(
            (
                jnp.where(index == count - 1, 0.0, near),
                jnp.where(index == 0, 0.0, near),
                jnp.where(index == count - 2, 0.0, far),
                jnp.where(index == 0, 0.0, far),
            )
        )
    centre = jnp.where(here.z_at % 2 == 0, 3.5, 2.0) + jnp.where(x_at % 2 == 0, 3.5, 2.0)

    def along(f, axis, count):
        m1, p1, m2, p2 = weights[axis]
        return slope_and_bend(
            pltpu.roll(f * m1, 1, axis),
            pltpu.roll(f * p1, count - 1, axis),
            pltpu.roll(f * m2, 2, axis),
            pltpu.roll(f * p2, count - 2, axis),
        )

    zero = jnp.zeros(shape, F32)
    for b in range(BINS):
        kappa, settle = DIFFUSIVITY[b], SETTLING[b]

        def tile(y, b=b):
            return field[b, here.at(y), :] if 0 <= y < size else zero

        for y in range(size):
            f = tile(y)
            if y % 2 == 0:
                gy, ky = slope_and_bend(
                    tile(y - 1), tile(y + 1), 0.25 * tile(y - 2), 0.25 * tile(y + 2)
                )
                own = centre + 3.5
            else:
                gy, ky = 0.5 * (tile(y + 1) - tile(y - 1)), -(tile(y + 1) + tile(y - 1))
                own = centre + 2.0
            gz, kz = along(f, 0, size)
            gx, kx = along(f, 1, length)
            u0, u1, u2 = (vel_ref[i, here.at(y), :] for i in range(3))
            moved = (u0 - settle) * gy + u1 * gz + u2 * gx
            yield b, y, f, -(moved + kappa * (own * f + (ky + kz + kx)))


def first_inner_kernel(side, size, dust_ref, vel_ref, part_ref, y_w, z_w, x_w):
    here = Place(side, size, dust_ref.shape[-1])
    for b, y, f, rate in inner_rates(here, dust_ref, vel_ref):
        part_ref[b, here.at(y), :] = here.off_wall(y, f + TIME_STEP * rate)
    ends = (0, size - 2, size - 1)
    y_flow = [vel_ref[0, here.at(y), :] for y in ends]
    z_flow = [here.rows(vel_ref, 1, z) for z in ends]
    for b in range(BINS):
        kappa = DIFFUSIVITY[b]
        for out, flow in ((y_w, [u - SETTLING[b] for u in y_flow]), (z_w, z_flow)):
            out[b, 0], out[b, 1] = low_weights(flow[0], kappa)
            out[b, 2] = (0.25 * TIME_STEP) * (flow[1] - kappa)
            out[b, 3] = (-TIME_STEP) * (0.5 * flow[2] - kappa)
    kappa = here.by_bin(DIFFUSIVITY)
    even = here.lane % 2 == 0
    flow = here.for_bins(here.columns(vel_ref, [2], False, (0, 1)))
    far, _ = low_weights(roll(flow, 2), kappa)
    _, near = low_weights(roll(flow, 3), kappa)
    inside = here.strip_x >= 2
    x_w[0] = jnp.where(inside, jnp.where(even, far, near), 0.0)
    flow = here.for_bins(here.columns(vel_ref, [2], True, (2, 4)))
    far, near = (0.25 * TIME_STEP) * (flow - kappa), (-TIME_STEP) * (0.5 * flow - kappa)
    x_w[1] = jnp.where(inside, jnp.where(even, far, near), 0.0)


def add_halo(here, part_ref, x_w, y_add, z_add, low_strip, high_strip, share):
    size, length = here.size, here.length
    x_low = low_strip * (share * x_w[0])
    x_low = x_low + roll(x_low, -1)
    high = jnp.where(here.strip_x == 2, roll(high_strip, 2), roll(high_strip, 3))
    x_high = high * (share * x_w[1])
    first, last = here.lane == 0, here.lane >= LANES - 2
    for b in range(BINS):
        z_low, z_before, z_last = z_add[b]
        y_low, y_before, y_last = y_add[b]
        for y in range(size):
            tile = part_ref[b, here.at(y), :]

            def row(plane, y=y):
                return jnp.broadcast_to(plane[y : y + 1, :], here.shape)

            add = jnp.where(
                here.z_at == 0,
                row(z_low),
                jnp.where(here.z_at == size - 1, row(z_last), row(z_before)),
            )
            tile += share * jnp.where((here.z_at == 0) | (here.z_at >= size - 2), add, 0.0)
            for at, plane in ((0, y_low), (size - 2, y_before), (size - 1, y_last)):
                if y == at:
                    tile += share * plane
            to = 4 * (b * size + y) + 2
            low = jnp.where(first, roll(x_low, -to), 0.0)
            high = jnp.where(last, roll(x_high, -2 - to), 0.0)
            inner = [jnp.zeros((size, length - 2 * LANES), F32)] if length > 2 * LANES else []
            tile += jnp.concatenate([low] + inner + [high], 1)
            yield b, y, here.off_wall(y, tile)


def first_outer_kernel(side, size, part_ref, y_w, z_w, x_w, *refs):
    here = Place(side, size, part_ref.shape[-1])
    got = dict(zip(ORDER, refs[:4]))
    seg_ref, sends = refs[4], refs[5:]
    bins = range(BINS)
    adds, flows = [], []
    for name, weights, at in (("y", y_w, here.row), ("z", z_w, here.col)):
        ref = got[name]
        hi = 0 if side == 2 else 2 * BINS
        add = []
        for b in bins:
            low = ref[2 * b] * weights[b, 0] + ref[2 * b + 1] * weights[b, 1]
            nxt = jnp.where(at == side - 1, 0.0, ref[hi + b])
            add.append((low, nxt * weights[b, 2], nxt * weights[b, 3]))
        adds.append(add)
        flows.append(ref[hi + BINS])
    from_left, from_right = here.read_tunnel(got["pair"], got["other"])
    for b, y, tile in add_halo(
        here, part_ref, x_w, adds[0], adds[1], from_left, from_right, 1.0
    ):
        seg_ref[b, here.at(y), :] = tile
    strip = jnp.where(here.strip_x < 2, from_right, from_left)

    send = dict(zip(SECOND, sends))
    messages = []
    for axis, flow in enumerate(flows):
        up, down = [], []
        for b in bins:
            if axis == 0:
                far, near, own = (seg_ref[b, here.at(y), :] for y in (size - 2, size - 1, 0))
                weights = low_weights(flow - SETTLING[b], DIFFUSIVITY[b])
            else:
                far, near, own = (here.rows(seg_ref, b, z) for z in (size - 2, size - 1, 0))
                weights = low_weights(flow, DIFFUSIVITY[b])
            up.append(far * weights[0] + near * weights[1])
            down.append(own)
        messages.append((up, down))
    tiles = [slice(at, at + LANES) for at in range(0, here.length, LANES)]
    for name, (up, down), forward in zip(("y", "z"), messages, (here.row == 0, here.col == 0)):
        up, down = ([p[:, at] for p in planes for at in tiles] + [strip] for planes in (up, down))
        here.write_across(send[name], up, down, forward)


def stencil(even, c, m1, p1, m2, p2):
    g = jnp.where(even, p1 - m1 - 0.25 * (p2 - m2), 0.5 * (p1 - m1))
    k = jnp.where(even, 3.5 * c - 2.0 * (p1 + m1) + 0.25 * (p2 + m2), 2.0 * c - (p1 + m1))
    return g, k


def advance_strip(here, dust_ref, from_left, from_right, strip_w):
    size, half = here.size, LANES // 2
    bins = range(BINS)
    own_first = here.columns(dust_ref, bins, False, (0, 4))
    own_last = here.columns(dust_ref, bins, True, (0, 4))
    x, y = here.strip_x, here.strip_y
    z = lax.broadcasted_iota(jnp.int32, here.lane.shape, 0)
    used = (here.lane < 4 * size * BINS) & (x != 1)
    right, before = x == 0, x == 2
    c = jnp.where(right, from_right, from_left)
    c = jnp.where(used, c, 0.0)
    gx, kx = stencil(
        x != 3,
        c,
        jnp.where(right, roll(own_last, -3), roll(from_left, 1)),
        jnp.where(right, roll(from_right, -1), jnp.where(before, roll(from_left, -1), roll(own_first, 3))),
        jnp.where(right, roll(own_last, -2), roll(from_left, 2)),
        jnp.where(right, roll(from_right, -2), roll(own_first, 2)),
    )
    gy, ky = stencil(
        y % 2 == 0,
        c,
        jnp.where(y == 0, 0.0, roll(c, 4)),
        jnp.where(y == size - 1, 0.0, roll(c, -4)),
        jnp.where(y == 0, 0.0, roll(c, 8)),
        jnp.where(y == size - 2, 0.0, roll(c, -8)),
    )
    gz, kz = stencil(
        z % 2 == 0,
        c,
        jnp.where(z == 0, 0.0, pltpu.roll(c, 1, 0)),
        jnp.where(z == size - 1, 0.0, pltpu.roll(c, size - 1, 0)),
        jnp.where(z == 0, 0.0, pltpu.roll(c, 2, 0)),
        jnp.where(z == size - 2, 0.0, pltpu.roll(c, size - 2, 0)),
    )

    def flow(left_by, right_by):
        both = jnp.where(right, roll(from_right, right_by), roll(from_left, left_by))
        return here.for_bins(jnp.where(here.lane < 4 * size, both, 0.0))

    u0 = flow(-half, -half) - here.by_bin(SETTLING)
    u1 = flow(2 - half, -half - 1)
    u2 = flow(-half - 4 * size, -half - 2)
    kappa = here.by_bin(DIFFUSIVITY)
    rate = u0 * gy + u1 * gz + u2 * gx + kappa * (kx + ky + kz)
    done = jnp.where(used, here.off_strip_wall(c - TIME_STEP * rate), 0.0)
    n = 0
    for at, flow, place in ((y, u0, here.row), (z, u1, here.col)):
        far, near = low_weights(flow, kappa)
        low, inside = (at == 0) & (place > 0), place < here.side - 1
        for mask, weight in (
            (low, far),
            (low, near),
            ((at == size - 2) & inside, (0.25 * TIME_STEP) * (flow - kappa)),
            ((at == size - 1) & inside, (-TIME_STEP) * (0.5 * flow - kappa)),
        ):
            strip_w[n] = jnp.where(used & mask, here.off_strip_wall(weight), 0.0)
            n += 1
    return done


def second_inner_kernel(
    side, size, dust_ref, vel_ref, seg_ref, pair_in, other_in, part_ref, strip_ref, strip_w
):
    here = Place(side, size, dust_ref.shape[-1])
    for b, y, f, rate in inner_rates(here, seg_ref, vel_ref):
        result = 0.5 * dust_ref[b, here.at(y), :] + 0.5 * (f + TIME_STEP * rate)
        part_ref[b, here.at(y), :] = here.off_wall(y, result)
    from_left, from_right = here.read_tunnel(pair_in, other_in)
    strip_ref[...] = advance_strip(here, dust_ref, from_left, from_right, strip_w)


def second_outer_kernel(
    side, size, part_ref, y_w, z_w, x_w, strip_ref, strip_w, y_in, z_in, out_hbm, result, sems
):
    here = Place(side, size, part_ref.shape[-1])
    count = here.length // LANES
    hi = 0 if side == 2 else BINS * count + 1
    adds = []
    for ref, weights, at in ((y_in, y_w, here.row), (z_in, z_w, here.col)):
        add = []
        for b in range(BINS):
            low, nxt = (
                jnp.concatenate([ref[first + b * count + t] for t in range(count)], 1)
                for first in (0, hi)
            )
            nxt = jnp.where(at == side - 1, 0.0, nxt)
            add.append((low, nxt * weights[b, 2], nxt * weights[b, 3]))
        adds.append(add)
    low, high = y_in[BINS * count], y_in[hi + BINS * count]
    far, near = 4 * (size - 2), 4 * (size - 1)
    strip = strip_ref[...] + roll(low, -far) * strip_w[0] + roll(low, -near) * strip_w[1]
    strip += roll(high, far) * strip_w[2] + roll(high, near) * strip_w[3]
    low, high = z_in[BINS * count], z_in[hi + BINS * count]
    strip += pltpu.roll(low, 2, 0) * strip_w[4] + pltpu.roll(low, 1, 0) * strip_w[5]
    strip += pltpu.roll(high, size - 2, 0) * strip_w[6] + pltpu.roll(high, size - 1, 0) * strip_w[7]
    stores = [
        pltpu.make_async_copy(result.at[b], out_hbm.at[b], sems.at[b]) for b in range(BINS)
    ]
    for b, y, tile in add_halo(here, part_ref, x_w, adds[0], adds[1], strip, strip, 0.5):
        result[b, here.at(y), :] = tile
        if y == size - 1:
            stores[b].start()
    for store in stores:
        store.wait()


def shift(block, axis, moves):
    return lax.ppermute(block, axis, [(s, moves(s)) for s in range(lax.axis_size(axis))])


def body(concentration, velocity):
    side = math.isqrt(lax.axis_size("sec"))
    tunnel = lax.axis_size("tun")
    size, length = concentration.shape[-2:]
    conc = concentration.reshape(BINS, size * size, length)
    vel = velocity.reshape(3, size * size, length)
    vmem = pl.BlockSpec(memory_space=pltpu.VMEM)
    hbm = pl.BlockSpec(memory_space=pltpu.HBM)

    def planes(up, down):
        return max(up, down) if side == 2 else up + down

    def call(kernel, outs, *args):
        args = [pltpu.with_memory_space_constraint(arg, pltpu.VMEM) for arg in args]
        return pl.pallas_call(
            lambda *refs: kernel(side, size, *refs),
            out_shape=outs,
            in_specs=[vmem] * len(args),
            out_specs=[vmem] * len(outs),
            name=kernel.__name__,
        )(*args)

    def along_pair(s):
        return s + 1 - 2 * (s % 2)

    def along_other(s):
        return (s - 1 + 2 * (s % 2)) % tunnel

    def along_y(d):
        return lambda s: (s // side + d) % side * side + s % side

    def along_z(d):
        return lambda s: s // side * side + (s % side + d) % side

    def across(out, up, move):
        if side == 2:
            return shift(out, "sec", move(1))
        return jnp.concatenate(
            [shift(out[:up], "sec", move(1)), shift(out[up:], "sec", move(-1))], 0
        )

    moves = {
        "y": lambda out, up: across(out, up, along_y),
        "z": lambda out, up: across(out, up, along_z),
        "pair": lambda out, up: shift(out, "tun", along_pair),
        "other": lambda out, up: shift(out, "tun", along_other),
    }
    shapes = {name: (planes(2 * BINS, BINS + 1), size, length) for name in ("y", "z")}
    first = [pltpu.VMEM(shapes.get(name, (size, LANES)), F32) for name in ORDER]
    tiles = BINS * (length // LANES) + 1
    second = [pltpu.VMEM((planes(tiles, tiles), size, LANES), F32)] * 2
    dust, vel, *sends = pl.pallas_call(
        lambda *refs: pack_kernel(side, size, *refs),
        out_shape=[pltpu.VMEM(conc.shape, F32), pltpu.VMEM(vel.shape, F32)] + first,
        in_specs=[hbm] * 2,
        out_specs=[vmem] * (2 + len(first)),
        scratch_shapes=[pltpu.SemaphoreType.DMA((2,))],
        name="pack_kernel",
    )(conc, vel)
    halo = [moves[name](out, 2 * BINS) for name, out in zip(ORDER, sends)]
    field, strip = pltpu.VMEM(conc.shape, F32), (size, LANES)
    weights = [pltpu.VMEM((BINS, 4, size, length), F32)] * 2 + [pltpu.VMEM((2,) + strip, F32)]
    part, *weights = call(first_inner_kernel, [field] + weights, dust, vel)
    segment, *sends = call(first_outer_kernel, [field] + second, part, *weights, *halo)
    strips = [pltpu.VMEM(strip, F32), pltpu.VMEM((8,) + strip, F32)]
    got = dict(zip(ORDER, halo))
    part, *strips = call(
        second_inner_kernel, [field] + strips, dust, vel, segment, got["pair"], got["other"]
    )
    halo = [moves[name](out, tiles) for name, out in zip(SECOND, sends)]
    y_in, z_in = (halo[SECOND.index(name)] for name in ("y", "z"))
    args = (part, *weights, *strips, y_in, z_in)
    args = [pltpu.with_memory_space_constraint(arg, pltpu.VMEM) for arg in args]
    result = pl.pallas_call(
        lambda *refs: second_outer_kernel(side, size, *refs),
        out_shape=jax.ShapeDtypeStruct(conc.shape, F32),
        in_specs=[vmem] * len(args),
        out_specs=hbm,
        scratch_shapes=[pltpu.VMEM(conc.shape, F32), pltpu.SemaphoreType.DMA((BINS,))],
        name="second_outer_kernel",
    )(*args)
    return result.reshape(concentration.shape)


def solution(mesh):
    spec = P(None, "sec", None, None, "tun")
    return jax.shard_map(
        body, mesh=mesh, in_specs=(spec, spec), out_specs=spec, check_vma=False
    )
```

```python
import functools
import math

import jax
import jax.numpy as jnp
from jax import lax
from jax.experimental import pallas as pl
from jax.experimental.pallas import tpu as pltpu
from jax.sharding import PartitionSpec as P

TIME_STEP = 0.1
DIFFUSIVITY = (0.4, 0.15)
SETTLING = (0.05, 0.6)
BINS = 2
LANES = 128
FIRST = ("y", "other", "z", "pair")
SECOND = ("y", "z")
PAD = True
F32 = jnp.float32


def roll(tile, by):
    by %= LANES
    return pltpu.roll(tile, by, 1) if by else tile


class Place:
    def __init__(self, side, size, length):
        self.side, self.size, self.length = side, size, length
        place = lax.axis_index("sec")
        self.row, self.col = place // side, lax.rem(place, side)
        self.pair_right = lax.rem(lax.axis_index("tun"), 2) == 0
        self.shape = (size, length)
        self.z_at = lax.broadcasted_iota(jnp.int32, self.shape, 0)
        self.lane = lax.broadcasted_iota(jnp.int32, (size, LANES), 1)
        self.strip_x, self.strip_y = self.lane % 4, self.lane // 4 % size

    def off_wall(self, y, tile):
        wall = (self.z_at == 0) & (self.col == 0)
        if y == 0:
            wall = wall | (self.row == 0)
        return jnp.where(wall, 0.0, tile)

    def at(self, y):
        return slice(y * self.size, (y + 1) * self.size)

    def rows(self, ref, lead, z):
        rows = jnp.broadcast_to(ref[lead, z : z + 1, :], self.shape)
        for y in range(1, self.size):
            row = ref[lead, y * self.size + z : y * self.size + z + 1, :]
            rows = jnp.where(self.z_at == y, jnp.broadcast_to(row, self.shape), rows)
        return rows

    def columns(self, ref, leads, last, keep):
        packed = jnp.zeros((self.size, LANES), F32)
        for n, lead in enumerate(leads):
            for y in range(self.size):
                to = 4 * (n * self.size + y)
                if last:
                    tile = pltpu.roll(ref[lead, self.at(y), self.length - LANES :], (to + 4) % LANES, 1)
                else:
                    tile = ref[lead, self.at(y), :LANES]
                    tile = pltpu.roll(tile, to, 1) if to else tile
                packed = jnp.where((self.lane >= to + keep[0]) & (self.lane < to + keep[1]), tile, packed)
        return packed

    def for_bins(self, packed):
        return sum((roll(packed, b * 4 * self.size) for b in range(1, BINS)), packed)

    def by_bin(self, values):
        out = values[-1]
        for b in reversed(range(BINS - 1)):
            out = jnp.where(self.lane < 4 * self.size * (b + 1), values[b], out)
        return out

    def off_strip_wall(self, strip):
        z_at = lax.broadcasted_iota(jnp.int32, strip.shape, 0)
        wall = (z_at == 0) & (self.col == 0) | (self.strip_y == 0) & (self.row == 0)
        return jnp.where(wall, 0.0, strip)

    def only_neighbour(self, up, down, forward):
        count = max(len(up), len(down))
        up, down = up + down[len(up) :], down + up[len(down) :]
        return [jnp.where(forward, up[i], down[i]) for i in range(count)]

    def write_across(self, out, up, down, forward):
        planes = self.only_neighbour(up, down, forward) if self.side == 2 else up + down
        for i, plane in enumerate(planes):
            out[i] = plane

    def across(self, got, planes):
        z_in = [got["z"][i] for i in planes]
        return [got["y"][i] for i in planes], z_in

    def write_tunnel(self, pair, other, right, left):
        pair[...] = jnp.where(self.pair_right, right, left)
        if PAD:
            other[0] = jnp.where(self.pair_right, left, right)
            for i in range(1, other.shape[0]):
                other[i] = jnp.zeros(pair.shape, F32)
        else:
            other[...] = jnp.where(self.pair_right, left, right)

    def read_tunnel(self, pair, other):
        pair, other = pair[...], other[0] if PAD else other[...]
        return jnp.where(self.pair_right, other, pair), jnp.where(self.pair_right, pair, other)


def low_weights(flow, kappa):
    return (-0.25 * TIME_STEP) * (flow + kappa), TIME_STEP * (flow + 2.0 * kappa)


def pack_kernel(side, size, names, conc_hbm, vel_hbm, dust_ref, vel_ref, *refs):
    *sends, sems = refs
    load = pltpu.make_async_copy(conc_hbm, dust_ref, sems.at[0])
    load_vel = pltpu.make_async_copy(vel_hbm, vel_ref, sems.at[1])
    load.start()
    load_vel.start()
    here = Place(side, size, dust_ref.shape[-1])
    load.wait()
    for b in range(BINS):
        for y in range(size):
            dust_ref[b, here.at(y), :] = here.off_wall(y, dust_ref[b, here.at(y), :])
    send = dict(zip(names, sends))
    bins = range(BINS)
    ends = (size - 2, size - 1)
    y_up = [dust_ref[b, here.at(y), :] for b in bins for y in ends]
    y_down = [dust_ref[b, here.at(0), :] for b in bins]
    z_up = [here.rows(dust_ref, b, z) for b in bins for z in ends]
    z_down = [here.rows(dust_ref, b, 0) for b in bins]
    right = here.columns(dust_ref, bins, True, (0, 4))
    left = here.columns(dust_ref, bins, False, (0, 4))
    load_vel.wait()
    y_down.append(vel_ref[0, here.at(0), :])
    z_down.append(here.rows(vel_ref, 1, 0))
    here.write_across(send["y"], y_up, y_down, here.row == 0)
    here.write_across(send["z"], z_up, z_down, here.col == 0)
    half = LANES // 2
    u0, u1, u2 = (here.columns(vel_ref, [i], True, (2, 4)) for i in range(3))
    right += roll(u0, half) + roll(u1, half - 2) + roll(u2, half + 4 * size)
    u0, u1, u2 = (here.columns(vel_ref, [i], False, (0, 1)) for i in range(3))
    left += roll(u0, half) + roll(u1, half + 1) + roll(u2, half + 2)
    here.write_tunnel(send["pair"], send["other"], right, left)


def slope_and_bend(m1, p1, m2, p2):
    return (p1 - m1) - (p2 - m2), (p2 + m2) - 2.0 * (p1 + m1)


def inner_rates(here, field, vel_ref):
    size, length, shape = here.size, here.length, here.shape
    x_at = lax.broadcasted_iota(jnp.int32, shape, 1)
    weights = []
    for index, count in ((here.z_at, size), (x_at, length)):
        even = index % 2 == 0
        near, far = jnp.where(even, 0.5, 1.0), jnp.where(even, 0.25, 0.0)
        weights.append(
            (
                jnp.where(index == count - 1, 0.0, near),
                jnp.where(index == 0, 0.0, near),
                jnp.where(index == count - 2, 0.0, far),
                jnp.where(index == 0, 0.0, far),
            )
        )
    centre = jnp.where(here.z_at % 2 == 0, 3.5, 2.0) + jnp.where(x_at % 2 == 0, 3.5, 2.0)

    def along(f, axis, count):
        m1, p1, m2, p2 = weights[axis]
        return slope_and_bend(
            pltpu.roll(f * m1, 1, axis),
            pltpu.roll(f * p1, count - 1, axis),
            pltpu.roll(f * m2, 2, axis),
            pltpu.roll(f * p2, count - 2, axis),
        )

    zero = jnp.zeros(shape, F32)
    for b in range(BINS):
        kappa, settle = DIFFUSIVITY[b], SETTLING[b]

        def tile(y, b=b):
            return field[b, here.at(y), :] if 0 <= y < size else zero

        for y in range(size):
            f = tile(y)
            if y % 2 == 0:
                gy, ky = slope_and_bend(
                    tile(y - 1), tile(y + 1), 0.25 * tile(y - 2), 0.25 * tile(y + 2)
                )
                own = centre + 3.5
            else:
                gy, ky = 0.5 * (tile(y + 1) - tile(y - 1)), -(tile(y + 1) + tile(y - 1))
                own = centre + 2.0
            gz, kz = along(f, 0, size)
            gx, kx = along(f, 1, length)
            u0, u1, u2 = (vel_ref[i, here.at(y), :] for i in range(3))
            moved = (u0 - settle) * gy + u1 * gz + u2 * gx
            yield b, y, f, -(moved + kappa * (own * f + (ky + kz + kx)))


def first_inner_kernel(side, size, dust_ref, vel_ref, part_ref, y_w, z_w, x_w):
    here = Place(side, size, dust_ref.shape[-1])
    for b, y, f, rate in inner_rates(here, dust_ref, vel_ref):
        part_ref[b, here.at(y), :] = here.off_wall(y, f + TIME_STEP * rate)
    ends = (0, size - 2, size - 1)
    y_flow = [vel_ref[0, here.at(y), :] for y in ends]
    z_flow = [here.rows(vel_ref, 1, z) for z in ends]
    for b in range(BINS):
        kappa = DIFFUSIVITY[b]
        for out, flow in ((y_w, [u - SETTLING[b] for u in y_flow]), (z_w, z_flow)):
            out[b, 0], out[b, 1] = low_weights(flow[0], kappa)
            out[b, 2] = (0.25 * TIME_STEP) * (flow[1] - kappa)
            out[b, 3] = (-TIME_STEP) * (0.5 * flow[2] - kappa)
    kappa = here.by_bin(DIFFUSIVITY)
    even = here.lane % 2 == 0
    flow = here.for_bins(here.columns(vel_ref, [2], False, (0, 1)))
    far, _ = low_weights(roll(flow, 2), kappa)
    _, near = low_weights(roll(flow, 3), kappa)
    inside = here.strip_x >= 2
    x_w[0] = jnp.where(inside, jnp.where(even, far, near), 0.0)
    flow = here.for_bins(here.columns(vel_ref, [2], True, (2, 4)))
    far, near = (0.25 * TIME_STEP) * (flow - kappa), (-TIME_STEP) * (0.5 * flow - kappa)
    x_w[1] = jnp.where(inside, jnp.where(even, far, near), 0.0)


def add_halo(here, part_ref, x_w, y_add, z_add, low_strip, high_strip, share):
    size, length = here.size, here.length
    x_low = low_strip * (share * x_w[0])
    x_low = x_low + roll(x_low, -1)
    high = jnp.where(here.strip_x == 2, roll(high_strip, 2), roll(high_strip, 3))
    x_high = high * (share * x_w[1])
    first, last = here.lane == 0, here.lane >= LANES - 2
    for b in range(BINS):
        z_low, z_before, z_last = z_add[b]
        y_low, y_before, y_last = y_add[b]
        for y in range(size):
            tile = part_ref[b, here.at(y), :]

            def row(plane, y=y):
                return jnp.broadcast_to(plane[y : y + 1, :], here.shape)

            add = jnp.where(
                here.z_at == 0,
                row(z_low),
                jnp.where(here.z_at == size - 1, row(z_last), row(z_before)),
            )
            tile += share * jnp.where((here.z_at == 0) | (here.z_at >= size - 2), add, 0.0)
            for at, plane in ((0, y_low), (size - 2, y_before), (size - 1, y_last)):
                if y == at:
                    tile += share * plane
            to = 4 * (b * size + y) + 2
            low = jnp.where(first, roll(x_low, -to), 0.0)
            high = jnp.where(last, roll(x_high, -2 - to), 0.0)
            inner = [jnp.zeros((size, length - 2 * LANES), F32)] if length > 2 * LANES else []
            tile += jnp.concatenate([low] + inner + [high], 1)
            yield b, y, here.off_wall(y, tile)


def first_outer_kernel(side, size, part_ref, y_w, z_w, x_w, *refs, names, second):
    here = Place(side, size, part_ref.shape[-1])
    halos = len(names)
    got = dict(zip(names, refs[:halos]))
    seg_ref, sends = refs[halos], refs[halos + 1 :]
    bins = range(BINS)
    adds, flows = [], []
    planes = range(got["z"].shape[0])
    y_in, z_in = here.across(got, planes)
    for ref, weights, at in ((y_in, y_w, here.row), (z_in, z_w, here.col)):
        hi = 0 if side == 2 else 2 * BINS
        add = []
        for b in bins:
            low = ref[2 * b] * weights[b, 0] + ref[2 * b + 1] * weights[b, 1]
            nxt = jnp.where(at == side - 1, 0.0, ref[hi + b])
            add.append((low, nxt * weights[b, 2], nxt * weights[b, 3]))
        adds.append(add)
        flows.append(ref[hi + BINS])
    from_left, from_right = here.read_tunnel(got["pair"], got["other"])
    for b, y, tile in add_halo(
        here, part_ref, x_w, adds[0], adds[1], from_left, from_right, 1.0
    ):
        seg_ref[b, here.at(y), :] = tile
    strip = jnp.where(here.strip_x < 2, from_right, from_left)

    send = dict(zip(second, sends))
    messages = []
    for axis, flow in enumerate(flows):
        up, down = [], []
        for b in bins:
            if axis == 0:
                far, near, own = (seg_ref[b, here.at(y), :] for y in (size - 2, size - 1, 0))
                weights = low_weights(flow - SETTLING[b], DIFFUSIVITY[b])
            else:
                far, near, own = (here.rows(seg_ref, b, z) for z in (size - 2, size - 1, 0))
                weights = low_weights(flow, DIFFUSIVITY[b])
            up.append(far * weights[0] + near * weights[1])
            down.append(own)
        messages.append((up, down))
    tiles = [slice(at, at + LANES) for at in range(0, here.length, LANES)]
    for name, (up, down), forward in zip(("y", "z"), messages, (here.row == 0, here.col == 0)):
        up, down = ([p[:, at] for p in planes for at in tiles] + [strip] for planes in (up, down))
        here.write_across(send[name], up, down, forward)


def stencil(even, c, m1, p1, m2, p2):
    g = jnp.where(even, p1 - m1 - 0.25 * (p2 - m2), 0.5 * (p1 - m1))
    k = jnp.where(even, 3.5 * c - 2.0 * (p1 + m1) + 0.25 * (p2 + m2), 2.0 * c - (p1 + m1))
    return g, k


def advance_strip(here, dust_ref, from_left, from_right, strip_w):
    size, half = here.size, LANES // 2
    bins = range(BINS)
    own_first = here.columns(dust_ref, bins, False, (0, 4))
    own_last = here.columns(dust_ref, bins, True, (0, 4))
    x, y = here.strip_x, here.strip_y
    z = lax.broadcasted_iota(jnp.int32, here.lane.shape, 0)
    used = (here.lane < 4 * size * BINS) & (x != 1)
    right, before = x == 0, x == 2
    c = jnp.where(right, from_right, from_left)
    c = jnp.where(used, c, 0.0)
    gx, kx = stencil(
        x != 3,
        c,
        jnp.where(right, roll(own_last, -3), roll(from_left, 1)),
        jnp.where(right, roll(from_right, -1), jnp.where(before, roll(from_left, -1), roll(own_first, 3))),
        jnp.where(right, roll(own_last, -2), roll(from_left, 2)),
        jnp.where(right, roll(from_right, -2), roll(own_first, 2)),
    )
    gy, ky = stencil(
        y % 2 == 0,
        c,
        jnp.where(y == 0, 0.0, roll(c, 4)),
        jnp.where(y == size - 1, 0.0, roll(c, -4)),
        jnp.where(y == 0, 0.0, roll(c, 8)),
        jnp.where(y == size - 2, 0.0, roll(c, -8)),
    )
    gz, kz = stencil(
        z % 2 == 0,
        c,
        jnp.where(z == 0, 0.0, pltpu.roll(c, 1, 0)),
        jnp.where(z == size - 1, 0.0, pltpu.roll(c, size - 1, 0)),
        jnp.where(z == 0, 0.0, pltpu.roll(c, 2, 0)),
        jnp.where(z == size - 2, 0.0, pltpu.roll(c, size - 2, 0)),
    )

    def flow(left_by, right_by):
        both = jnp.where(right, roll(from_right, right_by), roll(from_left, left_by))
        return here.for_bins(jnp.where(here.lane < 4 * size, both, 0.0))

    u0 = flow(-half, -half) - here.by_bin(SETTLING)
    u1 = flow(2 - half, -half - 1)
    u2 = flow(-half - 4 * size, -half - 2)
    kappa = here.by_bin(DIFFUSIVITY)
    rate = u0 * gy + u1 * gz + u2 * gx + kappa * (kx + ky + kz)
    done = jnp.where(used, here.off_strip_wall(c - TIME_STEP * rate), 0.0)
    n = 0
    for at, flow, place in ((y, u0, here.row), (z, u1, here.col)):
        far, near = low_weights(flow, kappa)
        low, inside = (at == 0) & (place > 0), place < here.side - 1
        for mask, weight in (
            (low, far),
            (low, near),
            ((at == size - 2) & inside, (0.25 * TIME_STEP) * (flow - kappa)),
            ((at == size - 1) & inside, (-TIME_STEP) * (0.5 * flow - kappa)),
        ):
            strip_w[n] = jnp.where(used & mask, here.off_strip_wall(weight), 0.0)
            n += 1
    return done


def second_inner_kernel(
    side, size, dust_ref, vel_ref, seg_ref, pair_in, other_in, part_ref, strip_ref, strip_w
):
    here = Place(side, size, dust_ref.shape[-1])
    for b, y, f, rate in inner_rates(here, seg_ref, vel_ref):
        result = 0.5 * dust_ref[b, here.at(y), :] + 0.5 * (f + TIME_STEP * rate)
        part_ref[b, here.at(y), :] = here.off_wall(y, result)
    from_left, from_right = here.read_tunnel(pair_in, other_in)
    strip_ref[...] = advance_strip(here, dust_ref, from_left, from_right, strip_w)


def second_outer_kernel(
    side, size, names, part_ref, y_w, z_w, x_w, strip_ref, strip_w, *refs
):
    halos = len(names)
    got = dict(zip(names, refs[:halos]))
    out_hbm, result, sems = refs[halos:]
    here = Place(side, size, part_ref.shape[-1])
    count = here.length // LANES
    y_in, z_in = here.across(got, range(got["z"].shape[0]))
    hi = 0 if side == 2 else BINS * count + 1
    adds = []
    for ref, weights, at in ((y_in, y_w, here.row), (z_in, z_w, here.col)):
        add = []
        for b in range(BINS):
            low, nxt = (
                jnp.concatenate([ref[first + b * count + t] for t in range(count)], 1)
                for first in (0, hi)
            )
            nxt = jnp.where(at == side - 1, 0.0, nxt)
            add.append((low, nxt * weights[b, 2], nxt * weights[b, 3]))
        adds.append(add)
    low, high = y_in[BINS * count], y_in[hi + BINS * count]
    far, near = 4 * (size - 2), 4 * (size - 1)
    strip = strip_ref[...] + roll(low, -far) * strip_w[0] + roll(low, -near) * strip_w[1]
    strip += roll(high, far) * strip_w[2] + roll(high, near) * strip_w[3]
    low, high = z_in[BINS * count], z_in[hi + BINS * count]
    strip += pltpu.roll(low, 2, 0) * strip_w[4] + pltpu.roll(low, 1, 0) * strip_w[5]
    strip += pltpu.roll(high, size - 2, 0) * strip_w[6] + pltpu.roll(high, size - 1, 0) * strip_w[7]
    stores = [
        pltpu.make_async_copy(result.at[b], out_hbm.at[b], sems.at[b]) for b in range(BINS)
    ]
    for b, y, tile in add_halo(here, part_ref, x_w, adds[0], adds[1], strip, strip, 0.5):
        result[b, here.at(y), :] = tile
        if y == size - 1:
            stores[b].start()
    for store in stores:
        store.wait()


def shift(block, axis, moves):
    return lax.ppermute(block, axis, [(s, moves(s)) for s in range(lax.axis_size(axis))])


def body(concentration, velocity):
    side = math.isqrt(lax.axis_size("sec"))
    tunnel = lax.axis_size("tun")
    size, length = concentration.shape[-2:]
    conc = concentration.reshape(BINS, size * size, length)
    vel = velocity.reshape(3, size * size, length)
    vmem = pl.BlockSpec(memory_space=pltpu.VMEM)
    hbm = pl.BlockSpec(memory_space=pltpu.HBM)

    def planes(up, down):
        return max(up, down) if side == 2 else up + down

    def call(kernel, outs, *args):
        args = [pltpu.with_memory_space_constraint(arg, pltpu.VMEM) for arg in args]
        return pl.pallas_call(
            lambda *refs: kernel(side, size, *refs),
            out_shape=outs,
            in_specs=[vmem] * len(args),
            out_specs=[vmem] * len(outs),
            name=getattr(kernel, "func", kernel).__name__,
        )(*args)

    def along_pair(s):
        return s + 1 - 2 * (s % 2)

    def along_other(s):
        return (s - 1 + 2 * (s % 2)) % tunnel

    def along_y(d):
        return lambda s: (s // side + d) % side * side + s % side

    def along_z(d):
        return lambda s: s // side * side + (s % side + d) % side

    def across(out, up, move):
        if side == 2:
            return shift(out, "sec", move(1))
        return jnp.concatenate(
            [shift(out[:up], "sec", move(1)), shift(out[up:], "sec", move(-1))], 0
        )

    moves = {
        "y": lambda out, up: across(out, up, along_y),
        "z": lambda out, up: across(out, up, along_z),
        "pair": lambda out, up: shift(out, "tun", along_pair),
        "other": lambda out, up: shift(out, "tun", along_other),
    }
    across_shape = (planes(2 * BINS, BINS + 1), size, length)
    shapes = {"pair": (size, LANES), "other": (planes(4, 4) * 2, size, LANES) if PAD else (size, LANES)}
    first = [pltpu.VMEM(shapes.get(name, across_shape), F32) for name in FIRST]
    tiles = BINS * (length // LANES) + 1
    second = [pltpu.VMEM((planes(tiles, tiles), size, LANES), F32)] * len(SECOND)
    dust, vel, *sends = pl.pallas_call(
        lambda *refs: pack_kernel(side, size, FIRST, *refs),
        out_shape=[pltpu.VMEM(conc.shape, F32), pltpu.VMEM(vel.shape, F32)] + first,
        in_specs=[hbm] * 2,
        out_specs=[vmem] * (2 + len(first)),
        scratch_shapes=[pltpu.SemaphoreType.DMA((2,))],
        name="pack_kernel",
    )(conc, vel)
    halo = [moves[name](out, 2 * BINS) for name, out in zip(FIRST, sends)]
    field, strip = pltpu.VMEM(conc.shape, F32), (size, LANES)
    weights = [pltpu.VMEM((BINS, 4, size, length), F32)] * 2 + [pltpu.VMEM((2,) + strip, F32)]
    part, *weights = call(first_inner_kernel, [field] + weights, dust, vel)
    segment, *sends = call(functools.partial(first_outer_kernel, names=FIRST, second=SECOND), [field] + second, part, *weights, *halo)
    strips = [pltpu.VMEM(strip, F32), pltpu.VMEM((8,) + strip, F32)]
    got = dict(zip(FIRST, halo))
    part, *strips = call(
        second_inner_kernel, [field] + strips, dust, vel, segment, got["pair"], got["other"]
    )
    halo = [moves[name](out, tiles) for name, out in zip(SECOND, sends)]
    args = (part, *weights, *strips, *halo)
    args = [pltpu.with_memory_space_constraint(arg, pltpu.VMEM) for arg in args]
    result = pl.pallas_call(
        lambda *refs: second_outer_kernel(side, size, SECOND, *refs),
        out_shape=jax.ShapeDtypeStruct(conc.shape, F32),
        in_specs=[vmem] * len(args),
        out_specs=hbm,
        scratch_shapes=[pltpu.VMEM(conc.shape, F32), pltpu.SemaphoreType.DMA((BINS,))],
        name="second_outer_kernel",
    )(*args)
    return result.reshape(concentration.shape)


def solution(mesh):
    spec = P(None, "sec", None, None, "tun")
    return jax.shard_map(
        body, mesh=mesh, in_specs=(spec, spec), out_specs=spec, check_vma=False
    )
```

```python
import math

import jax
import jax.numpy as jnp
from jax import lax
from jax.experimental import pallas as pl
from jax.experimental.pallas import tpu as pltpu
from jax.sharding import PartitionSpec as P

TIME_STEP = 0.1
DIFFUSIVITY = (0.4, 0.15)
SETTLING = (0.05, 0.6)
BINS = 2
LANES = 128
FIRST = ("y", "other", "z", "pair")
SECOND = ("y", "z")
F32 = jnp.float32


def roll(tile, by):
    by %= LANES
    return pltpu.roll(tile, by, 1) if by else tile


class Place:
    def __init__(self, side, size, length):
        self.side, self.size, self.length = side, size, length
        place = lax.axis_index("sec")
        self.row, self.col = place // side, lax.rem(place, side)
        self.pair_right = lax.rem(lax.axis_index("tun"), 2) == 0
        self.shape = (size, length)
        self.z_at = lax.broadcasted_iota(jnp.int32, self.shape, 0)
        self.lane = lax.broadcasted_iota(jnp.int32, (size, LANES), 1)
        self.strip_x, self.strip_y = self.lane % 4, self.lane // 4 % size

    def off_wall(self, y, tile):
        wall = (self.z_at == 0) & (self.col == 0)
        if y == 0:
            wall = wall | (self.row == 0)
        return jnp.where(wall, 0.0, tile)

    def at(self, y):
        return slice(y * self.size, (y + 1) * self.size)

    def rows(self, ref, lead, z):
        rows = jnp.broadcast_to(ref[lead, z : z + 1, :], self.shape)
        for y in range(1, self.size):
            row = ref[lead, y * self.size + z : y * self.size + z + 1, :]
            rows = jnp.where(self.z_at == y, jnp.broadcast_to(row, self.shape), rows)
        return rows

    def columns(self, ref, leads, last, keep):
        packed = jnp.zeros((self.size, LANES), F32)
        for n, lead in enumerate(leads):
            for y in range(self.size):
                to = 4 * (n * self.size + y)
                if last:
                    tile = pltpu.roll(ref[lead, self.at(y), self.length - LANES :], (to + 4) % LANES, 1)
                else:
                    tile = ref[lead, self.at(y), :LANES]
                    tile = pltpu.roll(tile, to, 1) if to else tile
                packed = jnp.where((self.lane >= to + keep[0]) & (self.lane < to + keep[1]), tile, packed)
        return packed

    def for_bins(self, packed):
        return sum((roll(packed, b * 4 * self.size) for b in range(1, BINS)), packed)

    def by_bin(self, values):
        out = values[-1]
        for b in reversed(range(BINS - 1)):
            out = jnp.where(self.lane < 4 * self.size * (b + 1), values[b], out)
        return out

    def off_strip_wall(self, strip):
        z_at = lax.broadcasted_iota(jnp.int32, strip.shape, 0)
        wall = (z_at == 0) & (self.col == 0) | (self.strip_y == 0) & (self.row == 0)
        return jnp.where(wall, 0.0, strip)

    def only_neighbour(self, up, down, forward):
        count = max(len(up), len(down))
        up, down = up + down[len(up) :], down + up[len(down) :]
        return [jnp.where(forward, up[i], down[i]) for i in range(count)]

    def write_across(self, out, up, down, forward):
        planes = self.only_neighbour(up, down, forward) if self.side == 2 else up + down
        for i, plane in enumerate(planes):
            out[i] = plane
        for i in range(len(planes), out.shape[0]):
            out[i] = jnp.zeros(out.shape[1:], F32)

    def across(self, got, planes):
        z_in = [got["z"][i] for i in planes]
        return [got["y"][i] for i in planes], z_in

    def write_tunnel(self, pair, other, right, left):
        pair[...] = jnp.where(self.pair_right, right, left)
        other[0] = jnp.where(self.pair_right, left, right)
        for i in range(1, other.shape[0]):
            other[i] = jnp.zeros(pair.shape, F32)

    def read_tunnel(self, pair, other):
        pair, other = pair[...], other[0]
        return jnp.where(self.pair_right, other, pair), jnp.where(self.pair_right, pair, other)


def low_weights(flow, kappa):
    return (-0.25 * TIME_STEP) * (flow + kappa), TIME_STEP * (flow + 2.0 * kappa)


def pack_kernel(side, size, names, conc_hbm, vel_hbm, dust_ref, vel_ref, *refs):
    *sends, sems = refs
    load = pltpu.make_async_copy(conc_hbm, dust_ref, sems.at[0])
    load_vel = pltpu.make_async_copy(vel_hbm, vel_ref, sems.at[1])
    load.start()
    load_vel.start()
    here = Place(side, size, dust_ref.shape[-1])
    load.wait()
    for b in range(BINS):
        for y in range(size):
            dust_ref[b, here.at(y), :] = here.off_wall(y, dust_ref[b, here.at(y), :])
    send = dict(zip(names, sends))
    bins = range(BINS)
    ends = (size - 2, size - 1)
    y_up = [dust_ref[b, here.at(y), :] for b in bins for y in ends]
    y_down = [dust_ref[b, here.at(0), :] for b in bins]
    z_up = [here.rows(dust_ref, b, z) for b in bins for z in ends]
    z_down = [here.rows(dust_ref, b, 0) for b in bins]
    right = here.columns(dust_ref, bins, True, (0, 4))
    left = here.columns(dust_ref, bins, False, (0, 4))
    load_vel.wait()
    y_up += [vel_ref[1, here.at(y), :] for y in ends]
    y_down += [vel_ref[i, here.at(0), :] for i in (0, 1)]
    z_down.append(here.rows(vel_ref, 1, 0))
    here.write_across(send["y"], y_up, y_down, here.row == 0)
    here.write_across(send["z"], z_up, z_down, here.col == 0)
    half = LANES // 2
    u0, u1, u2 = (here.columns(vel_ref, [i], True, (2, 4)) for i in range(3))
    right += roll(u0, half) + roll(u1, half - 2) + roll(u2, half + 4 * size)
    u0, u1, u2 = (here.columns(vel_ref, [i], False, (0, 1)) for i in range(3))
    left += roll(u0, half) + roll(u1, half + 1) + roll(u2, half + 2)
    here.write_tunnel(send["pair"], send["other"], right, left)


def slope_and_bend(m1, p1, m2, p2):
    return (p1 - m1) - (p2 - m2), (p2 + m2) - 2.0 * (p1 + m1)


def inner_rates(here, field, vel_ref):
    size, length, shape = here.size, here.length, here.shape
    x_at = lax.broadcasted_iota(jnp.int32, shape, 1)
    weights = []
    for index, count in ((here.z_at, size), (x_at, length)):
        even = index % 2 == 0
        near, far = jnp.where(even, 0.5, 1.0), jnp.where(even, 0.25, 0.0)
        weights.append(
            (
                jnp.where(index == count - 1, 0.0, near),
                jnp.where(index == 0, 0.0, near),
                jnp.where(index == count - 2, 0.0, far),
                jnp.where(index == 0, 0.0, far),
            )
        )
    centre = jnp.where(here.z_at % 2 == 0, 3.5, 2.0) + jnp.where(x_at % 2 == 0, 3.5, 2.0)

    def along(f, axis, count):
        m1, p1, m2, p2 = weights[axis]
        return slope_and_bend(
            pltpu.roll(f * m1, 1, axis),
            pltpu.roll(f * p1, count - 1, axis),
            pltpu.roll(f * m2, 2, axis),
            pltpu.roll(f * p2, count - 2, axis),
        )

    zero = jnp.zeros(shape, F32)
    for b in range(BINS):
        kappa, settle = DIFFUSIVITY[b], SETTLING[b]

        def tile(y, b=b):
            return field[b, here.at(y), :] if 0 <= y < size else zero

        for y in range(size):
            f = tile(y)
            if y % 2 == 0:
                gy, ky = slope_and_bend(
                    tile(y - 1), tile(y + 1), 0.25 * tile(y - 2), 0.25 * tile(y + 2)
                )
                own = centre + 3.5
            else:
                gy, ky = 0.5 * (tile(y + 1) - tile(y - 1)), -(tile(y + 1) + tile(y - 1))
                own = centre + 2.0
            gz, kz = along(f, 0, size)
            gx, kx = along(f, 1, length)
            u0, u1, u2 = (vel_ref[i, here.at(y), :] for i in range(3))
            moved = (u0 - settle) * gy + u1 * gz + u2 * gx
            yield b, y, f, -(moved + kappa * (own * f + (ky + kz + kx)))


def first_inner_kernel(side, size, dust_ref, vel_ref, part_ref, y_w, z_w, x_w):
    here = Place(side, size, dust_ref.shape[-1])
    for b, y, f, rate in inner_rates(here, dust_ref, vel_ref):
        part_ref[b, here.at(y), :] = here.off_wall(y, f + TIME_STEP * rate)
    ends = (0, size - 2, size - 1)
    y_flow = [vel_ref[0, here.at(y), :] for y in ends]
    z_flow = [here.rows(vel_ref, 1, z) for z in ends]
    for b in range(BINS):
        kappa = DIFFUSIVITY[b]
        for out, flow in ((y_w, [u - SETTLING[b] for u in y_flow]), (z_w, z_flow)):
            out[b, 0], out[b, 1] = low_weights(flow[0], kappa)
            out[b, 2] = (0.25 * TIME_STEP) * (flow[1] - kappa)
            out[b, 3] = (-TIME_STEP) * (0.5 * flow[2] - kappa)
    kappa = here.by_bin(DIFFUSIVITY)
    even = here.lane % 2 == 0
    flow = here.for_bins(here.columns(vel_ref, [2], False, (0, 1)))
    far, _ = low_weights(roll(flow, 2), kappa)
    _, near = low_weights(roll(flow, 3), kappa)
    inside = here.strip_x >= 2
    x_w[0] = jnp.where(inside, jnp.where(even, far, near), 0.0)
    flow = here.for_bins(here.columns(vel_ref, [2], True, (2, 4)))
    far, near = (0.25 * TIME_STEP) * (flow - kappa), (-TIME_STEP) * (0.5 * flow - kappa)
    x_w[1] = jnp.where(inside, jnp.where(even, far, near), 0.0)


def add_halo(here, part_ref, x_w, y_add, z_add, low_strip, high_strip, share, rows=None):
    size, length = here.size, here.length
    x_low = low_strip * (share * x_w[0])
    x_low = x_low + roll(x_low, -1)
    high = jnp.where(here.strip_x == 2, roll(high_strip, 2), roll(high_strip, 3))
    x_high = high * (share * x_w[1])
    first, last = here.lane == 0, here.lane >= LANES - 2
    for b in range(BINS):
        y_low, y_before, y_last = y_add[b]
        for y in rows or range(size):
            tile = part_ref[b, here.at(y), :]

            if z_add is not None:
                z_low, z_before, z_last = (
                    jnp.broadcast_to(plane[y : y + 1, :], here.shape) for plane in z_add[b]
                )
                add = jnp.where(
                    here.z_at == 0, z_low, jnp.where(here.z_at == size - 1, z_last, z_before)
                )
                tile += share * jnp.where((here.z_at == 0) | (here.z_at >= size - 2), add, 0.0)
            for at, plane in ((0, y_low), (size - 2, y_before), (size - 1, y_last)):
                if y == at:
                    tile += share * plane
            to = 4 * (b * size + y) + 2
            low = jnp.where(first, roll(x_low, -to), 0.0)
            high = jnp.where(last, roll(x_high, -2 - to), 0.0)
            inner = [jnp.zeros((size, length - 2 * LANES), F32)] if length > 2 * LANES else []
            tile += jnp.concatenate([low] + inner + [high], 1)
            yield b, y, here.off_wall(y, tile)


def y_halo(here, ref, weights):
    hi = 0 if here.side == 2 else 2 * BINS + 2
    adds = []
    for b in range(BINS):
        low = ref[2 * b] * weights[b, 0] + ref[2 * b + 1] * weights[b, 1]
        nxt = jnp.where(here.row == here.side - 1, 0.0, ref[hi + b])
        adds.append((low, nxt * weights[b, 2], nxt * weights[b, 3]))
    return adds, ref[hi + BINS]


def in_tiles(here, planes):
    return [p[:, at : at + LANES] for p in planes for at in range(0, here.length, LANES)]


def first_y_kernel(side, size, part_ref, y_w, x_w, y_in, pair_in, other_in, y_out):
    here = Place(side, size, part_ref.shape[-1])
    adds, flow = y_halo(here, y_in, y_w)
    from_left, from_right = here.read_tunnel(pair_in, other_in)
    ends = (0, size - 2, size - 1)
    tiles = {
        (b, y): tile
        for b, y, tile in add_halo(
            here, part_ref, x_w, adds, None, from_left, from_right, 1.0, ends
        )
    }
    up, down = [], []
    for b in range(BINS):
        far, near = low_weights(flow - SETTLING[b], DIFFUSIVITY[b])
        up.append(tiles[b, size - 2] * far + tiles[b, size - 1] * near)
        down.append(tiles[b, 0])
    strip = jnp.where(here.strip_x < 2, from_right, from_left)
    up, down = (in_tiles(here, planes) + [strip] for planes in (up, down))
    here.write_across(y_out, up, down, here.row == 0)


def first_outer_kernel(
    side, size, part_ref, y_w, z_w, x_w, y_in, z_in, pair_in, other_in, _, seg_ref, z_out
):
    here = Place(side, size, part_ref.shape[-1])
    bins = range(BINS)
    y_adds, _ = y_halo(here, y_in, y_w)
    hi = 0 if side == 2 else 2 * BINS
    z_adds = []
    for b in bins:
        low = z_in[2 * b] * z_w[b, 0] + z_in[2 * b + 1] * z_w[b, 1]
        nxt = jnp.where(here.col == side - 1, 0.0, z_in[hi + b])
        z_adds.append((low, nxt * z_w[b, 2], nxt * z_w[b, 3]))
    flow = z_in[hi + BINS]
    from_left, from_right = here.read_tunnel(pair_in, other_in)
    for b, y, tile in add_halo(
        here, part_ref, x_w, y_adds, z_adds, from_left, from_right, 1.0
    ):
        seg_ref[b, here.at(y), :] = tile

    def corner_rows(z):
        at = [*range(2 * BINS)] if side == 2 else [*range(2 * BINS), *range(2 * BINS + 2, 3 * BINS + 2)]
        rows = jnp.zeros(here.shape, F32)
        for n, i in enumerate(at):
            rows = jnp.where(here.z_at == n, jnp.broadcast_to(y_in[i, z : z + 1, :], here.shape), rows)
        return rows

    up, down = [], []
    for b in bins:
        far, near, own = (here.rows(seg_ref, b, z) for z in (size - 2, size - 1, 0))
        weights = low_weights(flow, DIFFUSIVITY[b])
        up.append(far * weights[0] + near * weights[1])
        down.append(own)
    strip = jnp.where(here.strip_x < 2, from_right, from_left)
    up, down = (in_tiles(here, planes) + [strip] for planes in (up, down))
    up += in_tiles(here, [corner_rows(size - 2), corner_rows(size - 1)])
    down += in_tiles(here, [corner_rows(0)])
    here.write_across(z_out, up, down, here.col == 0)


def stencil(even, c, m1, p1, m2, p2):
    g = jnp.where(even, p1 - m1 - 0.25 * (p2 - m2), 0.5 * (p1 - m1))
    k = jnp.where(even, 3.5 * c - 2.0 * (p1 + m1) + 0.25 * (p2 + m2), 2.0 * c - (p1 + m1))
    return g, k


def advance_strip(here, dust_ref, from_left, from_right, strip_w):
    size, half = here.size, LANES // 2
    bins = range(BINS)
    own_first = here.columns(dust_ref, bins, False, (0, 4))
    own_last = here.columns(dust_ref, bins, True, (0, 4))
    x, y = here.strip_x, here.strip_y
    z = lax.broadcasted_iota(jnp.int32, here.lane.shape, 0)
    used = (here.lane < 4 * size * BINS) & (x != 1)
    right, before = x == 0, x == 2
    c = jnp.where(right, from_right, from_left)
    c = jnp.where(used, c, 0.0)
    gx, kx = stencil(
        x != 3,
        c,
        jnp.where(right, roll(own_last, -3), roll(from_left, 1)),
        jnp.where(right, roll(from_right, -1), jnp.where(before, roll(from_left, -1), roll(own_first, 3))),
        jnp.where(right, roll(own_last, -2), roll(from_left, 2)),
        jnp.where(right, roll(from_right, -2), roll(own_first, 2)),
    )
    gy, ky = stencil(
        y % 2 == 0,
        c,
        jnp.where(y == 0, 0.0, roll(c, 4)),
        jnp.where(y == size - 1, 0.0, roll(c, -4)),
        jnp.where(y == 0, 0.0, roll(c, 8)),
        jnp.where(y == size - 2, 0.0, roll(c, -8)),
    )
    gz, kz = stencil(
        z % 2 == 0,
        c,
        jnp.where(z == 0, 0.0, pltpu.roll(c, 1, 0)),
        jnp.where(z == size - 1, 0.0, pltpu.roll(c, size - 1, 0)),
        jnp.where(z == 0, 0.0, pltpu.roll(c, 2, 0)),
        jnp.where(z == size - 2, 0.0, pltpu.roll(c, size - 2, 0)),
    )

    def flow(left_by, right_by):
        both = jnp.where(right, roll(from_right, right_by), roll(from_left, left_by))
        return here.for_bins(jnp.where(here.lane < 4 * size, both, 0.0))

    u0 = flow(-half, -half) - here.by_bin(SETTLING)
    u1 = flow(2 - half, -half - 1)
    u2 = flow(-half - 4 * size, -half - 2)
    kappa = here.by_bin(DIFFUSIVITY)
    rate = u0 * gy + u1 * gz + u2 * gx + kappa * (kx + ky + kz)
    done = jnp.where(used, here.off_strip_wall(c - TIME_STEP * rate), 0.0)
    n = 0
    for at, flow, place in ((y, u0, here.row), (z, u1, here.col)):
        far, near = low_weights(flow, kappa)
        low, inside = (at == 0) & (place > 0), place < here.side - 1
        for mask, weight in (
            (low, far),
            (low, near),
            ((at == size - 2) & inside, (0.25 * TIME_STEP) * (flow - kappa)),
            ((at == size - 1) & inside, (-TIME_STEP) * (0.5 * flow - kappa)),
        ):
            strip_w[n] = jnp.where(used & mask, here.off_strip_wall(weight), 0.0)
            n += 1
    return done


def second_inner_kernel(
    side, size, dust_ref, vel_ref, seg_ref, y_w, y_in, pair_in, other_in, part_ref, strip_ref, strip_w, corner_w
):
    here = Place(side, size, dust_ref.shape[-1])
    for b, y, f, rate in inner_rates(here, seg_ref, vel_ref):
        result = 0.5 * dust_ref[b, here.at(y), :] + 0.5 * (f + TIME_STEP * rate)
        part_ref[b, here.at(y), :] = here.off_wall(y, result)
    from_left, from_right = here.read_tunnel(pair_in, other_in)
    strip_ref[...] = advance_strip(here, dust_ref, from_left, from_right, strip_w)
    hi = BINS + 1 if side == 2 else 3 * BINS + 3
    has_low, has_high = here.row > 0, here.row < side - 1
    for b in range(BINS):
        kappa = DIFFUSIVITY[b]
        n = 0
        for z in (0, size - 2, size - 1):

            def row(plane, z=z):
                return jnp.broadcast_to(plane[z : z + 1, :], here.shape)

            for k in range(2):
                low, above = row(y_in[2 * BINS + k]), row(y_in[hi])
                flow = jnp.where(here.z_at == 0, low, above)
                take = jnp.where((here.z_at == 0) & has_low, row(y_w[b, k]), 0.0)
                if k == 0:
                    take += jnp.where((here.z_at == size - 2) & has_high, row(y_w[b, 2]), 0.0)
                    take += jnp.where((here.z_at == size - 1) & has_high, row(y_w[b, 3]), 0.0)
                if z == 0:
                    ways = [jnp.where(here.col > 0, w, 0.0) for w in low_weights(flow, kappa)]
                else:
                    way = 0.25 * (flow - kappa) if z == size - 2 else kappa - 0.5 * flow
                    ways = [jnp.where(here.col < side - 1, TIME_STEP * way, 0.0)]
                for way in ways:
                    corner_w[b, n] = take * way
                    n += 1


def second_outer_kernel(
    side, size, names, part_ref, y_w, z_w, x_w, strip_ref, strip_w, corner_w, *refs
):
    halos = len(names)
    got = dict(zip(names, refs[:halos]))
    out_hbm, result, sems = refs[halos:]
    here = Place(side, size, part_ref.shape[-1])
    count = here.length // LANES
    y_in, z_in = here.across(got, range(got["z"].shape[0]))
    adds = []
    y_hi, z_hi = (0, 0) if side == 2 else (BINS * count + 1, (BINS + 2) * count + 1)
    for ref, weights, at, hi in ((y_in, y_w, here.row, y_hi), (z_in, z_w, here.col, z_hi)):
        add = []
        for b in range(BINS):
            low, nxt = (
                jnp.concatenate([ref[first + b * count + t] for t in range(count)], 1)
                for first in (0, hi)
            )
            nxt = jnp.where(at == side - 1, 0.0, nxt)
            add.append((low, nxt * weights[b, 2], nxt * weights[b, 3]))
        adds.append(add)

    def corner(first, n):
        return jnp.concatenate(
            [jnp.broadcast_to(z_in[first + t][n : n + 1, :], (size, LANES)) for t in range(count)], 1
        )

    start = BINS * count + 1
    sources = (start, start + count, z_hi + start)
    for b in range(BINS):
        extra, n = [], 0
        for z in (0, size - 2, size - 1):
            total = 0.0
            for k in range(2):
                high_row = b if side == 2 else 2 * BINS + b
                for source in sources[:2] if z == 0 else sources[2:]:
                    rows = jnp.where(here.z_at == 0, corner(source, 2 * b + k), corner(source, high_row))
                    total += rows * corner_w[b, n]
                    n += 1
            extra.append(total)
        adds[1][b] = tuple(p + q for p, q in zip(adds[1][b], extra))
    low, high = y_in[BINS * count], y_in[y_hi + BINS * count]
    far, near = 4 * (size - 2), 4 * (size - 1)
    strip = strip_ref[...] + roll(low, -far) * strip_w[0] + roll(low, -near) * strip_w[1]
    strip += roll(high, far) * strip_w[2] + roll(high, near) * strip_w[3]
    low, high = z_in[BINS * count], z_in[z_hi + BINS * count]
    strip += pltpu.roll(low, 2, 0) * strip_w[4] + pltpu.roll(low, 1, 0) * strip_w[5]
    strip += pltpu.roll(high, size - 2, 0) * strip_w[6] + pltpu.roll(high, size - 1, 0) * strip_w[7]
    stores = [
        pltpu.make_async_copy(result.at[b], out_hbm.at[b], sems.at[b]) for b in range(BINS)
    ]
    for b, y, tile in add_halo(here, part_ref, x_w, adds[0], adds[1], strip, strip, 0.5):
        result[b, here.at(y), :] = tile
        if y == size - 1:
            stores[b].start()
    for store in stores:
        store.wait()


def shift(block, axis, moves):
    return lax.ppermute(block, axis, [(s, moves(s)) for s in range(lax.axis_size(axis))])


def body(concentration, velocity):
    side = math.isqrt(lax.axis_size("sec"))
    tunnel = lax.axis_size("tun")
    size, length = concentration.shape[-2:]
    conc = concentration.reshape(BINS, size * size, length)
    vel = velocity.reshape(3, size * size, length)
    vmem = pl.BlockSpec(memory_space=pltpu.VMEM)
    hbm = pl.BlockSpec(memory_space=pltpu.HBM)

    def planes(up, down):
        return max(up, down) if side == 2 else up + down

    def call(kernel, outs, *args):
        args = [pltpu.with_memory_space_constraint(arg, pltpu.VMEM) for arg in args]
        return pl.pallas_call(
            lambda *refs: kernel(side, size, *refs),
            out_shape=outs,
            in_specs=[vmem] * len(args),
            out_specs=[vmem] * len(outs),
            name=kernel.__name__,
        )(*args)

    def along_pair(s):
        return s + 1 - 2 * (s % 2)

    def along_other(s):
        return (s - 1 + 2 * (s % 2)) % tunnel

    def along_y(d):
        return lambda s: (s // side + d) % side * side + s % side

    def along_z(d):
        return lambda s: s // side * side + (s % side + d) % side

    def across(out, up, move):
        if side == 2:
            return shift(out, "sec", move(1))
        return jnp.concatenate(
            [shift(out[:up], "sec", move(1)), shift(out[up:], "sec", move(-1))], 0
        )

    moves = {
        "y": lambda out, up: across(out, up, along_y),
        "z": lambda out, up: across(out, up, along_z),
        "pair": lambda out, up: shift(out, "tun", along_pair),
        "other": lambda out, up: shift(out, "tun", along_other),
    }
    across_shape = (planes(2 * BINS, BINS + 1), size, length)
    y_shape = (planes(2 * BINS + 2, BINS + 2), size, length)
    shapes = {"y": y_shape, "pair": (size, LANES), "other": (10, size, LANES)}
    first = [pltpu.VMEM(shapes.get(name, across_shape), F32) for name in FIRST]
    tiles = BINS * (length // LANES) + 1
    z_up, z_down = tiles + 2 * (length // LANES), tiles + length // LANES
    y_message = pltpu.VMEM((z_up + 1 if side == 2 else 2 * tiles, size, LANES), F32)
    z_message = pltpu.VMEM((planes(z_up, z_down), size, LANES), F32)
    dust, vel, *sends = pl.pallas_call(
        lambda *refs: pack_kernel(side, size, FIRST, *refs),
        out_shape=[pltpu.VMEM(conc.shape, F32), pltpu.VMEM(vel.shape, F32)] + first,
        in_specs=[hbm] * 2,
        out_specs=[vmem] * (2 + len(first)),
        scratch_shapes=[pltpu.SemaphoreType.DMA((2,))],
        name="pack_kernel",
    )(conc, vel)
    y_up_planes = 2 * BINS + 2
    halo = [moves[name](out, y_up_planes if name == "y" else 2 * BINS) for name, out in zip(FIRST, sends)]
    field, strip = pltpu.VMEM(conc.shape, F32), (size, LANES)
    weights = [pltpu.VMEM((BINS, 4, size, length), F32)] * 2 + [pltpu.VMEM((2,) + strip, F32)]
    part, *weights = call(first_inner_kernel, [field] + weights, dust, vel)
    got = dict(zip(FIRST, halo))
    y_w, z_w, x_w = weights
    tunnel_in = got["pair"], got["other"]
    (y_send,) = call(first_y_kernel, [y_message], part, y_w, x_w, got["y"], *tunnel_in)
    segment, z_send = call(
        first_outer_kernel, [field, z_message], part, *weights, got["y"], got["z"], *tunnel_in, y_send
    )
    strips = [pltpu.VMEM(strip, F32), pltpu.VMEM((8,) + strip, F32)]
    strips.append(pltpu.VMEM((BINS, 8, size, length), F32))
    part, *strips = call(
        second_inner_kernel, [field] + strips, dust, vel, segment, y_w, got["y"], *tunnel_in
    )
    halo = [moves["y"](y_send, tiles), moves["z"](z_send, z_up)]
    args = (part, *weights, *strips, *halo)
    args = [pltpu.with_memory_space_constraint(arg, pltpu.VMEM) for arg in args]
    result = pl.pallas_call(
        lambda *refs: second_outer_kernel(side, size, SECOND, *refs),
        out_shape=jax.ShapeDtypeStruct(conc.shape, F32),
        in_specs=[vmem] * len(args),
        out_specs=hbm,
        scratch_shapes=[pltpu.VMEM(conc.shape, F32), pltpu.SemaphoreType.DMA((BINS,))],
        name="second_outer_kernel",
    )(*args)
    return result.reshape(concentration.shape)


def solution(mesh):
    spec = P(None, "sec", None, None, "tun")
    return jax.shard_map(
        body, mesh=mesh, in_specs=(spec, spec), out_specs=spec, check_vma=False
    )
```

```python
import math

import jax
import jax.numpy as jnp
from jax import lax
from jax.experimental import pallas as pl
from jax.experimental.pallas import tpu as pltpu
from jax.sharding import PartitionSpec as P

TIME_STEP = 0.1
DIFFUSIVITY = (0.4, 0.15)
SETTLING = (0.05, 0.6)
BINS = 2
LANES = 128
FIRST = ("y", "other", "z", "pair")
SECOND = ("y", "z")
F32 = jnp.float32


def roll(tile, by):
    by %= LANES
    return pltpu.roll(tile, by, 1) if by else tile


class Place:
    def __init__(self, side, size, length):
        self.side, self.size, self.length = side, size, length
        place = lax.axis_index("sec")
        self.row, self.col = place // side, lax.rem(place, side)
        self.pair_right = lax.rem(lax.axis_index("tun"), 2) == 0
        self.shape = (size, length)
        self.z_at = lax.broadcasted_iota(jnp.int32, self.shape, 0)
        self.lane = lax.broadcasted_iota(jnp.int32, (size, LANES), 1)
        self.strip_x, self.strip_y = self.lane % 4, self.lane // 4 % size

    def off_wall(self, y, tile):
        wall = (self.z_at == 0) & (self.col == 0)
        if y == 0:
            wall = wall | (self.row == 0)
        return jnp.where(wall, 0.0, tile)

    def at(self, y):
        return slice(y * self.size, (y + 1) * self.size)

    def rows(self, ref, lead, z):
        rows = jnp.broadcast_to(ref[lead, z : z + 1, :], self.shape)
        for y in range(1, self.size):
            row = ref[lead, y * self.size + z : y * self.size + z + 1, :]
            rows = jnp.where(self.z_at == y, jnp.broadcast_to(row, self.shape), rows)
        return rows

    def stack(self, rows):
        planes = []
        for n in range(0, len(rows), self.size):
            plane = jnp.zeros(self.shape, F32)
            for i, row in enumerate(rows[n : n + self.size]):
                plane = jnp.where(self.z_at == i, jnp.broadcast_to(row[...], self.shape), plane)
            planes.append(plane)
        return planes

    def columns(self, ref, leads, last, keep):
        packed = jnp.zeros((self.size, LANES), F32)
        for n, lead in enumerate(leads):
            for y in range(self.size):
                to = 4 * (n * self.size + y)
                if last:
                    tile = pltpu.roll(ref[lead, self.at(y), self.length - LANES :], (to + 4) % LANES, 1)
                else:
                    tile = ref[lead, self.at(y), :LANES]
                    tile = pltpu.roll(tile, to, 1) if to else tile
                packed = jnp.where((self.lane >= to + keep[0]) & (self.lane < to + keep[1]), tile, packed)
        return packed

    def for_bins(self, packed):
        return sum((roll(packed, b * 4 * self.size) for b in range(1, BINS)), packed)

    def by_bin(self, values):
        out = values[-1]
        for b in reversed(range(BINS - 1)):
            out = jnp.where(self.lane < 4 * self.size * (b + 1), values[b], out)
        return out

    def off_strip_wall(self, strip):
        z_at = lax.broadcasted_iota(jnp.int32, strip.shape, 0)
        wall = (z_at == 0) & (self.col == 0) | (self.strip_y == 0) & (self.row == 0)
        return jnp.where(wall, 0.0, strip)

    def only_neighbour(self, up, down, forward):
        count = max(len(up), len(down))
        up, down = up + down[len(up) :], down + up[len(down) :]
        return [jnp.where(forward, up[i], down[i]) for i in range(count)]

    def write_across(self, out, up, down, forward):
        planes = self.only_neighbour(up, down, forward) if self.side == 2 else up + down
        for i, plane in enumerate(planes):
            out[i] = plane
        for i in range(len(planes), out.shape[0]):
            out[i] = jnp.zeros(out.shape[1:], F32)

    def across(self, got, planes):
        z_in = [got["z"][i] for i in planes]
        return [got["y"][i] for i in planes], z_in

    def write_tunnel(self, pair, other, right, left):
        pair[...] = jnp.where(self.pair_right, right, left)
        other[0] = jnp.where(self.pair_right, left, right)
        for i in range(1, other.shape[0]):
            other[i] = jnp.zeros(pair.shape, F32)

    def read_tunnel(self, pair, other):
        pair, other = pair[...], other[0]
        return jnp.where(self.pair_right, other, pair), jnp.where(self.pair_right, pair, other)


def low_weights(flow, kappa):
    return (-0.25 * TIME_STEP) * (flow + kappa), TIME_STEP * (flow + 2.0 * kappa)


def pack_kernel(side, size, names, conc_hbm, vel_hbm, dust_ref, vel_ref, *refs):
    *sends, sems = refs
    load = pltpu.make_async_copy(conc_hbm, dust_ref, sems.at[0])
    load_vel = pltpu.make_async_copy(vel_hbm, vel_ref, sems.at[1])
    load.start()
    load_vel.start()
    here = Place(side, size, dust_ref.shape[-1])
    load.wait()
    for b in range(BINS):
        for y in range(size):
            dust_ref[b, here.at(y), :] = here.off_wall(y, dust_ref[b, here.at(y), :])
    send = dict(zip(names, sends))
    bins = range(BINS)
    ends = (size - 2, size - 1)
    y_up = [dust_ref[b, here.at(y), :] for b in bins for y in ends]
    y_down = [dust_ref[b, here.at(0), :] for b in bins]
    z_up = [here.rows(dust_ref, b, z) for b in bins for z in ends]
    z_down = [here.rows(dust_ref, b, 0) for b in bins]
    right = here.columns(dust_ref, bins, True, (0, 4))
    left = here.columns(dust_ref, bins, False, (0, 4))
    load_vel.wait()
    sides = (0, size - 2, size - 1)
    y_up += here.stack([vel_ref.at[1, pl.ds(y * size + z, 1), :] for y in ends for z in sides])
    y_down.append(vel_ref[0, here.at(0), :])
    y_down += here.stack([vel_ref.at[1, pl.ds(z, 1), :] for z in sides])
    z_down.append(here.rows(vel_ref, 1, 0))
    here.write_across(send["y"], y_up, y_down, here.row == 0)
    here.write_across(send["z"], z_up, z_down, here.col == 0)
    half = LANES // 2
    u0, u1, u2 = (here.columns(vel_ref, [i], True, (2, 4)) for i in range(3))
    right += roll(u0, half) + roll(u1, half - 2) + roll(u2, half + 4 * size)
    u0, u1, u2 = (here.columns(vel_ref, [i], False, (0, 1)) for i in range(3))
    left += roll(u0, half) + roll(u1, half + 1) + roll(u2, half + 2)
    here.write_tunnel(send["pair"], send["other"], right, left)


def slope_and_bend(m1, p1, m2, p2):
    return (p1 - m1) - (p2 - m2), (p2 + m2) - 2.0 * (p1 + m1)


def inner_rates(here, field, vel_ref):
    size, length, shape = here.size, here.length, here.shape
    x_at = lax.broadcasted_iota(jnp.int32, shape, 1)
    weights = []
    for index, count in ((here.z_at, size), (x_at, length)):
        even = index % 2 == 0
        near, far = jnp.where(even, 0.5, 1.0), jnp.where(even, 0.25, 0.0)
        weights.append(
            (
                jnp.where(index == count - 1, 0.0, near),
                jnp.where(index == 0, 0.0, near),
                jnp.where(index == count - 2, 0.0, far),
                jnp.where(index == 0, 0.0, far),
            )
        )
    centre = jnp.where(here.z_at % 2 == 0, 3.5, 2.0) + jnp.where(x_at % 2 == 0, 3.5, 2.0)

    def along(f, axis, count):
        m1, p1, m2, p2 = weights[axis]
        return slope_and_bend(
            pltpu.roll(f * m1, 1, axis),
            pltpu.roll(f * p1, count - 1, axis),
            pltpu.roll(f * m2, 2, axis),
            pltpu.roll(f * p2, count - 2, axis),
        )

    zero = jnp.zeros(shape, F32)
    for b in range(BINS):
        kappa, settle = DIFFUSIVITY[b], SETTLING[b]

        def tile(y, b=b):
            return field[b, here.at(y), :] if 0 <= y < size else zero

        for y in range(size):
            f = tile(y)
            if y % 2 == 0:
                gy, ky = slope_and_bend(
                    tile(y - 1), tile(y + 1), 0.25 * tile(y - 2), 0.25 * tile(y + 2)
                )
                own = centre + 3.5
            else:
                gy, ky = 0.5 * (tile(y + 1) - tile(y - 1)), -(tile(y + 1) + tile(y - 1))
                own = centre + 2.0
            gz, kz = along(f, 0, size)
            gx, kx = along(f, 1, length)
            u0, u1, u2 = (vel_ref[i, here.at(y), :] for i in range(3))
            moved = (u0 - settle) * gy + u1 * gz + u2 * gx
            yield b, y, f, -(moved + kappa * (own * f + (ky + kz + kx)))


def first_inner_kernel(side, size, dust_ref, vel_ref, part_ref, y_w, z_w, x_w):
    here = Place(side, size, dust_ref.shape[-1])
    for b, y, f, rate in inner_rates(here, dust_ref, vel_ref):
        part_ref[b, here.at(y), :] = here.off_wall(y, f + TIME_STEP * rate)
    ends = (0, size - 2, size - 1)
    y_flow = [vel_ref[0, here.at(y), :] for y in ends]
    z_flow = [here.rows(vel_ref, 1, z) for z in ends]
    for b in range(BINS):
        kappa = DIFFUSIVITY[b]
        for out, flow in ((y_w, [u - SETTLING[b] for u in y_flow]), (z_w, z_flow)):
            out[b, 0], out[b, 1] = low_weights(flow[0], kappa)
            out[b, 2] = (0.25 * TIME_STEP) * (flow[1] - kappa)
            out[b, 3] = (-TIME_STEP) * (0.5 * flow[2] - kappa)
    kappa = here.by_bin(DIFFUSIVITY)
    even = here.lane % 2 == 0
    flow = here.for_bins(here.columns(vel_ref, [2], False, (0, 1)))
    far, _ = low_weights(roll(flow, 2), kappa)
    _, near = low_weights(roll(flow, 3), kappa)
    inside = here.strip_x >= 2
    x_w[0] = jnp.where(inside, jnp.where(even, far, near), 0.0)
    flow = here.for_bins(here.columns(vel_ref, [2], True, (2, 4)))
    far, near = (0.25 * TIME_STEP) * (flow - kappa), (-TIME_STEP) * (0.5 * flow - kappa)
    x_w[1] = jnp.where(inside, jnp.where(even, far, near), 0.0)


def add_halo(here, part_ref, x_w, y_add, z_add, low_strip, high_strip, share, rows=None):
    size, length = here.size, here.length
    x_low = low_strip * (share * x_w[0])
    x_low = x_low + roll(x_low, -1)
    high = jnp.where(here.strip_x == 2, roll(high_strip, 2), roll(high_strip, 3))
    x_high = high * (share * x_w[1])
    first, last = here.lane == 0, here.lane >= LANES - 2
    for b in range(BINS):
        y_low, y_before, y_last = y_add[b]
        for y in rows or range(size):
            tile = part_ref[b, here.at(y), :]

            if z_add is not None:
                z_low, z_before, z_last = (
                    jnp.broadcast_to(plane[y : y + 1, :], here.shape) for plane in z_add[b]
                )
                add = jnp.where(
                    here.z_at == 0, z_low, jnp.where(here.z_at == size - 1, z_last, z_before)
                )
                tile += share * jnp.where((here.z_at == 0) | (here.z_at >= size - 2), add, 0.0)
            for at, plane in ((0, y_low), (size - 2, y_before), (size - 1, y_last)):
                if y == at:
                    tile += share * plane
            to = 4 * (b * size + y) + 2
            low = jnp.where(first, roll(x_low, -to), 0.0)
            high = jnp.where(last, roll(x_high, -2 - to), 0.0)
            inner = [jnp.zeros((size, length - 2 * LANES), F32)] if length > 2 * LANES else []
            tile += jnp.concatenate([low] + inner + [high], 1)
            yield b, y, here.off_wall(y, tile)


def y_halo(here, ref, weights):
    hi = 0 if here.side == 2 else 2 * BINS + 1
    adds = []
    for b in range(BINS):
        low = ref[2 * b] * weights[b, 0] + ref[2 * b + 1] * weights[b, 1]
        nxt = jnp.where(here.row == here.side - 1, 0.0, ref[hi + b])
        adds.append((low, nxt * weights[b, 2], nxt * weights[b, 3]))
    return adds, ref[hi + BINS]


def corner_planes(side):
    below = [*range(2 * BINS)]
    return below if side == 2 else below + [2 * BINS + 1 + b for b in range(BINS)]


def in_tiles(here, planes):
    return [p[:, at : at + LANES] for p in planes for at in range(0, here.length, LANES)]


def first_y_kernel(side, size, part_ref, y_w, x_w, y_in, pair_in, other_in, y_out):
    here = Place(side, size, part_ref.shape[-1])
    adds, flow = y_halo(here, y_in, y_w)
    from_left, from_right = here.read_tunnel(pair_in, other_in)
    ends = (0, size - 2, size - 1)
    tiles = {
        (b, y): tile
        for b, y, tile in add_halo(
            here, part_ref, x_w, adds, None, from_left, from_right, 1.0, ends
        )
    }
    up, down = [], []
    for b in range(BINS):
        far, near = low_weights(flow - SETTLING[b], DIFFUSIVITY[b])
        up.append(tiles[b, size - 2] * far + tiles[b, size - 1] * near)
        down.append(tiles[b, 0])
    strip = jnp.where(here.strip_x < 2, from_right, from_left)
    up, down = (in_tiles(here, planes) + [strip] for planes in (up, down))
    here.write_across(y_out, up, down, here.row == 0)


def first_outer_kernel(
    side, size, part_ref, y_w, z_w, x_w, y_in, z_in, pair_in, other_in, _, seg_ref, z_out
):
    here = Place(side, size, part_ref.shape[-1])
    bins = range(BINS)
    y_adds, _ = y_halo(here, y_in, y_w)
    hi = 0 if side == 2 else 2 * BINS
    z_adds = []
    for b in bins:
        low = z_in[2 * b] * z_w[b, 0] + z_in[2 * b + 1] * z_w[b, 1]
        nxt = jnp.where(here.col == side - 1, 0.0, z_in[hi + b])
        z_adds.append((low, nxt * z_w[b, 2], nxt * z_w[b, 3]))
    flow = z_in[hi + BINS]
    from_left, from_right = here.read_tunnel(pair_in, other_in)
    for b, y, tile in add_halo(
        here, part_ref, x_w, y_adds, z_adds, from_left, from_right, 1.0
    ):
        seg_ref[b, here.at(y), :] = tile

    up, down = [], []
    for b in bins:
        far, near, own = (here.rows(seg_ref, b, z) for z in (size - 2, size - 1, 0))
        weights = low_weights(flow, DIFFUSIVITY[b])
        up.append(far * weights[0] + near * weights[1])
        down.append(own)
    strip = jnp.where(here.strip_x < 2, from_right, from_left)
    up, down = (in_tiles(here, planes) + [strip] for planes in (up, down))
    at = corner_planes(side)
    up += in_tiles(here, here.stack([y_in.at[i, z : z + 1, :] for z in (size - 2, size - 1) for i in at]))
    down += in_tiles(here, here.stack([y_in.at[i, 0:1, :] for i in at]))
    here.write_across(z_out, up, down, here.col == 0)


def stencil(even, c, m1, p1, m2, p2):
    g = jnp.where(even, p1 - m1 - 0.25 * (p2 - m2), 0.5 * (p1 - m1))
    k = jnp.where(even, 3.5 * c - 2.0 * (p1 + m1) + 0.25 * (p2 + m2), 2.0 * c - (p1 + m1))
    return g, k


def advance_strip(here, dust_ref, from_left, from_right, strip_w):
    size, half = here.size, LANES // 2
    bins = range(BINS)
    own_first = here.columns(dust_ref, bins, False, (0, 4))
    own_last = here.columns(dust_ref, bins, True, (0, 4))
    x, y = here.strip_x, here.strip_y
    z = lax.broadcasted_iota(jnp.int32, here.lane.shape, 0)
    used = (here.lane < 4 * size * BINS) & (x != 1)
    right, before = x == 0, x == 2
    c = jnp.where(right, from_right, from_left)
    c = jnp.where(used, c, 0.0)
    gx, kx = stencil(
        x != 3,
        c,
        jnp.where(right, roll(own_last, -3), roll(from_left, 1)),
        jnp.where(right, roll(from_right, -1), jnp.where(before, roll(from_left, -1), roll(own_first, 3))),
        jnp.where(right, roll(own_last, -2), roll(from_left, 2)),
        jnp.where(right, roll(from_right, -2), roll(own_first, 2)),
    )
    gy, ky = stencil(
        y % 2 == 0,
        c,
        jnp.where(y == 0, 0.0, roll(c, 4)),
        jnp.where(y == size - 1, 0.0, roll(c, -4)),
        jnp.where(y == 0, 0.0, roll(c, 8)),
        jnp.where(y == size - 2, 0.0, roll(c, -8)),
    )
    gz, kz = stencil(
        z % 2 == 0,
        c,
        jnp.where(z == 0, 0.0, pltpu.roll(c, 1, 0)),
        jnp.where(z == size - 1, 0.0, pltpu.roll(c, size - 1, 0)),
        jnp.where(z == 0, 0.0, pltpu.roll(c, 2, 0)),
        jnp.where(z == size - 2, 0.0, pltpu.roll(c, size - 2, 0)),
    )

    def flow(left_by, right_by):
        both = jnp.where(right, roll(from_right, right_by), roll(from_left, left_by))
        return here.for_bins(jnp.where(here.lane < 4 * size, both, 0.0))

    u0 = flow(-half, -half) - here.by_bin(SETTLING)
    u1 = flow(2 - half, -half - 1)
    u2 = flow(-half - 4 * size, -half - 2)
    kappa = here.by_bin(DIFFUSIVITY)
    rate = u0 * gy + u1 * gz + u2 * gx + kappa * (kx + ky + kz)
    done = jnp.where(used, here.off_strip_wall(c - TIME_STEP * rate), 0.0)
    n = 0
    for at, flow, place in ((y, u0, here.row), (z, u1, here.col)):
        far, near = low_weights(flow, kappa)
        low, inside = (at == 0) & (place > 0), place < here.side - 1
        for mask, weight in (
            (low, far),
            (low, near),
            ((at == size - 2) & inside, (0.25 * TIME_STEP) * (flow - kappa)),
            ((at == size - 1) & inside, (-TIME_STEP) * (0.5 * flow - kappa)),
        ):
            strip_w[n] = jnp.where(used & mask, here.off_strip_wall(weight), 0.0)
            n += 1
    return done


def second_inner_kernel(
    side, size, dust_ref, vel_ref, seg_ref, y_w, y_in, pair_in, other_in, part_ref, strip_ref, strip_w, corner_w
):
    here = Place(side, size, dust_ref.shape[-1])
    for b, y, f, rate in inner_rates(here, seg_ref, vel_ref):
        result = 0.5 * dust_ref[b, here.at(y), :] + 0.5 * (f + TIME_STEP * rate)
        part_ref[b, here.at(y), :] = here.off_wall(y, result)
    from_left, from_right = here.read_tunnel(pair_in, other_in)
    strip_ref[...] = advance_strip(here, dust_ref, from_left, from_right, strip_w)
    hi = BINS + 1 if side == 2 else 3 * BINS + 2
    has_low, has_high = here.row > 0, here.row < side - 1
    for b in range(BINS):
        kappa = DIFFUSIVITY[b]
        n = 0
        for at, z in enumerate((0, size - 2, size - 1)):

            def row(plane, z=z):
                return jnp.broadcast_to(plane[z : z + 1, :], here.shape)

            for k in range(2):
                low, above = row(y_in[2 * BINS], 3 * k + at), row(y_in[hi], at)
                flow = jnp.where(here.z_at == 0, low, above)
                take = jnp.where((here.z_at == 0) & has_low, row(y_w[b, k]), 0.0)
                if k == 0:
                    take += jnp.where((here.z_at == size - 2) & has_high, row(y_w[b, 2]), 0.0)
                    take += jnp.where((here.z_at == size - 1) & has_high, row(y_w[b, 3]), 0.0)
                if z == 0:
                    ways = [jnp.where(here.col > 0, w, 0.0) for w in low_weights(flow, kappa)]
                else:
                    way = 0.25 * (flow - kappa) if z == size - 2 else kappa - 0.5 * flow
                    ways = [jnp.where(here.col < side - 1, TIME_STEP * way, 0.0)]
                for way in ways:
                    corner_w[b, n] = take * way
                    n += 1


def second_outer_kernel(
    side, size, names, part_ref, y_w, z_w, x_w, strip_ref, strip_w, corner_w, *refs
):
    halos = len(names)
    got = dict(zip(names, refs[:halos]))
    out_hbm, result, sems = refs[halos:]
    here = Place(side, size, part_ref.shape[-1])
    count = here.length // LANES
    y_in, z_in = here.across(got, range(got["z"].shape[0]))
    adds = []
    y_hi, z_hi = (0, 0) if side == 2 else (BINS * count + 1, BINS * count + 1 + -(-2 * len(corner_planes(side)) // size) * count)
    for ref, weights, at, hi in ((y_in, y_w, here.row, y_hi), (z_in, z_w, here.col, z_hi)):
        add = []
        for b in range(BINS):
            low, nxt = (
                jnp.concatenate([ref[first + b * count + t] for t in range(count)], 1)
                for first in (0, hi)
            )
            nxt = jnp.where(at == side - 1, 0.0, nxt)
            add.append((low, nxt * weights[b, 2], nxt * weights[b, 3]))
        adds.append(add)

    def corner(first, n):
        first, n = first + n // size * count, n % size
        return jnp.concatenate(
            [jnp.broadcast_to(z_in[first + t][n : n + 1, :], (size, LANES)) for t in range(count)], 1
        )

    start, rows = BINS * count + 1, len(corner_planes(side))
    sources = ((start, 0), (start, rows), (z_hi + start, 0))
    for b in range(BINS):
        extra, n = [], 0
        for z in (0, size - 2, size - 1):
            total = 0.0
            for k in range(2):
                high_row = b if side == 2 else 2 * BINS + b
                for source in sources[:2] if z == 0 else sources[2:]:
                    first, skip = source
                    plane = jnp.where(
                        here.z_at == 0,
                        corner(first, skip + 2 * b + k),
                        corner(first, skip + high_row),
                    )
                    total += plane * corner_w[b, n]
                    n += 1
            extra.append(total)
        adds[1][b] = tuple(p + q for p, q in zip(adds[1][b], extra))
    low, high = y_in[BINS * count], y_in[y_hi + BINS * count]
    far, near = 4 * (size - 2), 4 * (size - 1)
    strip = strip_ref[...] + roll(low, -far) * strip_w[0] + roll(low, -near) * strip_w[1]
    strip += roll(high, far) * strip_w[2] + roll(high, near) * strip_w[3]
    low, high = z_in[BINS * count], z_in[z_hi + BINS * count]
    strip += pltpu.roll(low, 2, 0) * strip_w[4] + pltpu.roll(low, 1, 0) * strip_w[5]
    strip += pltpu.roll(high, size - 2, 0) * strip_w[6] + pltpu.roll(high, size - 1, 0) * strip_w[7]
    stores = [
        pltpu.make_async_copy(result.at[b], out_hbm.at[b], sems.at[b]) for b in range(BINS)
    ]
    for b, y, tile in add_halo(here, part_ref, x_w, adds[0], adds[1], strip, strip, 0.5):
        result[b, here.at(y), :] = tile
        if y == size - 1:
            stores[b].start()
    for store in stores:
        store.wait()


def shift(block, axis, moves):
    return lax.ppermute(block, axis, [(s, moves(s)) for s in range(lax.axis_size(axis))])


def body(concentration, velocity):
    side = math.isqrt(lax.axis_size("sec"))
    tunnel = lax.axis_size("tun")
    size, length = concentration.shape[-2:]
    conc = concentration.reshape(BINS, size * size, length)
    vel = velocity.reshape(3, size * size, length)
    vmem = pl.BlockSpec(memory_space=pltpu.VMEM)
    hbm = pl.BlockSpec(memory_space=pltpu.HBM)

    def planes(up, down):
        return max(up, down) if side == 2 else up + down

    def call(kernel, outs, *args):
        args = [pltpu.with_memory_space_constraint(arg, pltpu.VMEM) for arg in args]
        return pl.pallas_call(
            lambda *refs: kernel(side, size, *refs),
            out_shape=outs,
            in_specs=[vmem] * len(args),
            out_specs=[vmem] * len(outs),
            name=kernel.__name__,
        )(*args)

    def along_pair(s):
        return s + 1 - 2 * (s % 2)

    def along_other(s):
        return (s - 1 + 2 * (s % 2)) % tunnel

    def along_y(d):
        return lambda s: (s // side + d) % side * side + s % side

    def along_z(d):
        return lambda s: s // side * side + (s % side + d) % side

    def across(out, up, move):
        if side == 2:
            return shift(out, "sec", move(1))
        return jnp.concatenate(
            [shift(out[:up], "sec", move(1)), shift(out[up:], "sec", move(-1))], 0
        )

    moves = {
        "y": lambda out, up: across(out, up, along_y),
        "z": lambda out, up: across(out, up, along_z),
        "pair": lambda out, up: shift(out, "tun", along_pair),
        "other": lambda out, up: shift(out, "tun", along_other),
    }
    across_shape = (planes(2 * BINS, BINS + 1), size, length)
    y_shape = (planes(2 * BINS + 1, BINS + 2), size, length)
    shapes = {"y": y_shape, "pair": (size, LANES), "other": (9, size, LANES)}
    first = [pltpu.VMEM(shapes.get(name, across_shape), F32) for name in FIRST]
    tiles = BINS * (length // LANES) + 1
    corners = len(corner_planes(side))
    z_up, z_down = (tiles + -(-n // size) * (length // LANES) for n in (2 * corners, corners))
    y_message = pltpu.VMEM((z_up + 1 if side == 2 else 2 * tiles, size, LANES), F32)
    z_message = pltpu.VMEM((planes(z_up, z_down), size, LANES), F32)
    dust, vel, *sends = pl.pallas_call(
        lambda *refs: pack_kernel(side, size, FIRST, *refs),
        out_shape=[pltpu.VMEM(conc.shape, F32), pltpu.VMEM(vel.shape, F32)] + first,
        in_specs=[hbm] * 2,
        out_specs=[vmem] * (2 + len(first)),
        scratch_shapes=[pltpu.SemaphoreType.DMA((2,))],
        name="pack_kernel",
    )(conc, vel)
    y_up_planes = 2 * BINS + 1
    halo = [moves[name](out, y_up_planes if name == "y" else 2 * BINS) for name, out in zip(FIRST, sends)]
    field, strip = pltpu.VMEM(conc.shape, F32), (size, LANES)
    weights = [pltpu.VMEM((BINS, 4, size, length), F32)] * 2 + [pltpu.VMEM((2,) + strip, F32)]
    part, *weights = call(first_inner_kernel, [field] + weights, dust, vel)
    got = dict(zip(FIRST, halo))
    y_w, z_w, x_w = weights
    tunnel_in = got["pair"], got["other"]
    (y_send,) = call(first_y_kernel, [y_message], part, y_w, x_w, got["y"], *tunnel_in)
    segment, z_send = call(
        first_outer_kernel, [field, z_message], part, *weights, got["y"], got["z"], *tunnel_in, y_send
    )
    strips = [pltpu.VMEM(strip, F32), pltpu.VMEM((8,) + strip, F32)]
    strips.append(pltpu.VMEM((BINS, 8, size, length), F32))
    part, *strips = call(
        second_inner_kernel, [field] + strips, dust, vel, segment, y_w, got["y"], *tunnel_in
    )
    halo = [moves["y"](y_send, tiles), moves["z"](z_send, z_up)]
    args = (part, *weights, *strips, *halo)
    args = [pltpu.with_memory_space_constraint(arg, pltpu.VMEM) for arg in args]
    result = pl.pallas_call(
        lambda *refs: second_outer_kernel(side, size, SECOND, *refs),
        out_shape=jax.ShapeDtypeStruct(conc.shape, F32),
        in_specs=[vmem] * len(args),
        out_specs=hbm,
        scratch_shapes=[pltpu.VMEM(conc.shape, F32), pltpu.SemaphoreType.DMA((BINS,))],
        name="second_outer_kernel",
    )(*args)
    return result.reshape(concentration.shape)


def solution(mesh):
    spec = P(None, "sec", None, None, "tun")
    return jax.shard_map(
        body, mesh=mesh, in_specs=(spec, spec), out_specs=spec, check_vma=False
    )
```

```python
import math

import jax
import jax.numpy as jnp
from jax import lax
from jax.experimental import pallas as pl
from jax.experimental.pallas import tpu as pltpu
from jax.sharding import PartitionSpec as P

TIME_STEP = 0.1
DIFFUSIVITY = (0.4, 0.15)
SETTLING = (0.05, 0.6)
BINS = 2
LANES = 128
FIRST = ("y", "other", "z", "pair")
SECOND = ("y", "z")
F32 = jnp.float32


def roll(tile, by):
    by %= LANES
    return pltpu.roll(tile, by, 1) if by else tile


class Place:
    def __init__(self, side, size, length):
        self.side, self.size, self.length = side, size, length
        place = lax.axis_index("sec")
        self.row, self.col = place // side, lax.rem(place, side)
        self.pair_right = lax.rem(lax.axis_index("tun"), 2) == 0
        self.shape = (size, length)
        self.z_at = lax.broadcasted_iota(jnp.int32, self.shape, 0)
        self.lane = lax.broadcasted_iota(jnp.int32, (size, LANES), 1)
        self.strip_x, self.strip_y = self.lane % 4, self.lane // 4 % size

    def off_wall(self, y, tile):
        wall = (self.z_at == 0) & (self.col == 0)
        if y == 0:
            wall = wall | (self.row == 0)
        return jnp.where(wall, 0.0, tile)

    def at(self, y):
        return slice(y * self.size, (y + 1) * self.size)

    def rows(self, ref, lead, z):
        rows = jnp.broadcast_to(ref[lead, z : z + 1, :], self.shape)
        for y in range(1, self.size):
            row = ref[lead, y * self.size + z : y * self.size + z + 1, :]
            rows = jnp.where(self.z_at == y, jnp.broadcast_to(row, self.shape), rows)
        return rows

    def stack(self, rows):
        planes = []
        for n in range(0, len(rows), self.size):
            plane = jnp.zeros(self.shape, F32)
            for i, row in enumerate(rows[n : n + self.size]):
                plane = jnp.where(self.z_at == i, jnp.broadcast_to(row[...], self.shape), plane)
            planes.append(plane)
        return planes

    def columns(self, ref, leads, last, keep):
        packed = jnp.zeros((self.size, LANES), F32)
        for n, lead in enumerate(leads):
            for y in range(self.size):
                to = 4 * (n * self.size + y)
                if last:
                    tile = pltpu.roll(ref[lead, self.at(y), self.length - LANES :], (to + 4) % LANES, 1)
                else:
                    tile = ref[lead, self.at(y), :LANES]
                    tile = pltpu.roll(tile, to, 1) if to else tile
                packed = jnp.where((self.lane >= to + keep[0]) & (self.lane < to + keep[1]), tile, packed)
        return packed

    def for_bins(self, packed):
        return sum((roll(packed, b * 4 * self.size) for b in range(1, BINS)), packed)

    def by_bin(self, values):
        out = values[-1]
        for b in reversed(range(BINS - 1)):
            out = jnp.where(self.lane < 4 * self.size * (b + 1), values[b], out)
        return out

    def off_strip_wall(self, strip):
        z_at = lax.broadcasted_iota(jnp.int32, strip.shape, 0)
        wall = (z_at == 0) & (self.col == 0) | (self.strip_y == 0) & (self.row == 0)
        return jnp.where(wall, 0.0, strip)

    def only_neighbour(self, up, down, forward):
        count = max(len(up), len(down))
        up, down = up + down[len(up) :], down + up[len(down) :]
        return [jnp.where(forward, up[i], down[i]) for i in range(count)]

    def write_across(self, out, up, down, forward):
        planes = self.only_neighbour(up, down, forward) if self.side == 2 else up + down
        for i, plane in enumerate(planes):
            out[i] = plane
        for i in range(len(planes), out.shape[0]):
            out[i] = jnp.zeros(out.shape[1:], F32)

    def across(self, got, planes):
        z_in = [got["z"][i] for i in planes]
        return [got["y"][i] for i in planes], z_in

    def write_tunnel(self, pair, other, right, left):
        pair[...] = jnp.where(self.pair_right, right, left)
        other[0] = jnp.where(self.pair_right, left, right)
        for i in range(1, other.shape[0]):
            other[i] = jnp.zeros(pair.shape, F32)

    def read_tunnel(self, pair, other):
        pair, other = pair[...], other[0]
        return jnp.where(self.pair_right, other, pair), jnp.where(self.pair_right, pair, other)


def low_weights(flow, kappa):
    return (-0.25 * TIME_STEP) * (flow + kappa), TIME_STEP * (flow + 2.0 * kappa)


def pack_kernel(side, size, names, conc_hbm, vel_hbm, dust_ref, vel_ref, *refs):
    *sends, sems = refs
    load = pltpu.make_async_copy(conc_hbm, dust_ref, sems.at[0])
    load_vel = pltpu.make_async_copy(vel_hbm, vel_ref, sems.at[1])
    load.start()
    load_vel.start()
    here = Place(side, size, dust_ref.shape[-1])
    load.wait()
    for b in range(BINS):
        for y in range(size):
            dust_ref[b, here.at(y), :] = here.off_wall(y, dust_ref[b, here.at(y), :])
    send = dict(zip(names, sends))
    bins = range(BINS)
    ends = (size - 2, size - 1)
    y_up = [dust_ref[b, here.at(y), :] for b in bins for y in ends]
    y_down = [dust_ref[b, here.at(0), :] for b in bins]
    z_up = [here.rows(dust_ref, b, z) for b in bins for z in ends]
    z_down = [here.rows(dust_ref, b, 0) for b in bins]
    right = here.columns(dust_ref, bins, True, (0, 4))
    left = here.columns(dust_ref, bins, False, (0, 4))
    load_vel.wait()
    y_down.append(vel_ref[0, here.at(0), :])
    z_down.append(here.rows(vel_ref, 1, 0))
    here.write_across(send["y"], y_up, y_down, here.row == 0)
    here.write_across(send["z"], z_up, z_down, here.col == 0)
    half = LANES // 2
    u0, u1, u2 = (here.columns(vel_ref, [i], True, (2, 4)) for i in range(3))
    right += roll(u0, half) + roll(u1, half - 2) + roll(u2, half + 4 * size)
    u0, u1, u2 = (here.columns(vel_ref, [i], False, (0, 1)) for i in range(3))
    left += roll(u0, half) + roll(u1, half + 1) + roll(u2, half + 2)
    here.write_tunnel(send["pair"], send["other"], right, left)


def slope_and_bend(m1, p1, m2, p2):
    return (p1 - m1) - (p2 - m2), (p2 + m2) - 2.0 * (p1 + m1)


def inner_rates(here, field, vel_ref):
    size, length, shape = here.size, here.length, here.shape
    x_at = lax.broadcasted_iota(jnp.int32, shape, 1)
    weights = []
    for index, count in ((here.z_at, size), (x_at, length)):
        even = index % 2 == 0
        near, far = jnp.where(even, 0.5, 1.0), jnp.where(even, 0.25, 0.0)
        weights.append(
            (
                jnp.where(index == count - 1, 0.0, near),
                jnp.where(index == 0, 0.0, near),
                jnp.where(index == count - 2, 0.0, far),
                jnp.where(index == 0, 0.0, far),
            )
        )
    centre = jnp.where(here.z_at % 2 == 0, 3.5, 2.0) + jnp.where(x_at % 2 == 0, 3.5, 2.0)

    def along(f, axis, count):
        m1, p1, m2, p2 = weights[axis]
        return slope_and_bend(
            pltpu.roll(f * m1, 1, axis),
            pltpu.roll(f * p1, count - 1, axis),
            pltpu.roll(f * m2, 2, axis),
            pltpu.roll(f * p2, count - 2, axis),
        )

    zero = jnp.zeros(shape, F32)
    for b in range(BINS):
        kappa, settle = DIFFUSIVITY[b], SETTLING[b]

        def tile(y, b=b):
            return field[b, here.at(y), :] if 0 <= y < size else zero

        for y in range(size):
            f = tile(y)
            if y % 2 == 0:
                gy, ky = slope_and_bend(
                    tile(y - 1), tile(y + 1), 0.25 * tile(y - 2), 0.25 * tile(y + 2)
                )
                own = centre + 3.5
            else:
                gy, ky = 0.5 * (tile(y + 1) - tile(y - 1)), -(tile(y + 1) + tile(y - 1))
                own = centre + 2.0
            gz, kz = along(f, 0, size)
            gx, kx = along(f, 1, length)
            u0, u1, u2 = (vel_ref[i, here.at(y), :] for i in range(3))
            moved = (u0 - settle) * gy + u1 * gz + u2 * gx
            yield b, y, f, -(moved + kappa * (own * f + (ky + kz + kx)))


def first_inner_kernel(side, size, dust_ref, vel_ref, part_ref, y_w, z_w, x_w, rows_ref):
    here = Place(side, size, dust_ref.shape[-1])
    for b, y, f, rate in inner_rates(here, dust_ref, vel_ref):
        part_ref[b, here.at(y), :] = here.off_wall(y, f + TIME_STEP * rate)
    ends = (0, size - 2, size - 1)
    y_flow = [vel_ref[0, here.at(y), :] for y in ends]
    z_flow = [here.rows(vel_ref, 1, z) for z in ends]
    for b in range(BINS):
        kappa = DIFFUSIVITY[b]
        for out, flow in ((y_w, [u - SETTLING[b] for u in y_flow]), (z_w, z_flow)):
            out[b, 0], out[b, 1] = low_weights(flow[0], kappa)
            out[b, 2] = (0.25 * TIME_STEP) * (flow[1] - kappa)
            out[b, 3] = (-TIME_STEP) * (0.5 * flow[2] - kappa)
    for n, at in enumerate(((size - 2, size - 1), (0,))):
        rows = [vel_ref.at[1, pl.ds(y * size + z, 1), :] for y in at for z in ends]
        (rows_ref[n],) = here.stack(rows)
    kappa = here.by_bin(DIFFUSIVITY)
    even = here.lane % 2 == 0
    flow = here.for_bins(here.columns(vel_ref, [2], False, (0, 1)))
    far, _ = low_weights(roll(flow, 2), kappa)
    _, near = low_weights(roll(flow, 3), kappa)
    inside = here.strip_x >= 2
    x_w[0] = jnp.where(inside, jnp.where(even, far, near), 0.0)
    flow = here.for_bins(here.columns(vel_ref, [2], True, (2, 4)))
    far, near = (0.25 * TIME_STEP) * (flow - kappa), (-TIME_STEP) * (0.5 * flow - kappa)
    x_w[1] = jnp.where(inside, jnp.where(even, far, near), 0.0)


def add_halo(here, part_ref, x_w, y_add, z_add, low_strip, high_strip, share, rows=None):
    size, length = here.size, here.length
    x_low = low_strip * (share * x_w[0])
    x_low = x_low + roll(x_low, -1)
    high = jnp.where(here.strip_x == 2, roll(high_strip, 2), roll(high_strip, 3))
    x_high = high * (share * x_w[1])
    first, last = here.lane == 0, here.lane >= LANES - 2
    for b in range(BINS):
        y_low, y_before, y_last = y_add[b]
        for y in rows or range(size):
            tile = part_ref[b, here.at(y), :]

            if z_add is not None:
                z_low, z_before, z_last = (
                    jnp.broadcast_to(plane[y : y + 1, :], here.shape) for plane in z_add[b]
                )
                add = jnp.where(
                    here.z_at == 0, z_low, jnp.where(here.z_at == size - 1, z_last, z_before)
                )
                tile += share * jnp.where((here.z_at == 0) | (here.z_at >= size - 2), add, 0.0)
            for at, plane in ((0, y_low), (size - 2, y_before), (size - 1, y_last)):
                if y == at:
                    tile += share * plane
            to = 4 * (b * size + y) + 2
            low = jnp.where(first, roll(x_low, -to), 0.0)
            high = jnp.where(last, roll(x_high, -2 - to), 0.0)
            inner = [jnp.zeros((size, length - 2 * LANES), F32)] if length > 2 * LANES else []
            tile += jnp.concatenate([low] + inner + [high], 1)
            yield b, y, here.off_wall(y, tile)


def y_halo(here, ref, weights):
    hi = 0 if here.side == 2 else 2 * BINS
    adds = []
    for b in range(BINS):
        low = ref[2 * b] * weights[b, 0] + ref[2 * b + 1] * weights[b, 1]
        nxt = jnp.where(here.row == here.side - 1, 0.0, ref[hi + b])
        adds.append((low, nxt * weights[b, 2], nxt * weights[b, 3]))
    return adds, ref[hi + BINS]


def corner_planes(side):
    below = [*range(2 * BINS)]
    return below if side == 2 else below + [2 * BINS + b for b in range(BINS)]


def in_tiles(here, planes):
    return [p[:, at : at + LANES] for p in planes for at in range(0, here.length, LANES)]


def first_y_kernel(side, size, part_ref, y_w, x_w, rows_ref, y_in, pair_in, other_in, y_out):
    here = Place(side, size, part_ref.shape[-1])
    adds, flow = y_halo(here, y_in, y_w)
    from_left, from_right = here.read_tunnel(pair_in, other_in)
    ends = (0, size - 2, size - 1)
    tiles = {
        (b, y): tile
        for b, y, tile in add_halo(
            here, part_ref, x_w, adds, None, from_left, from_right, 1.0, ends
        )
    }
    up, down = [], []
    for b in range(BINS):
        far, near = low_weights(flow - SETTLING[b], DIFFUSIVITY[b])
        up.append(tiles[b, size - 2] * far + tiles[b, size - 1] * near)
        down.append(tiles[b, 0])
    strip = jnp.where(here.strip_x < 2, from_right, from_left)
    up, down = (in_tiles(here, planes) + [strip] for planes in (up, down))
    up += in_tiles(here, [rows_ref[0]])
    down += in_tiles(here, [rows_ref[1]])
    here.write_across(y_out, up, down, here.row == 0)


def first_outer_kernel(
    side, size, part_ref, y_w, z_w, x_w, y_in, z_in, pair_in, other_in, _, seg_ref, z_out
):
    here = Place(side, size, part_ref.shape[-1])
    bins = range(BINS)
    y_adds, _ = y_halo(here, y_in, y_w)
    hi = 0 if side == 2 else 2 * BINS
    z_adds = []
    for b in bins:
        low = z_in[2 * b] * z_w[b, 0] + z_in[2 * b + 1] * z_w[b, 1]
        nxt = jnp.where(here.col == side - 1, 0.0, z_in[hi + b])
        z_adds.append((low, nxt * z_w[b, 2], nxt * z_w[b, 3]))
    flow = z_in[hi + BINS]
    from_left, from_right = here.read_tunnel(pair_in, other_in)
    for b, y, tile in add_halo(
        here, part_ref, x_w, y_adds, z_adds, from_left, from_right, 1.0
    ):
        seg_ref[b, here.at(y), :] = tile

    up, down = [], []
    for b in bins:
        far, near, own = (here.rows(seg_ref, b, z) for z in (size - 2, size - 1, 0))
        weights = low_weights(flow, DIFFUSIVITY[b])
        up.append(far * weights[0] + near * weights[1])
        down.append(own)
    strip = jnp.where(here.strip_x < 2, from_right, from_left)
    up, down = (in_tiles(here, planes) + [strip] for planes in (up, down))
    at = corner_planes(side)
    up += in_tiles(here, here.stack([y_in.at[i, z : z + 1, :] for z in (size - 2, size - 1) for i in at]))
    down += in_tiles(here, here.stack([y_in.at[i, 0:1, :] for i in at]))
    here.write_across(z_out, up, down, here.col == 0)


def stencil(even, c, m1, p1, m2, p2):
    g = jnp.where(even, p1 - m1 - 0.25 * (p2 - m2), 0.5 * (p1 - m1))
    k = jnp.where(even, 3.5 * c - 2.0 * (p1 + m1) + 0.25 * (p2 + m2), 2.0 * c - (p1 + m1))
    return g, k


def advance_strip(here, dust_ref, from_left, from_right, strip_w):
    size, half = here.size, LANES // 2
    bins = range(BINS)
    own_first = here.columns(dust_ref, bins, False, (0, 4))
    own_last = here.columns(dust_ref, bins, True, (0, 4))
    x, y = here.strip_x, here.strip_y
    z = lax.broadcasted_iota(jnp.int32, here.lane.shape, 0)
    used = (here.lane < 4 * size * BINS) & (x != 1)
    right, before = x == 0, x == 2
    c = jnp.where(right, from_right, from_left)
    c = jnp.where(used, c, 0.0)
    gx, kx = stencil(
        x != 3,
        c,
        jnp.where(right, roll(own_last, -3), roll(from_left, 1)),
        jnp.where(right, roll(from_right, -1), jnp.where(before, roll(from_left, -1), roll(own_first, 3))),
        jnp.where(right, roll(own_last, -2), roll(from_left, 2)),
        jnp.where(right, roll(from_right, -2), roll(own_first, 2)),
    )
    gy, ky = stencil(
        y % 2 == 0,
        c,
        jnp.where(y == 0, 0.0, roll(c, 4)),
        jnp.where(y == size - 1, 0.0, roll(c, -4)),
        jnp.where(y == 0, 0.0, roll(c, 8)),
        jnp.where(y == size - 2, 0.0, roll(c, -8)),
    )
    gz, kz = stencil(
        z % 2 == 0,
        c,
        jnp.where(z == 0, 0.0, pltpu.roll(c, 1, 0)),
        jnp.where(z == size - 1, 0.0, pltpu.roll(c, size - 1, 0)),
        jnp.where(z == 0, 0.0, pltpu.roll(c, 2, 0)),
        jnp.where(z == size - 2, 0.0, pltpu.roll(c, size - 2, 0)),
    )

    def flow(left_by, right_by):
        both = jnp.where(right, roll(from_right, right_by), roll(from_left, left_by))
        return here.for_bins(jnp.where(here.lane < 4 * size, both, 0.0))

    u0 = flow(-half, -half) - here.by_bin(SETTLING)
    u1 = flow(2 - half, -half - 1)
    u2 = flow(-half - 4 * size, -half - 2)
    kappa = here.by_bin(DIFFUSIVITY)
    rate = u0 * gy + u1 * gz + u2 * gx + kappa * (kx + ky + kz)
    done = jnp.where(used, here.off_strip_wall(c - TIME_STEP * rate), 0.0)
    n = 0
    for at, flow, place in ((y, u0, here.row), (z, u1, here.col)):
        far, near = low_weights(flow, kappa)
        low, inside = (at == 0) & (place > 0), place < here.side - 1
        for mask, weight in (
            (low, far),
            (low, near),
            ((at == size - 2) & inside, (0.25 * TIME_STEP) * (flow - kappa)),
            ((at == size - 1) & inside, (-TIME_STEP) * (0.5 * flow - kappa)),
        ):
            strip_w[n] = jnp.where(used & mask, here.off_strip_wall(weight), 0.0)
            n += 1
    return done


def second_inner_kernel(
    side, size, dust_ref, vel_ref, seg_ref, y_w, pair_in, other_in, part_ref, strip_ref, strip_w, corner_w
):
    here = Place(side, size, dust_ref.shape[-1])
    for b, y, f, rate in inner_rates(here, seg_ref, vel_ref):
        result = 0.5 * dust_ref[b, here.at(y), :] + 0.5 * (f + TIME_STEP * rate)
        part_ref[b, here.at(y), :] = here.off_wall(y, result)
    from_left, from_right = here.read_tunnel(pair_in, other_in)
    strip_ref[...] = advance_strip(here, dust_ref, from_left, from_right, strip_w)
    has_low, has_high = here.row > 0, here.row < side - 1
    for b in range(BINS):
        for n, z in enumerate((0, size - 2, size - 1)):
            has_next = here.col > 0 if z == 0 else here.col < side - 1

            def row(plane, z=z):
                return jnp.broadcast_to(plane[z : z + 1, :], here.shape)

            for k in range(2):
                take = jnp.where((here.z_at == 0) & has_low, row(y_w[b, k]), 0.0)
                if k == 0:
                    take += jnp.where((here.z_at == size - 2) & has_high, row(y_w[b, 2]), 0.0)
                    take += jnp.where((here.z_at == size - 1) & has_high, row(y_w[b, 3]), 0.0)
                corner_w[b, 2 * n + k] = jnp.where(has_next, take, 0.0)


def second_outer_kernel(
    side, size, names, part_ref, y_w, z_w, x_w, strip_ref, strip_w, corner_w, *refs
):
    halos = len(names)
    got = dict(zip(names, refs[:halos]))
    out_hbm, result, sems = refs[halos:]
    here = Place(side, size, part_ref.shape[-1])
    count = here.length // LANES
    y_in, z_in = here.across(got, range(got["z"].shape[0]))
    adds = []
    y_hi, z_hi = (0, 0) if side == 2 else ((BINS + 1) * count + 1, BINS * count + 1 + -(-2 * len(corner_planes(side)) // size) * count)
    for ref, weights, at, hi in ((y_in, y_w, here.row, y_hi), (z_in, z_w, here.col, z_hi)):
        add = []
        for b in range(BINS):
            low, nxt = (
                jnp.concatenate([ref[first + b * count + t] for t in range(count)], 1)
                for first in (0, hi)
            )
            nxt = jnp.where(at == side - 1, 0.0, nxt)
            add.append((low, nxt * weights[b, 2], nxt * weights[b, 3]))
        adds.append(add)

    def corner(first, n, z_in=z_in):
        first, n = first + n // size * count, n % size
        return jnp.concatenate(
            [jnp.broadcast_to(z_in[first + t][n : n + 1, :], (size, LANES)) for t in range(count)], 1
        )

    start, rows = BINS * count + 1, len(corner_planes(side))
    sources = ((start, 0), (start, rows), (z_hi + start, 0))
    flows = [
        jnp.where(
            here.z_at == 0, corner(start, 3 * k + n, y_in), corner(y_hi + start, n, y_in)
        )
        for n in range(3)
        for k in range(2)
    ]
    for b in range(BINS):
        extra, kappa = [], DIFFUSIVITY[b]
        for n, z in enumerate((0, size - 2, size - 1)):
            total = 0.0
            for k in range(2):
                high_row = b if side == 2 else 2 * BINS + b
                flow = flows[2 * n + k]
                if z == 0:
                    ways = low_weights(flow, kappa)
                else:
                    ways = [TIME_STEP * (0.25 * (flow - kappa) if z == size - 2 else kappa - 0.5 * flow)]
                amount = 0.0
                for (first, skip), way in zip(sources[:2] if z == 0 else sources[2:], ways):
                    plane = jnp.where(
                        here.z_at == 0,
                        corner(first, skip + 2 * b + k),
                        corner(first, skip + high_row),
                    )
                    amount += plane * way
                total += amount * corner_w[b, 2 * n + k]
            extra.append(total)
        adds[1][b] = tuple(p + q for p, q in zip(adds[1][b], extra))
    low, high = y_in[BINS * count], y_in[y_hi + BINS * count]
    far, near = 4 * (size - 2), 4 * (size - 1)
    strip = strip_ref[...] + roll(low, -far) * strip_w[0] + roll(low, -near) * strip_w[1]
    strip += roll(high, far) * strip_w[2] + roll(high, near) * strip_w[3]
    low, high = z_in[BINS * count], z_in[z_hi + BINS * count]
    strip += pltpu.roll(low, 2, 0) * strip_w[4] + pltpu.roll(low, 1, 0) * strip_w[5]
    strip += pltpu.roll(high, size - 2, 0) * strip_w[6] + pltpu.roll(high, size - 1, 0) * strip_w[7]
    stores = [
        pltpu.make_async_copy(result.at[b], out_hbm.at[b], sems.at[b]) for b in range(BINS)
    ]
    for b, y, tile in add_halo(here, part_ref, x_w, adds[0], adds[1], strip, strip, 0.5):
        result[b, here.at(y), :] = tile
        if y == size - 1:
            stores[b].start()
    for store in stores:
        store.wait()


def shift(block, axis, moves):
    return lax.ppermute(block, axis, [(s, moves(s)) for s in range(lax.axis_size(axis))])


def body(concentration, velocity):
    side = math.isqrt(lax.axis_size("sec"))
    tunnel = lax.axis_size("tun")
    size, length = concentration.shape[-2:]
    conc = concentration.reshape(BINS, size * size, length)
    vel = velocity.reshape(3, size * size, length)
    vmem = pl.BlockSpec(memory_space=pltpu.VMEM)
    hbm = pl.BlockSpec(memory_space=pltpu.HBM)

    def planes(up, down):
        return max(up, down) if side == 2 else up + down

    def call(kernel, outs, *args):
        args = [pltpu.with_memory_space_constraint(arg, pltpu.VMEM) for arg in args]
        return pl.pallas_call(
            lambda *refs: kernel(side, size, *refs),
            out_shape=outs,
            in_specs=[vmem] * len(args),
            out_specs=[vmem] * len(outs),
            name=kernel.__name__,
        )(*args)

    def along_pair(s):
        return s + 1 - 2 * (s % 2)

    def along_other(s):
        return (s - 1 + 2 * (s % 2)) % tunnel

    def along_y(d):
        return lambda s: (s // side + d) % side * side + s % side

    def along_z(d):
        return lambda s: s // side * side + (s % side + d) % side

    def across(out, up, move):
        if side == 2:
            return shift(out, "sec", move(1))
        return jnp.concatenate(
            [shift(out[:up], "sec", move(1)), shift(out[up:], "sec", move(-1))], 0
        )

    moves = {
        "y": lambda out, up: across(out, up, along_y),
        "z": lambda out, up: across(out, up, along_z),
        "pair": lambda out, up: shift(out, "tun", along_pair),
        "other": lambda out, up: shift(out, "tun", along_other),
    }
    across_shape = (planes(2 * BINS, BINS + 1), size, length)
    shapes = {"pair": (size, LANES), "other": (8, size, LANES)}
    first = [pltpu.VMEM(shapes.get(name, across_shape), F32) for name in FIRST]
    tiles = BINS * (length // LANES) + 1
    corners = len(corner_planes(side))
    y_tiles = tiles + length // LANES
    z_up, z_down = (tiles + -(-n // size) * (length // LANES) for n in (2 * corners, corners))
    y_message = pltpu.VMEM((z_up + 1 if side == 2 else 2 * y_tiles, size, LANES), F32)
    z_message = pltpu.VMEM((planes(z_up, z_down), size, LANES), F32)
    dust, vel, *sends = pl.pallas_call(
        lambda *refs: pack_kernel(side, size, FIRST, *refs),
        out_shape=[pltpu.VMEM(conc.shape, F32), pltpu.VMEM(vel.shape, F32)] + first,
        in_specs=[hbm] * 2,
        out_specs=[vmem] * (2 + len(first)),
        scratch_shapes=[pltpu.SemaphoreType.DMA((2,))],
        name="pack_kernel",
    )(conc, vel)
    halo = [moves[name](out, 2 * BINS) for name, out in zip(FIRST, sends)]
    field, strip = pltpu.VMEM(conc.shape, F32), (size, LANES)
    weights = [pltpu.VMEM((BINS, 4, size, length), F32)] * 2 + [pltpu.VMEM((2,) + strip, F32)]
    weights.append(pltpu.VMEM((2, size, length), F32))
    part, *weights, rows = call(first_inner_kernel, [field] + weights, dust, vel)
    got = dict(zip(FIRST, halo))
    y_w, z_w, x_w = weights
    tunnel_in = got["pair"], got["other"]
    (y_send,) = call(first_y_kernel, [y_message], part, y_w, x_w, rows, got["y"], *tunnel_in)
    segment, z_send = call(
        first_outer_kernel, [field, z_message], part, *weights, got["y"], got["z"], *tunnel_in, y_send
    )
    strips = [pltpu.VMEM(strip, F32), pltpu.VMEM((8,) + strip, F32)]
    strips.append(pltpu.VMEM((BINS, 6, size, length), F32))
    part, *strips = call(
        second_inner_kernel, [field] + strips, dust, vel, segment, y_w, *tunnel_in
    )
    halo = [moves["y"](y_send, y_tiles), moves["z"](z_send, z_up)]
    args = (part, *weights, *strips, *halo)
    args = [pltpu.with_memory_space_constraint(arg, pltpu.VMEM) for arg in args]
    result = pl.pallas_call(
        lambda *refs: second_outer_kernel(side, size, SECOND, *refs),
        out_shape=jax.ShapeDtypeStruct(conc.shape, F32),
        in_specs=[vmem] * len(args),
        out_specs=hbm,
        scratch_shapes=[pltpu.VMEM(conc.shape, F32), pltpu.SemaphoreType.DMA((BINS,))],
        name="second_outer_kernel",
    )(*args)
    return result.reshape(concentration.shape)


def solution(mesh):
    spec = P(None, "sec", None, None, "tun")
    return jax.shard_map(
        body, mesh=mesh, in_specs=(spec, spec), out_specs=spec, check_vma=False
    )
```

```python
import math

import jax
import jax.numpy as jnp
from jax import lax
from jax.experimental import pallas as pl
from jax.experimental.pallas import tpu as pltpu
from jax.sharding import PartitionSpec as P

TIME_STEP = 0.1
DIFFUSIVITY = (0.4, 0.15)
SETTLING = (0.05, 0.6)
BINS = 2
LANES = 128
FIRST = ("y", "other", "z", "pair")
SECOND = ("y", "z")
F32 = jnp.float32


def roll(tile, by):
    by %= LANES
    return pltpu.roll(tile, by, 1) if by else tile


class Place:
    def __init__(self, side, size, length):
        self.side, self.size, self.length = side, size, length
        place = lax.axis_index("sec")
        self.row, self.col = place // side, lax.rem(place, side)
        self.pair_right = lax.rem(lax.axis_index("tun"), 2) == 0
        self.shape = (size, length)
        self.z_at = lax.broadcasted_iota(jnp.int32, self.shape, 0)
        self.lane = lax.broadcasted_iota(jnp.int32, (size, LANES), 1)
        self.strip_x, self.strip_y = self.lane % 4, self.lane // 4 % size

    def off_wall(self, y, tile):
        wall = (self.z_at == 0) & (self.col == 0)
        if y == 0:
            wall = wall | (self.row == 0)
        return jnp.where(wall, 0.0, tile)

    def at(self, y):
        return slice(y * self.size, (y + 1) * self.size)

    def rows(self, ref, lead, z):
        rows = jnp.broadcast_to(ref[lead, z : z + 1, :], self.shape)
        for y in range(1, self.size):
            row = ref[lead, y * self.size + z : y * self.size + z + 1, :]
            rows = jnp.where(self.z_at == y, jnp.broadcast_to(row, self.shape), rows)
        return rows

    def stack(self, rows):
        planes = []
        for n in range(0, len(rows), self.size):
            plane = jnp.zeros(self.shape, F32)
            for i, row in enumerate(rows[n : n + self.size]):
                plane = jnp.where(self.z_at == i, jnp.broadcast_to(row[...], self.shape), plane)
            planes.append(plane)
        return planes

    def columns(self, ref, leads, last, keep):
        packed = jnp.zeros((self.size, LANES), F32)
        for n, lead in enumerate(leads):
            for y in range(self.size):
                to = 4 * (n * self.size + y)
                if last:
                    tile = pltpu.roll(ref[lead, self.at(y), self.length - LANES :], (to + 4) % LANES, 1)
                else:
                    tile = ref[lead, self.at(y), :LANES]
                    tile = pltpu.roll(tile, to, 1) if to else tile
                packed = jnp.where((self.lane >= to + keep[0]) & (self.lane < to + keep[1]), tile, packed)
        return packed

    def for_bins(self, packed):
        return sum((roll(packed, b * 4 * self.size) for b in range(1, BINS)), packed)

    def by_bin(self, values):
        out = values[-1]
        for b in reversed(range(BINS - 1)):
            out = jnp.where(self.lane < 4 * self.size * (b + 1), values[b], out)
        return out

    def off_strip_wall(self, strip):
        z_at = lax.broadcasted_iota(jnp.int32, strip.shape, 0)
        wall = (z_at == 0) & (self.col == 0) | (self.strip_y == 0) & (self.row == 0)
        return jnp.where(wall, 0.0, strip)

    def only_neighbour(self, up, down, forward):
        count = max(len(up), len(down))
        up, down = up + down[len(up) :], down + up[len(down) :]
        return [jnp.where(forward, up[i], down[i]) for i in range(count)]

    def write_across(self, out, up, down, forward):
        planes = self.only_neighbour(up, down, forward) if self.side == 2 else up + down
        for i, plane in enumerate(planes):
            out[i] = plane
        for i in range(len(planes), out.shape[0]):
            out[i] = jnp.zeros(out.shape[1:], F32)

    def across(self, got, planes):
        z_in = [got["z"][i] for i in planes]
        return [got["y"][i] for i in planes], z_in

    def write_tunnel(self, pair, other, right, left):
        pair[...] = jnp.where(self.pair_right, right, left)
        other[0] = jnp.where(self.pair_right, left, right)
        for i in range(1, other.shape[0]):
            other[i] = jnp.zeros(pair.shape, F32)

    def read_tunnel(self, pair, other):
        pair, other = pair[...], other[0]
        return jnp.where(self.pair_right, other, pair), jnp.where(self.pair_right, pair, other)


def low_weights(flow, kappa):
    return (-0.25 * TIME_STEP) * (flow + kappa), TIME_STEP * (flow + 2.0 * kappa)


def pack_kernel(side, size, names, conc_hbm, vel_hbm, dust_ref, vel_ref, *refs):
    *sends, sems = refs
    load = pltpu.make_async_copy(conc_hbm, dust_ref, sems.at[0])
    load_vel = pltpu.make_async_copy(vel_hbm, vel_ref, sems.at[1])
    load.start()
    load_vel.start()
    here = Place(side, size, dust_ref.shape[-1])
    load.wait()
    for b in range(BINS):
        for y in range(size):
            dust_ref[b, here.at(y), :] = here.off_wall(y, dust_ref[b, here.at(y), :])
    send = dict(zip(names, sends))
    bins = range(BINS)
    ends = (size - 2, size - 1)
    y_up = [dust_ref[b, here.at(y), :] for b in bins for y in ends]
    y_down = [dust_ref[b, here.at(0), :] for b in bins]
    z_up = [here.rows(dust_ref, b, z) for b in bins for z in ends]
    z_down = [here.rows(dust_ref, b, 0) for b in bins]
    right = here.columns(dust_ref, bins, True, (0, 4))
    left = here.columns(dust_ref, bins, False, (0, 4))
    load_vel.wait()
    y_down.append(vel_ref[0, here.at(0), :])
    z_down.append(here.rows(vel_ref, 1, 0))
    here.write_across(send["y"], y_up, y_down, here.row == 0)
    here.write_across(send["z"], z_up, z_down, here.col == 0)
    half = LANES // 2
    u0, u1, u2 = (here.columns(vel_ref, [i], True, (2, 4)) for i in range(3))
    right += roll(u0, half) + roll(u1, half - 2) + roll(u2, half + 4 * size)
    u0, u1, u2 = (here.columns(vel_ref, [i], False, (0, 1)) for i in range(3))
    left += roll(u0, half) + roll(u1, half + 1) + roll(u2, half + 2)
    here.write_tunnel(send["pair"], send["other"], right, left)


def slope_and_bend(m1, p1, m2, p2):
    return (p1 - m1) - (p2 - m2), (p2 + m2) - 2.0 * (p1 + m1)


def inner_rates(here, field, vel_ref):
    size, length, shape = here.size, here.length, here.shape
    x_at = lax.broadcasted_iota(jnp.int32, shape, 1)
    weights = []
    for index, count in ((here.z_at, size), (x_at, length)):
        even = index % 2 == 0
        near, far = jnp.where(even, 0.5, 1.0), jnp.where(even, 0.25, 0.0)
        weights.append(
            (
                jnp.where(index == count - 1, 0.0, near),
                jnp.where(index == 0, 0.0, near),
                jnp.where(index == count - 2, 0.0, far),
                jnp.where(index == 0, 0.0, far),
            )
        )
    centre = jnp.where(here.z_at % 2 == 0, 3.5, 2.0) + jnp.where(x_at % 2 == 0, 3.5, 2.0)

    def along(f, axis, count):
        m1, p1, m2, p2 = weights[axis]
        return slope_and_bend(
            pltpu.roll(f * m1, 1, axis),
            pltpu.roll(f * p1, count - 1, axis),
            pltpu.roll(f * m2, 2, axis),
            pltpu.roll(f * p2, count - 2, axis),
        )

    zero = jnp.zeros(shape, F32)
    for b in range(BINS):
        kappa, settle = DIFFUSIVITY[b], SETTLING[b]

        def tile(y, b=b):
            return field[b, here.at(y), :] if 0 <= y < size else zero

        for y in range(size):
            f = tile(y)
            if y % 2 == 0:
                gy, ky = slope_and_bend(
                    tile(y - 1), tile(y + 1), 0.25 * tile(y - 2), 0.25 * tile(y + 2)
                )
                own = centre + 3.5
            else:
                gy, ky = 0.5 * (tile(y + 1) - tile(y - 1)), -(tile(y + 1) + tile(y - 1))
                own = centre + 2.0
            gz, kz = along(f, 0, size)
            gx, kx = along(f, 1, length)
            u0, u1, u2 = (vel_ref[i, here.at(y), :] for i in range(3))
            moved = (u0 - settle) * gy + u1 * gz + u2 * gx
            yield b, y, f, -(moved + kappa * (own * f + (ky + kz + kx)))


def first_inner_kernel(side, size, dust_ref, vel_ref, part_ref, y_w, z_w, x_w, rows_ref):
    here = Place(side, size, dust_ref.shape[-1])
    for b, y, f, rate in inner_rates(here, dust_ref, vel_ref):
        part_ref[b, here.at(y), :] = here.off_wall(y, f + TIME_STEP * rate)
    ends = (0, size - 2, size - 1)
    y_flow = [vel_ref[0, here.at(y), :] for y in ends]
    z_flow = [here.rows(vel_ref, 1, z) for z in ends]
    for b in range(BINS):
        kappa = DIFFUSIVITY[b]
        for out, flow in ((y_w, [u - SETTLING[b] for u in y_flow]), (z_w, z_flow)):
            out[b, 0], out[b, 1] = low_weights(flow[0], kappa)
            out[b, 2] = (0.25 * TIME_STEP) * (flow[1] - kappa)
            out[b, 3] = (-TIME_STEP) * (0.5 * flow[2] - kappa)
    for n, at in enumerate(((size - 2, size - 1), (0,))):
        rows = [vel_ref.at[1, pl.ds(y * size + z, 1), :] for y in at for z in ends]
        (rows_ref[n],) = here.stack(rows)
    kappa = here.by_bin(DIFFUSIVITY)
    even = here.lane % 2 == 0
    flow = here.for_bins(here.columns(vel_ref, [2], False, (0, 1)))
    far, _ = low_weights(roll(flow, 2), kappa)
    _, near = low_weights(roll(flow, 3), kappa)
    inside = here.strip_x >= 2
    x_w[0] = jnp.where(inside, jnp.where(even, far, near), 0.0)
    flow = here.for_bins(here.columns(vel_ref, [2], True, (2, 4)))
    far, near = (0.25 * TIME_STEP) * (flow - kappa), (-TIME_STEP) * (0.5 * flow - kappa)
    x_w[1] = jnp.where(inside, jnp.where(even, far, near), 0.0)


def add_halo(here, part_ref, x_w, y_add, z_add, low_strip, high_strip, share, rows=None):
    size, length = here.size, here.length
    x_low = low_strip * (share * x_w[0])
    x_low = x_low + roll(x_low, -1)
    high = jnp.where(here.strip_x == 2, roll(high_strip, 2), roll(high_strip, 3))
    x_high = high * (share * x_w[1])
    first, last = here.lane == 0, here.lane >= LANES - 2
    for b in range(BINS):
        y_low, y_before, y_last = y_add[b]
        for y in rows or range(size):
            tile = part_ref[b, here.at(y), :]

            if z_add is not None:
                z_low, z_before, z_last = (
                    jnp.broadcast_to(plane[y : y + 1, :], here.shape) for plane in z_add[b]
                )
                add = jnp.where(
                    here.z_at == 0, z_low, jnp.where(here.z_at == size - 1, z_last, z_before)
                )
                tile += share * jnp.where((here.z_at == 0) | (here.z_at >= size - 2), add, 0.0)
            for at, plane in ((0, y_low), (size - 2, y_before), (size - 1, y_last)):
                if y == at:
                    tile += share * plane
            to = 4 * (b * size + y) + 2
            low = jnp.where(first, roll(x_low, -to), 0.0)
            high = jnp.where(last, roll(x_high, -2 - to), 0.0)
            inner = [jnp.zeros((size, length - 2 * LANES), F32)] if length > 2 * LANES else []
            tile += jnp.concatenate([low] + inner + [high], 1)
            yield b, y, here.off_wall(y, tile)


def y_halo(here, ref, weights):
    hi = 0 if here.side == 2 else 2 * BINS
    adds = []
    for b in range(BINS):
        low = ref[2 * b] * weights[b, 0] + ref[2 * b + 1] * weights[b, 1]
        nxt = jnp.where(here.row == here.side - 1, 0.0, ref[hi + b])
        adds.append((low, nxt * weights[b, 2], nxt * weights[b, 3]))
    return adds, ref[hi + BINS]


def corner_planes(side):
    below = [*range(2 * BINS)]
    return below if side == 2 else below + [2 * BINS + b for b in range(BINS)]


def in_tiles(here, planes):
    return [p[:, at : at + LANES] for p in planes for at in range(0, here.length, LANES)]


def first_y_kernel(side, size, part_ref, y_w, x_w, rows_ref, y_in, pair_in, other_in, y_out):
    here = Place(side, size, part_ref.shape[-1])
    adds, flow = y_halo(here, y_in, y_w)
    from_left, from_right = here.read_tunnel(pair_in, other_in)
    ends = (0, size - 2, size - 1)
    tiles = {
        (b, y): tile
        for b, y, tile in add_halo(
            here, part_ref, x_w, adds, None, from_left, from_right, 1.0, ends
        )
    }
    up, down = [], []
    for b in range(BINS):
        far, near = low_weights(flow - SETTLING[b], DIFFUSIVITY[b])
        up.append(tiles[b, size - 2] * far + tiles[b, size - 1] * near)
        down.append(tiles[b, 0])
    strip = jnp.where(here.strip_x < 2, from_right, from_left)
    up, down = (in_tiles(here, planes) + [strip] for planes in (up, down))
    up += in_tiles(here, [rows_ref[0]])
    down += in_tiles(here, [rows_ref[1]])
    here.write_across(y_out, up, down, here.row == 0)


def corner_counts(side, size):
    rows = len(corner_planes(side))
    return -(-2 * rows // size), -(-rows // size)


def first_middle_kernel(
    side, size, part_ref, y_w, x_w, y_in, pair_in, other_in, _, middle_ref, corner_ref
):
    here = Place(side, size, part_ref.shape[-1])
    y_adds, _ = y_halo(here, y_in, y_w)
    from_left, from_right = here.read_tunnel(pair_in, other_in)
    for b, y, tile in add_halo(
        here, part_ref, x_w, y_adds, None, from_left, from_right, 1.0
    ):
        middle_ref[b, here.at(y), :] = tile
    at = corner_planes(side)
    planes = here.stack([y_in.at[i, z : z + 1, :] for z in (size - 2, size - 1) for i in at])
    planes += here.stack([y_in.at[i, 0:1, :] for i in at])
    for n, plane in enumerate(planes):
        corner_ref[n] = plane


def first_outer_kernel(
    side, size, middle_ref, z_w, z_in, pair_in, other_in, corner_ref, seg_ref, z_out
):
    here = Place(side, size, middle_ref.shape[-1])
    hi = 0 if side == 2 else 2 * BINS
    flow = z_in[hi + BINS]
    from_left, from_right = here.read_tunnel(pair_in, other_in)
    at_first, at_before, at_last = (here.z_at == z for z in (0, size - 2, size - 1))
    for b in range(BINS):
        low = z_in[2 * b] * z_w[b, 0] + z_in[2 * b + 1] * z_w[b, 1]
        nxt = jnp.where(here.col == side - 1, 0.0, z_in[hi + b])
        adds = low, nxt * z_w[b, 2], nxt * z_w[b, 3]
        for y in range(size):
            first, before, last = (
                jnp.broadcast_to(plane[y : y + 1, :], here.shape) for plane in adds
            )
            add = jnp.where(at_last, last, jnp.where(at_before, before, 0.0))
            tile = middle_ref[b, here.at(y), :] + jnp.where(at_first, first, add)
            seg_ref[b, here.at(y), :] = here.off_wall(y, tile)
    up, down = [], []
    for b in range(BINS):
        far, near, own = (here.rows(seg_ref, b, z) for z in (size - 2, size - 1, 0))
        weights = low_weights(flow, DIFFUSIVITY[b])
        up.append(far * weights[0] + near * weights[1])
        down.append(own)
    strip = jnp.where(here.strip_x < 2, from_right, from_left)
    up, down = (in_tiles(here, planes) + [strip] for planes in (up, down))
    count, more = corner_counts(side, size)
    up += in_tiles(here, [corner_ref[n] for n in range(count)])
    down += in_tiles(here, [corner_ref[count + n] for n in range(more)])
    here.write_across(z_out, up, down, here.col == 0)


def stencil(even, c, m1, p1, m2, p2):
    g = jnp.where(even, p1 - m1 - 0.25 * (p2 - m2), 0.5 * (p1 - m1))
    k = jnp.where(even, 3.5 * c - 2.0 * (p1 + m1) + 0.25 * (p2 + m2), 2.0 * c - (p1 + m1))
    return g, k


def advance_strip(here, dust_ref, from_left, from_right, strip_w):
    size, half = here.size, LANES // 2
    bins = range(BINS)
    own_first = here.columns(dust_ref, bins, False, (0, 4))
    own_last = here.columns(dust_ref, bins, True, (0, 4))
    x, y = here.strip_x, here.strip_y
    z = lax.broadcasted_iota(jnp.int32, here.lane.shape, 0)
    used = (here.lane < 4 * size * BINS) & (x != 1)
    right, before = x == 0, x == 2
    c = jnp.where(right, from_right, from_left)
    c = jnp.where(used, c, 0.0)
    gx, kx = stencil(
        x != 3,
        c,
        jnp.where(right, roll(own_last, -3), roll(from_left, 1)),
        jnp.where(right, roll(from_right, -1), jnp.where(before, roll(from_left, -1), roll(own_first, 3))),
        jnp.where(right, roll(own_last, -2), roll(from_left, 2)),
        jnp.where(right, roll(from_right, -2), roll(own_first, 2)),
    )
    gy, ky = stencil(
        y % 2 == 0,
        c,
        jnp.where(y == 0, 0.0, roll(c, 4)),
        jnp.where(y == size - 1, 0.0, roll(c, -4)),
        jnp.where(y == 0, 0.0, roll(c, 8)),
        jnp.where(y == size - 2, 0.0, roll(c, -8)),
    )
    gz, kz = stencil(
        z % 2 == 0,
        c,
        jnp.where(z == 0, 0.0, pltpu.roll(c, 1, 0)),
        jnp.where(z == size - 1, 0.0, pltpu.roll(c, size - 1, 0)),
        jnp.where(z == 0, 0.0, pltpu.roll(c, 2, 0)),
        jnp.where(z == size - 2, 0.0, pltpu.roll(c, size - 2, 0)),
    )

    def flow(left_by, right_by):
        both = jnp.where(right, roll(from_right, right_by), roll(from_left, left_by))
        return here.for_bins(jnp.where(here.lane < 4 * size, both, 0.0))

    u0 = flow(-half, -half) - here.by_bin(SETTLING)
    u1 = flow(2 - half, -half - 1)
    u2 = flow(-half - 4 * size, -half - 2)
    kappa = here.by_bin(DIFFUSIVITY)
    rate = u0 * gy + u1 * gz + u2 * gx + kappa * (kx + ky + kz)
    done = jnp.where(used, here.off_strip_wall(c - TIME_STEP * rate), 0.0)
    n = 0
    for at, flow, place in ((y, u0, here.row), (z, u1, here.col)):
        far, near = low_weights(flow, kappa)
        low, inside = (at == 0) & (place > 0), place < here.side - 1
        for mask, weight in (
            (low, far),
            (low, near),
            ((at == size - 2) & inside, (0.25 * TIME_STEP) * (flow - kappa)),
            ((at == size - 1) & inside, (-TIME_STEP) * (0.5 * flow - kappa)),
        ):
            strip_w[n] = jnp.where(used & mask, here.off_strip_wall(weight), 0.0)
            n += 1
    return done


def second_inner_kernel(
    side, size, dust_ref, vel_ref, seg_ref, y_w, pair_in, other_in, part_ref, strip_ref, strip_w, corner_w
):
    here = Place(side, size, dust_ref.shape[-1])
    for b, y, f, rate in inner_rates(here, seg_ref, vel_ref):
        result = 0.5 * dust_ref[b, here.at(y), :] + 0.5 * (f + TIME_STEP * rate)
        part_ref[b, here.at(y), :] = here.off_wall(y, result)
    from_left, from_right = here.read_tunnel(pair_in, other_in)
    strip_ref[...] = advance_strip(here, dust_ref, from_left, from_right, strip_w)
    has_low, has_high = here.row > 0, here.row < side - 1
    for b in range(BINS):
        for n, z in enumerate((0, size - 2, size - 1)):
            has_next = here.col > 0 if z == 0 else here.col < side - 1

            def row(plane, z=z):
                return jnp.broadcast_to(plane[z : z + 1, :], here.shape)

            for k in range(2):
                take = jnp.where((here.z_at == 0) & has_low, row(y_w[b, k]), 0.0)
                if k == 0:
                    take += jnp.where((here.z_at == size - 2) & has_high, row(y_w[b, 2]), 0.0)
                    take += jnp.where((here.z_at == size - 1) & has_high, row(y_w[b, 3]), 0.0)
                corner_w[b, 2 * n + k] = jnp.where(has_next, take, 0.0)


def second_outer_kernel(
    side, size, names, part_ref, y_w, z_w, x_w, strip_ref, strip_w, corner_w, *refs
):
    halos = len(names)
    got = dict(zip(names, refs[:halos]))
    out_hbm, result, sems = refs[halos:]
    here = Place(side, size, part_ref.shape[-1])
    count = here.length // LANES
    y_in, z_in = here.across(got, range(got["z"].shape[0]))
    adds = []
    y_hi, z_hi = (0, 0) if side == 2 else ((BINS + 1) * count + 1, BINS * count + 1 + -(-2 * len(corner_planes(side)) // size) * count)
    for ref, weights, at, hi in ((y_in, y_w, here.row, y_hi), (z_in, z_w, here.col, z_hi)):
        add = []
        for b in range(BINS):
            low, nxt = (
                jnp.concatenate([ref[first + b * count + t] for t in range(count)], 1)
                for first in (0, hi)
            )
            nxt = jnp.where(at == side - 1, 0.0, nxt)
            add.append((low, nxt * weights[b, 2], nxt * weights[b, 3]))
        adds.append(add)

    def corner(first, n, z_in=z_in):
        first, n = first + n // size * count, n % size
        return jnp.concatenate(
            [jnp.broadcast_to(z_in[first + t][n : n + 1, :], (size, LANES)) for t in range(count)], 1
        )

    start, rows = BINS * count + 1, len(corner_planes(side))
    sources = ((start, 0), (start, rows), (z_hi + start, 0))
    flows = [
        jnp.where(
            here.z_at == 0, corner(start, 3 * k + n, y_in), corner(y_hi + start, n, y_in)
        )
        for n in range(3)
        for k in range(2)
    ]
    for b in range(BINS):
        extra, kappa = [], DIFFUSIVITY[b]
        for n, z in enumerate((0, size - 2, size - 1)):
            total = 0.0
            for k in range(2):
                high_row = b if side == 2 else 2 * BINS + b
                flow = flows[2 * n + k]
                if z == 0:
                    ways = low_weights(flow, kappa)
                else:
                    ways = [TIME_STEP * (0.25 * (flow - kappa) if z == size - 2 else kappa - 0.5 * flow)]
                amount = 0.0
                for (first, skip), way in zip(sources[:2] if z == 0 else sources[2:], ways):
                    plane = jnp.where(
                        here.z_at == 0,
                        corner(first, skip + 2 * b + k),
                        corner(first, skip + high_row),
                    )
                    amount += plane * way
                total += amount * corner_w[b, 2 * n + k]
            extra.append(total)
        adds[1][b] = tuple(p + q for p, q in zip(adds[1][b], extra))
    low, high = y_in[BINS * count], y_in[y_hi + BINS * count]
    far, near = 4 * (size - 2), 4 * (size - 1)
    strip = strip_ref[...] + roll(low, -far) * strip_w[0] + roll(low, -near) * strip_w[1]
    strip += roll(high, far) * strip_w[2] + roll(high, near) * strip_w[3]
    low, high = z_in[BINS * count], z_in[z_hi + BINS * count]
    strip += pltpu.roll(low, 2, 0) * strip_w[4] + pltpu.roll(low, 1, 0) * strip_w[5]
    strip += pltpu.roll(high, size - 2, 0) * strip_w[6] + pltpu.roll(high, size - 1, 0) * strip_w[7]
    stores = [
        pltpu.make_async_copy(result.at[b], out_hbm.at[b], sems.at[b]) for b in range(BINS)
    ]
    for b, y, tile in add_halo(here, part_ref, x_w, adds[0], adds[1], strip, strip, 0.5):
        result[b, here.at(y), :] = tile
        if y == size - 1:
            stores[b].start()
    for store in stores:
        store.wait()


def shift(block, axis, moves):
    return lax.ppermute(block, axis, [(s, moves(s)) for s in range(lax.axis_size(axis))])


def body(concentration, velocity):
    side = math.isqrt(lax.axis_size("sec"))
    tunnel = lax.axis_size("tun")
    size, length = concentration.shape[-2:]
    conc = concentration.reshape(BINS, size * size, length)
    vel = velocity.reshape(3, size * size, length)
    vmem = pl.BlockSpec(memory_space=pltpu.VMEM)
    hbm = pl.BlockSpec(memory_space=pltpu.HBM)

    def planes(up, down):
        return max(up, down) if side == 2 else up + down

    def call(kernel, outs, *args):
        args = [pltpu.with_memory_space_constraint(arg, pltpu.VMEM) for arg in args]
        return pl.pallas_call(
            lambda *refs: kernel(side, size, *refs),
            out_shape=outs,
            in_specs=[vmem] * len(args),
            out_specs=[vmem] * len(outs),
            name=kernel.__name__,
        )(*args)

    def along_pair(s):
        return s + 1 - 2 * (s % 2)

    def along_other(s):
        return (s - 1 + 2 * (s % 2)) % tunnel

    def along_y(d):
        return lambda s: (s // side + d) % side * side + s % side

    def along_z(d):
        return lambda s: s // side * side + (s % side + d) % side

    def across(out, up, move):
        if side == 2:
            return shift(out, "sec", move(1))
        return jnp.concatenate(
            [shift(out[:up], "sec", move(1)), shift(out[up:], "sec", move(-1))], 0
        )

    moves = {
        "y": lambda out, up: across(out, up, along_y),
        "z": lambda out, up: across(out, up, along_z),
        "pair": lambda out, up: shift(out, "tun", along_pair),
        "other": lambda out, up: shift(out, "tun", along_other),
    }
    across_shape = (planes(2 * BINS, BINS + 1), size, length)
    shapes = {"pair": (size, LANES), "other": (8, size, LANES)}
    first = [pltpu.VMEM(shapes.get(name, across_shape), F32) for name in FIRST]
    tiles = BINS * (length // LANES) + 1
    corners = len(corner_planes(side))
    y_tiles = tiles + length // LANES
    z_up, z_down = (tiles + -(-n // size) * (length // LANES) for n in (2 * corners, corners))
    y_message = pltpu.VMEM((z_up + 1 if side == 2 else 2 * y_tiles, size, LANES), F32)
    z_message = pltpu.VMEM((planes(z_up, z_down), size, LANES), F32)
    dust, vel, *sends = pl.pallas_call(
        lambda *refs: pack_kernel(side, size, FIRST, *refs),
        out_shape=[pltpu.VMEM(conc.shape, F32), pltpu.VMEM(vel.shape, F32)] + first,
        in_specs=[hbm] * 2,
        out_specs=[vmem] * (2 + len(first)),
        scratch_shapes=[pltpu.SemaphoreType.DMA((2,))],
        name="pack_kernel",
    )(conc, vel)
    halo = [moves[name](out, 2 * BINS) for name, out in zip(FIRST, sends)]
    field, strip = pltpu.VMEM(conc.shape, F32), (size, LANES)
    weights = [pltpu.VMEM((BINS, 4, size, length), F32)] * 2 + [pltpu.VMEM((2,) + strip, F32)]
    weights.append(pltpu.VMEM((2, size, length), F32))
    part, *weights, rows = call(first_inner_kernel, [field] + weights, dust, vel)
    got = dict(zip(FIRST, halo))
    y_w, z_w, x_w = weights
    tunnel_in = got["pair"], got["other"]
    (y_send,) = call(first_y_kernel, [y_message], part, y_w, x_w, rows, got["y"], *tunnel_in)
    corner_shape = pltpu.VMEM((sum(corner_counts(side, size)), size, length), F32)
    middle, corner = call(
        first_middle_kernel, [field, corner_shape], part, y_w, x_w, got["y"], *tunnel_in, y_send
    )
    segment, z_send = call(
        first_outer_kernel, [field, z_message], middle, z_w, got["z"], *tunnel_in, corner
    )
    strips = [pltpu.VMEM(strip, F32), pltpu.VMEM((8,) + strip, F32)]
    strips.append(pltpu.VMEM((BINS, 6, size, length), F32))
    part, *strips = call(
        second_inner_kernel, [field] + strips, dust, vel, segment, y_w, *tunnel_in
    )
    halo = [moves["y"](y_send, y_tiles), moves["z"](z_send, z_up)]
    args = (part, *weights, *strips, *halo)
    args = [pltpu.with_memory_space_constraint(arg, pltpu.VMEM) for arg in args]
    result = pl.pallas_call(
        lambda *refs: second_outer_kernel(side, size, SECOND, *refs),
        out_shape=jax.ShapeDtypeStruct(conc.shape, F32),
        in_specs=[vmem] * len(args),
        out_specs=hbm,
        scratch_shapes=[pltpu.VMEM(conc.shape, F32), pltpu.SemaphoreType.DMA((BINS,))],
        name="second_outer_kernel",
    )(*args)
    return result.reshape(concentration.shape)


def solution(mesh):
    spec = P(None, "sec", None, None, "tun")
    return jax.shard_map(
        body, mesh=mesh, in_specs=(spec, spec), out_specs=spec, check_vma=False
    )
```

```python
import math

import jax
import jax.numpy as jnp
from jax import lax
from jax.experimental import pallas as pl
from jax.experimental.pallas import tpu as pltpu
from jax.sharding import PartitionSpec as P

TIME_STEP = 0.1
DIFFUSIVITY = (0.4, 0.15)
SETTLING = (0.05, 0.6)
BINS = 2
LANES = 128
FIRST = ("y", "other", "z", "pair")
SECOND = ("y", "z")
F32 = jnp.float32


def roll(tile, by):
    by %= LANES
    return pltpu.roll(tile, by, 1) if by else tile


class Place:
    def __init__(self, side, size, length):
        self.side, self.size, self.length = side, size, length
        place = lax.axis_index("sec")
        self.row, self.col = place // side, lax.rem(place, side)
        self.pair_right = lax.rem(lax.axis_index("tun"), 2) == 0
        self.shape = (size, length)
        self.z_at = lax.broadcasted_iota(jnp.int32, self.shape, 0)
        self.lane = lax.broadcasted_iota(jnp.int32, (size, LANES), 1)
        self.strip_x, self.strip_y = self.lane % 4, self.lane // 4 % size

    def off_wall(self, y, tile):
        wall = (self.z_at == 0) & (self.col == 0)
        if y == 0:
            wall = wall | (self.row == 0)
        return jnp.where(wall, 0.0, tile)

    def at(self, y):
        return slice(y * self.size, (y + 1) * self.size)

    def rows(self, ref, lead, z):
        rows = jnp.broadcast_to(ref[lead, z : z + 1, :], self.shape)
        for y in range(1, self.size):
            row = ref[lead, y * self.size + z : y * self.size + z + 1, :]
            rows = jnp.where(self.z_at == y, jnp.broadcast_to(row, self.shape), rows)
        return rows

    def stack(self, rows):
        planes = []
        for n in range(0, len(rows), self.size):
            plane = jnp.zeros(self.shape, F32)
            for i, row in enumerate(rows[n : n + self.size]):
                plane = jnp.where(self.z_at == i, jnp.broadcast_to(row[...], self.shape), plane)
            planes.append(plane)
        return planes

    def columns(self, ref, leads, last, keep):
        start = LANES - 4 if last else 0
        kept = (self.lane >= start + keep[0]) & (self.lane < start + keep[1])
        lanes = slice(self.length - LANES, self.length) if last else slice(0, LANES)
        parts = []
        for n, lead in enumerate(leads):
            for y in range(self.size):
                tile = jnp.where(kept, ref[lead, self.at(y), lanes], 0.0)
                parts.append(roll(tile, 4 * (n * self.size + y) - start))
        while len(parts) > 1:
            parts = [sum(parts[i + 1 : i + 2], parts[i]) for i in range(0, len(parts), 2)]
        return parts[0]

    def for_bins(self, packed):
        return sum((roll(packed, b * 4 * self.size) for b in range(1, BINS)), packed)

    def by_bin(self, values):
        out = values[-1]
        for b in reversed(range(BINS - 1)):
            out = jnp.where(self.lane < 4 * self.size * (b + 1), values[b], out)
        return out

    def off_strip_wall(self, strip):
        z_at = lax.broadcasted_iota(jnp.int32, strip.shape, 0)
        wall = (z_at == 0) & (self.col == 0) | (self.strip_y == 0) & (self.row == 0)
        return jnp.where(wall, 0.0, strip)

    def only_neighbour(self, up, down, forward):
        count = max(len(up), len(down))
        up, down = up + down[len(up) :], down + up[len(down) :]
        return [jnp.where(forward, up[i], down[i]) for i in range(count)]

    def write_across(self, out, up, down, forward):
        planes = self.only_neighbour(up, down, forward) if self.side == 2 else up + down
        for i, plane in enumerate(planes):
            out[i] = plane
        for i in range(len(planes), out.shape[0]):
            out[i] = jnp.zeros(out.shape[1:], F32)

    def across(self, got, planes):
        z_in = [got["z"][i] for i in planes]
        return [got["y"][i] for i in planes], z_in

    def write_tunnel(self, pair, other, right, left):
        pair[...] = jnp.where(self.pair_right, right, left)
        other[0] = jnp.where(self.pair_right, left, right)
        for i in range(1, other.shape[0]):
            other[i] = jnp.zeros(pair.shape, F32)

    def read_tunnel(self, pair, other):
        pair, other = pair[...], other[0]
        return jnp.where(self.pair_right, other, pair), jnp.where(self.pair_right, pair, other)


def low_weights(flow, kappa):
    return (-0.25 * TIME_STEP) * (flow + kappa), TIME_STEP * (flow + 2.0 * kappa)


def pack_kernel(side, size, names, conc_hbm, vel_hbm, dust_ref, vel_ref, *refs):
    *sends, sems = refs
    load = pltpu.make_async_copy(conc_hbm, dust_ref, sems.at[0])
    load_vel = pltpu.make_async_copy(vel_hbm, vel_ref, sems.at[1])
    load.start()
    load_vel.start()
    here = Place(side, size, dust_ref.shape[-1])
    load.wait()
    for b in range(BINS):
        for y in range(size):
            dust_ref[b, here.at(y), :] = here.off_wall(y, dust_ref[b, here.at(y), :])
    send = dict(zip(names, sends))
    bins = range(BINS)
    ends = (size - 2, size - 1)
    y_up = [dust_ref[b, here.at(y), :] for b in bins for y in ends]
    y_down = [dust_ref[b, here.at(0), :] for b in bins]
    z_up = [here.rows(dust_ref, b, z) for b in bins for z in ends]
    z_down = [here.rows(dust_ref, b, 0) for b in bins]
    right = here.columns(dust_ref, bins, True, (0, 4))
    left = here.columns(dust_ref, bins, False, (0, 4))
    load_vel.wait()
    y_down.append(vel_ref[0, here.at(0), :])
    z_down.append(here.rows(vel_ref, 1, 0))
    here.write_across(send["y"], y_up, y_down, here.row == 0)
    here.write_across(send["z"], z_up, z_down, here.col == 0)
    half = LANES // 2
    u0, u1, u2 = (here.columns(vel_ref, [i], True, (2, 4)) for i in range(3))
    right += roll(u0, half) + roll(u1, half - 2) + roll(u2, half + 4 * size)
    u0, u1, u2 = (here.columns(vel_ref, [i], False, (0, 1)) for i in range(3))
    left += roll(u0, half) + roll(u1, half + 1) + roll(u2, half + 2)
    here.write_tunnel(send["pair"], send["other"], right, left)


def slope_and_bend(m1, p1, m2, p2):
    return (p1 - m1) - (p2 - m2), (p2 + m2) - 2.0 * (p1 + m1)


def inner_rates(here, field, vel_ref):
    size, length, shape = here.size, here.length, here.shape
    x_at = lax.broadcasted_iota(jnp.int32, shape, 1)
    weights = []
    for index, count in ((here.z_at, size), (x_at, length)):
        even = index % 2 == 0
        near, far = jnp.where(even, 0.5, 1.0), jnp.where(even, 0.25, 0.0)
        weights.append(
            (
                jnp.where(index == count - 1, 0.0, near),
                jnp.where(index == 0, 0.0, near),
                jnp.where(index == count - 2, 0.0, far),
                jnp.where(index == 0, 0.0, far),
            )
        )
    centre = jnp.where(here.z_at % 2 == 0, 3.5, 2.0) + jnp.where(x_at % 2 == 0, 3.5, 2.0)

    def along(f, axis, count):
        m1, p1, m2, p2 = weights[axis]
        return slope_and_bend(
            pltpu.roll(f * m1, 1, axis),
            pltpu.roll(f * p1, count - 1, axis),
            pltpu.roll(f * m2, 2, axis),
            pltpu.roll(f * p2, count - 2, axis),
        )

    zero = jnp.zeros(shape, F32)
    for b in range(BINS):
        kappa, settle = DIFFUSIVITY[b], SETTLING[b]

        def tile(y, b=b):
            return field[b, here.at(y), :] if 0 <= y < size else zero

        for y in range(size):
            f = tile(y)
            if y % 2 == 0:
                gy, ky = slope_and_bend(
                    tile(y - 1), tile(y + 1), 0.25 * tile(y - 2), 0.25 * tile(y + 2)
                )
                own = centre + 3.5
            else:
                gy, ky = 0.5 * (tile(y + 1) - tile(y - 1)), -(tile(y + 1) + tile(y - 1))
                own = centre + 2.0
            gz, kz = along(f, 0, size)
            gx, kx = along(f, 1, length)
            u0, u1, u2 = (vel_ref[i, here.at(y), :] for i in range(3))
            moved = (u0 - settle) * gy + u1 * gz + u2 * gx
            yield b, y, f, -(moved + kappa * (own * f + (ky + kz + kx)))


def first_inner_kernel(side, size, dust_ref, vel_ref, part_ref, y_w, z_w, x_w, rows_ref):
    here = Place(side, size, dust_ref.shape[-1])
    for b, y, f, rate in inner_rates(here, dust_ref, vel_ref):
        part_ref[b, here.at(y), :] = here.off_wall(y, f + TIME_STEP * rate)
    ends = (0, size - 2, size - 1)
    y_flow = [vel_ref[0, here.at(y), :] for y in ends]
    z_flow = [here.rows(vel_ref, 1, z) for z in ends]
    for b in range(BINS):
        kappa = DIFFUSIVITY[b]
        for out, flow in ((y_w, [u - SETTLING[b] for u in y_flow]), (z_w, z_flow)):
            out[b, 0], out[b, 1] = low_weights(flow[0], kappa)
            out[b, 2] = (0.25 * TIME_STEP) * (flow[1] - kappa)
            out[b, 3] = (-TIME_STEP) * (0.5 * flow[2] - kappa)
    for n, at in enumerate(((size - 2, size - 1), (0,))):
        rows = [vel_ref.at[1, pl.ds(y * size + z, 1), :] for y in at for z in ends]
        (rows_ref[n],) = here.stack(rows)
    kappa = here.by_bin(DIFFUSIVITY)
    even = here.lane % 2 == 0
    flow = here.for_bins(here.columns(vel_ref, [2], False, (0, 1)))
    far, _ = low_weights(roll(flow, 2), kappa)
    _, near = low_weights(roll(flow, 3), kappa)
    inside = here.strip_x >= 2
    x_w[0] = jnp.where(inside, jnp.where(even, far, near), 0.0)
    flow = here.for_bins(here.columns(vel_ref, [2], True, (2, 4)))
    far, near = (0.25 * TIME_STEP) * (flow - kappa), (-TIME_STEP) * (0.5 * flow - kappa)
    x_w[1] = jnp.where(inside, jnp.where(even, far, near), 0.0)


def add_halo(here, part_ref, x_w, y_add, z_add, low_strip, high_strip, share, rows=None):
    size, length = here.size, here.length
    x_low = low_strip * (share * x_w[0])
    x_low = x_low + roll(x_low, -1)
    high = jnp.where(here.strip_x == 2, roll(high_strip, 2), roll(high_strip, 3))
    x_high = high * (share * x_w[1])
    first, last = here.lane == 0, here.lane >= LANES - 2
    for b in range(BINS):
        y_low, y_before, y_last = y_add[b]
        for y in rows or range(size):
            tile = part_ref[b, here.at(y), :]

            if z_add is not None:
                z_low, z_before, z_last = (
                    jnp.broadcast_to(plane[y : y + 1, :], here.shape) for plane in z_add[b]
                )
                add = jnp.where(
                    here.z_at == 0, z_low, jnp.where(here.z_at == size - 1, z_last, z_before)
                )
                tile += share * jnp.where((here.z_at == 0) | (here.z_at >= size - 2), add, 0.0)
            for at, plane in ((0, y_low), (size - 2, y_before), (size - 1, y_last)):
                if y == at:
                    tile += share * plane
            to = 4 * (b * size + y) + 2
            low = jnp.where(first, roll(x_low, -to), 0.0)
            high = jnp.where(last, roll(x_high, -2 - to), 0.0)
            inner = [jnp.zeros((size, length - 2 * LANES), F32)] if length > 2 * LANES else []
            tile += jnp.concatenate([low] + inner + [high], 1)
            yield b, y, here.off_wall(y, tile)


def y_halo(here, ref, weights):
    hi = 0 if here.side == 2 else 2 * BINS
    adds = []
    for b in range(BINS):
        low = ref[2 * b] * weights[b, 0] + ref[2 * b + 1] * weights[b, 1]
        nxt = jnp.where(here.row == here.side - 1, 0.0, ref[hi + b])
        adds.append((low, nxt * weights[b, 2], nxt * weights[b, 3]))
    return adds, ref[hi + BINS]


def corner_planes(side):
    below = [*range(2 * BINS)]
    return below if side == 2 else below + [2 * BINS + b for b in range(BINS)]


def in_tiles(here, planes):
    return [p[:, at : at + LANES] for p in planes for at in range(0, here.length, LANES)]


def first_y_kernel(side, size, part_ref, y_w, x_w, rows_ref, y_in, pair_in, other_in, y_out):
    here = Place(side, size, part_ref.shape[-1])
    adds, flow = y_halo(here, y_in, y_w)
    from_left, from_right = here.read_tunnel(pair_in, other_in)
    ends = (0, size - 2, size - 1)
    tiles = {
        (b, y): tile
        for b, y, tile in add_halo(
            here, part_ref, x_w, adds, None, from_left, from_right, 1.0, ends
        )
    }
    up, down = [], []
    for b in range(BINS):
        far, near = low_weights(flow - SETTLING[b], DIFFUSIVITY[b])
        up.append(tiles[b, size - 2] * far + tiles[b, size - 1] * near)
        down.append(tiles[b, 0])
    strip = jnp.where(here.strip_x < 2, from_right, from_left)
    up, down = (in_tiles(here, planes) + [strip] for planes in (up, down))
    up += in_tiles(here, [rows_ref[0]])
    down += in_tiles(here, [rows_ref[1]])
    here.write_across(y_out, up, down, here.row == 0)


def corner_counts(side, size):
    rows = len(corner_planes(side))
    return -(-2 * rows // size), -(-rows // size)


def first_middle_kernel(
    side, size, part_ref, y_w, x_w, y_in, pair_in, other_in, _, middle_ref, corner_ref
):
    here = Place(side, size, part_ref.shape[-1])
    y_adds, _ = y_halo(here, y_in, y_w)
    from_left, from_right = here.read_tunnel(pair_in, other_in)
    for b, y, tile in add_halo(
        here, part_ref, x_w, y_adds, None, from_left, from_right, 1.0
    ):
        middle_ref[b, here.at(y), :] = tile
    at = corner_planes(side)
    planes = here.stack([y_in.at[i, z : z + 1, :] for z in (size - 2, size - 1) for i in at])
    planes += here.stack([y_in.at[i, 0:1, :] for i in at])
    for n, plane in enumerate(planes):
        corner_ref[n] = plane


def first_outer_kernel(
    side, size, middle_ref, z_w, z_in, pair_in, other_in, corner_ref, seg_ref, z_out
):
    here = Place(side, size, middle_ref.shape[-1])
    hi = 0 if side == 2 else 2 * BINS
    flow = z_in[hi + BINS]
    from_left, from_right = here.read_tunnel(pair_in, other_in)
    at_first, at_before, at_last = (here.z_at == z for z in (0, size - 2, size - 1))
    for b in range(BINS):
        low = z_in[2 * b] * z_w[b, 0] + z_in[2 * b + 1] * z_w[b, 1]
        nxt = jnp.where(here.col == side - 1, 0.0, z_in[hi + b])
        adds = low, nxt * z_w[b, 2], nxt * z_w[b, 3]
        for y in range(size):
            first, before, last = (
                jnp.broadcast_to(plane[y : y + 1, :], here.shape) for plane in adds
            )
            add = jnp.where(at_last, last, jnp.where(at_before, before, 0.0))
            tile = middle_ref[b, here.at(y), :] + jnp.where(at_first, first, add)
            seg_ref[b, here.at(y), :] = here.off_wall(y, tile)
    up, down = [], []
    for b in range(BINS):
        far, near, own = (here.rows(seg_ref, b, z) for z in (size - 2, size - 1, 0))
        weights = low_weights(flow, DIFFUSIVITY[b])
        up.append(far * weights[0] + near * weights[1])
        down.append(own)
    strip = jnp.where(here.strip_x < 2, from_right, from_left)
    up, down = (in_tiles(here, planes) + [strip] for planes in (up, down))
    count, more = corner_counts(side, size)
    up += in_tiles(here, [corner_ref[n] for n in range(count)])
    down += in_tiles(here, [corner_ref[count + n] for n in range(more)])
    here.write_across(z_out, up, down, here.col == 0)


def stencil(even, c, m1, p1, m2, p2):
    g = jnp.where(even, p1 - m1 - 0.25 * (p2 - m2), 0.5 * (p1 - m1))
    k = jnp.where(even, 3.5 * c - 2.0 * (p1 + m1) + 0.25 * (p2 + m2), 2.0 * c - (p1 + m1))
    return g, k


def advance_strip(here, dust_ref, from_left, from_right, strip_w):
    size, half = here.size, LANES // 2
    bins = range(BINS)
    own_first = here.columns(dust_ref, bins, False, (0, 4))
    own_last = here.columns(dust_ref, bins, True, (0, 4))
    x, y = here.strip_x, here.strip_y
    z = lax.broadcasted_iota(jnp.int32, here.lane.shape, 0)
    used = (here.lane < 4 * size * BINS) & (x != 1)
    right, before = x == 0, x == 2
    c = jnp.where(right, from_right, from_left)
    c = jnp.where(used, c, 0.0)
    gx, kx = stencil(
        x != 3,
        c,
        jnp.where(right, roll(own_last, -3), roll(from_left, 1)),
        jnp.where(right, roll(from_right, -1), jnp.where(before, roll(from_left, -1), roll(own_first, 3))),
        jnp.where(right, roll(own_last, -2), roll(from_left, 2)),
        jnp.where(right, roll(from_right, -2), roll(own_first, 2)),
    )
    gy, ky = stencil(
        y % 2 == 0,
        c,
        jnp.where(y == 0, 0.0, roll(c, 4)),
        jnp.where(y == size - 1, 0.0, roll(c, -4)),
        jnp.where(y == 0, 0.0, roll(c, 8)),
        jnp.where(y == size - 2, 0.0, roll(c, -8)),
    )
    gz, kz = stencil(
        z % 2 == 0,
        c,
        jnp.where(z == 0, 0.0, pltpu.roll(c, 1, 0)),
        jnp.where(z == size - 1, 0.0, pltpu.roll(c, size - 1, 0)),
        jnp.where(z == 0, 0.0, pltpu.roll(c, 2, 0)),
        jnp.where(z == size - 2, 0.0, pltpu.roll(c, size - 2, 0)),
    )

    def flow(left_by, right_by):
        both = jnp.where(right, roll(from_right, right_by), roll(from_left, left_by))
        return here.for_bins(jnp.where(here.lane < 4 * size, both, 0.0))

    u0 = flow(-half, -half) - here.by_bin(SETTLING)
    u1 = flow(2 - half, -half - 1)
    u2 = flow(-half - 4 * size, -half - 2)
    kappa = here.by_bin(DIFFUSIVITY)
    rate = u0 * gy + u1 * gz + u2 * gx + kappa * (kx + ky + kz)
    done = jnp.where(used, here.off_strip_wall(c - TIME_STEP * rate), 0.0)
    n = 0
    for at, flow, place in ((y, u0, here.row), (z, u1, here.col)):
        far, near = low_weights(flow, kappa)
        low, inside = (at == 0) & (place > 0), place < here.side - 1
        for mask, weight in (
            (low, far),
            (low, near),
            ((at == size - 2) & inside, (0.25 * TIME_STEP) * (flow - kappa)),
            ((at == size - 1) & inside, (-TIME_STEP) * (0.5 * flow - kappa)),
        ):
            strip_w[n] = jnp.where(used & mask, here.off_strip_wall(weight), 0.0)
            n += 1
    return done


def second_inner_kernel(
    side, size, dust_ref, vel_ref, seg_ref, y_w, pair_in, other_in, part_ref, strip_ref, strip_w, corner_w
):
    here = Place(side, size, dust_ref.shape[-1])
    for b, y, f, rate in inner_rates(here, seg_ref, vel_ref):
        result = 0.5 * dust_ref[b, here.at(y), :] + 0.5 * (f + TIME_STEP * rate)
        part_ref[b, here.at(y), :] = here.off_wall(y, result)
    from_left, from_right = here.read_tunnel(pair_in, other_in)
    strip_ref[...] = advance_strip(here, dust_ref, from_left, from_right, strip_w)
    has_low, has_high = here.row > 0, here.row < side - 1
    for b in range(BINS):
        for n, z in enumerate((0, size - 2, size - 1)):
            has_next = here.col > 0 if z == 0 else here.col < side - 1

            def row(plane, z=z):
                return jnp.broadcast_to(plane[z : z + 1, :], here.shape)

            for k in range(2):
                take = jnp.where((here.z_at == 0) & has_low, row(y_w[b, k]), 0.0)
                if k == 0:
                    take += jnp.where((here.z_at == size - 2) & has_high, row(y_w[b, 2]), 0.0)
                    take += jnp.where((here.z_at == size - 1) & has_high, row(y_w[b, 3]), 0.0)
                corner_w[b, 2 * n + k] = jnp.where(has_next, take, 0.0)


def second_outer_kernel(
    side, size, names, part_ref, y_w, z_w, x_w, strip_ref, strip_w, corner_w, *refs
):
    halos = len(names)
    got = dict(zip(names, refs[:halos]))
    out_hbm, result, sems = refs[halos:]
    here = Place(side, size, part_ref.shape[-1])
    count = here.length // LANES
    y_in, z_in = here.across(got, range(got["z"].shape[0]))
    adds = []
    y_hi, z_hi = (0, 0) if side == 2 else ((BINS + 1) * count + 1, BINS * count + 1 + -(-2 * len(corner_planes(side)) // size) * count)
    for ref, weights, at, hi in ((y_in, y_w, here.row, y_hi), (z_in, z_w, here.col, z_hi)):
        add = []
        for b in range(BINS):
            low, nxt = (
                jnp.concatenate([ref[first + b * count + t] for t in range(count)], 1)
                for first in (0, hi)
            )
            nxt = jnp.where(at == side - 1, 0.0, nxt)
            add.append((low, nxt * weights[b, 2], nxt * weights[b, 3]))
        adds.append(add)

    def corner(first, n, z_in=z_in):
        first, n = first + n // size * count, n % size
        return jnp.concatenate(
            [jnp.broadcast_to(z_in[first + t][n : n + 1, :], (size, LANES)) for t in range(count)], 1
        )

    start, rows = BINS * count + 1, len(corner_planes(side))
    sources = ((start, 0), (start, rows), (z_hi + start, 0))
    flows = [
        jnp.where(
            here.z_at == 0, corner(start, 3 * k + n, y_in), corner(y_hi + start, n, y_in)
        )
        for n in range(3)
        for k in range(2)
    ]
    for b in range(BINS):
        extra, kappa = [], DIFFUSIVITY[b]
        for n, z in enumerate((0, size - 2, size - 1)):
            total = 0.0
            for k in range(2):
                high_row = b if side == 2 else 2 * BINS + b
                flow = flows[2 * n + k]
                if z == 0:
                    ways = low_weights(flow, kappa)
                else:
                    ways = [TIME_STEP * (0.25 * (flow - kappa) if z == size - 2 else kappa - 0.5 * flow)]
                amount = 0.0
                for (first, skip), way in zip(sources[:2] if z == 0 else sources[2:], ways):
                    plane = jnp.where(
                        here.z_at == 0,
                        corner(first, skip + 2 * b + k),
                        corner(first, skip + high_row),
                    )
                    amount += plane * way
                total += amount * corner_w[b, 2 * n + k]
            extra.append(total)
        adds[1][b] = tuple(p + q for p, q in zip(adds[1][b], extra))
    low, high = y_in[BINS * count], y_in[y_hi + BINS * count]
    far, near = 4 * (size - 2), 4 * (size - 1)
    strip = strip_ref[...] + roll(low, -far) * strip_w[0] + roll(low, -near) * strip_w[1]
    strip += roll(high, far) * strip_w[2] + roll(high, near) * strip_w[3]
    low, high = z_in[BINS * count], z_in[z_hi + BINS * count]
    strip += pltpu.roll(low, 2, 0) * strip_w[4] + pltpu.roll(low, 1, 0) * strip_w[5]
    strip += pltpu.roll(high, size - 2, 0) * strip_w[6] + pltpu.roll(high, size - 1, 0) * strip_w[7]
    stores = [
        pltpu.make_async_copy(result.at[b], out_hbm.at[b], sems.at[b]) for b in range(BINS)
    ]
    for b, y, tile in add_halo(here, part_ref, x_w, adds[0], adds[1], strip, strip, 0.5):
        result[b, here.at(y), :] = tile
        if y == size - 1:
            stores[b].start()
    for store in stores:
        store.wait()


def shift(block, axis, moves):
    return lax.ppermute(block, axis, [(s, moves(s)) for s in range(lax.axis_size(axis))])


def body(concentration, velocity):
    side = math.isqrt(lax.axis_size("sec"))
    tunnel = lax.axis_size("tun")
    size, length = concentration.shape[-2:]
    conc = concentration.reshape(BINS, size * size, length)
    vel = velocity.reshape(3, size * size, length)
    vmem = pl.BlockSpec(memory_space=pltpu.VMEM)
    hbm = pl.BlockSpec(memory_space=pltpu.HBM)

    def planes(up, down):
        return max(up, down) if side == 2 else up + down

    def call(kernel, outs, *args):
        args = [pltpu.with_memory_space_constraint(arg, pltpu.VMEM) for arg in args]
        return pl.pallas_call(
            lambda *refs: kernel(side, size, *refs),
            out_shape=outs,
            in_specs=[vmem] * len(args),
            out_specs=[vmem] * len(outs),
            name=kernel.__name__,
        )(*args)

    def along_pair(s):
        return s + 1 - 2 * (s % 2)

    def along_other(s):
        return (s - 1 + 2 * (s % 2)) % tunnel

    def along_y(d):
        return lambda s: (s // side + d) % side * side + s % side

    def along_z(d):
        return lambda s: s // side * side + (s % side + d) % side

    def across(out, up, move):
        if side == 2:
            return shift(out, "sec", move(1))
        return jnp.concatenate(
            [shift(out[:up], "sec", move(1)), shift(out[up:], "sec", move(-1))], 0
        )

    moves = {
        "y": lambda out, up: across(out, up, along_y),
        "z": lambda out, up: across(out, up, along_z),
        "pair": lambda out, up: shift(out, "tun", along_pair),
        "other": lambda out, up: shift(out, "tun", along_other),
    }
    across_shape = (planes(2 * BINS, BINS + 1), size, length)
    shapes = {"pair": (size, LANES), "other": (8, size, LANES)}
    first = [pltpu.VMEM(shapes.get(name, across_shape), F32) for name in FIRST]
    tiles = BINS * (length // LANES) + 1
    corners = len(corner_planes(side))
    y_tiles = tiles + length // LANES
    z_up, z_down = (tiles + -(-n // size) * (length // LANES) for n in (2 * corners, corners))
    y_message = pltpu.VMEM((z_up + 1 if side == 2 else 2 * y_tiles, size, LANES), F32)
    z_message = pltpu.VMEM((planes(z_up, z_down), size, LANES), F32)
    dust, vel, *sends = pl.pallas_call(
        lambda *refs: pack_kernel(side, size, FIRST, *refs),
        out_shape=[pltpu.VMEM(conc.shape, F32), pltpu.VMEM(vel.shape, F32)] + first,
        in_specs=[hbm] * 2,
        out_specs=[vmem] * (2 + len(first)),
        scratch_shapes=[pltpu.SemaphoreType.DMA((2,))],
        name="pack_kernel",
    )(conc, vel)
    halo = [moves[name](out, 2 * BINS) for name, out in zip(FIRST, sends)]
    field, strip = pltpu.VMEM(conc.shape, F32), (size, LANES)
    weights = [pltpu.VMEM((BINS, 4, size, length), F32)] * 2 + [pltpu.VMEM((2,) + strip, F32)]
    weights.append(pltpu.VMEM((2, size, length), F32))
    part, *weights, rows = call(first_inner_kernel, [field] + weights, dust, vel)
    got = dict(zip(FIRST, halo))
    y_w, z_w, x_w = weights
    tunnel_in = got["pair"], got["other"]
    (y_send,) = call(first_y_kernel, [y_message], part, y_w, x_w, rows, got["y"], *tunnel_in)
    corner_shape = pltpu.VMEM((sum(corner_counts(side, size)), size, length), F32)
    middle, corner = call(
        first_middle_kernel, [field, corner_shape], part, y_w, x_w, got["y"], *tunnel_in, y_send
    )
    segment, z_send = call(
        first_outer_kernel, [field, z_message], middle, z_w, got["z"], *tunnel_in, corner
    )
    strips = [pltpu.VMEM(strip, F32), pltpu.VMEM((8,) + strip, F32)]
    strips.append(pltpu.VMEM((BINS, 6, size, length), F32))
    part, *strips = call(
        second_inner_kernel, [field] + strips, dust, vel, segment, y_w, *tunnel_in
    )
    halo = [moves["y"](y_send, y_tiles), moves["z"](z_send, z_up)]
    args = (part, *weights, *strips, *halo)
    args = [pltpu.with_memory_space_constraint(arg, pltpu.VMEM) for arg in args]
    result = pl.pallas_call(
        lambda *refs: second_outer_kernel(side, size, SECOND, *refs),
        out_shape=jax.ShapeDtypeStruct(conc.shape, F32),
        in_specs=[vmem] * len(args),
        out_specs=hbm,
        scratch_shapes=[pltpu.VMEM(conc.shape, F32), pltpu.SemaphoreType.DMA((BINS,))],
        name="second_outer_kernel",
    )(*args)
    return result.reshape(concentration.shape)


def solution(mesh):
    spec = P(None, "sec", None, None, "tun")
    return jax.shard_map(
        body, mesh=mesh, in_specs=(spec, spec), out_specs=spec, check_vma=False
    )
```
